32 devices in a mesh: grp: 2 (over y), ti: 4 (over x, core), tj: 4 (over z).
Axes of the slice: x: 2, y: 2, z: 4, core: 2. Of those that a mesh axis runs over, the one named last changes fastest.
Arguments:
- corpus: bfloat16 [2, 24576, 1024], P('grp', ('ti', 'tj')), may hold values from -64 to 64
- slot_of_row: int32 [2, 24576], P('grp', ('ti', 'tj')), may hold values from -1 to 24575, as said below
Outputs:
- max_similarity: float32 [2, 12288], P('grp', ('ti', 'tj'))
The draws below stay inside these ranges and needn't reach their ends.
Inputs may be any that keep to these rules, and one draw needn't show every extreme that they name: `slot_of_row`: every value from 0 to 24575 appears exactly once; a row with value v lies on a device whose ti index is (v % 12288) // 3072; from one device at most 192 rows have values in one aligned group of 768 consecutive values, and some device sends exactly 192 to some group.
All inputs are finite; a program needn't handle non-finite values.
Results may differ from the reference program's by a relative error of at most 0.0009.
Values may be sent and summed in bfloat16 or wider, within the bound.
A program may use at most 64 MiB of HBM per device.

```python
import jax
import jax.numpy as jnp
from jax import lax

D = 1024
BLK = 3072
GROUPS = 2
SUB_ROWS = 768
CAP = 192
SRC_DEV = 1536
CLUSTER = 12288
GRID_ROWS = 24576


def slot_table(key):
    lane_count = BLK // SUB_ROWS
    owners = 2 * lane_count
    average = CAP // 2
    key_list = jax.random.split(jax.random.fold_in(key, 11), 4)
    swings = jax.random.randint(key_list[0], (lane_count, lane_count), -average, average + 1)
    swings = swings.at[:, 0].set(average)
    paired = jnp.stack([average + swings, average - swings], axis=2).reshape(lane_count, owners)
    orders = jax.vmap(lambda sub_key: jax.random.permutation(sub_key, owners))(jax.random.split(key_list[1], lane_count))
    shares = jnp.take_along_axis(paired, orders, axis=1)
    sender = jnp.arange(owners)
    offsets = (sender[None, :] - sender[:, None]) % owners
    counts = shares[:, offsets]
    ends = jnp.cumsum(counts, axis=2)
    starts = ends - counts
    members = jnp.arange(SUB_ROWS)
    target = jnp.sum((members[None, None, :, None] >= ends[:, :, None, :]).astype(jnp.int32), axis=3)
    within = members[None, None, :] - jnp.take_along_axis(starts, target, axis=2)
    arrival = jnp.cumsum(counts, axis=1) - counts
    position = jnp.take_along_axis(arrival, target, axis=2) + within
    shuffles = jax.vmap(lambda sub_key: jax.random.permutation(sub_key, SUB_ROWS))(jax.random.split(key_list[2], lane_count * owners))
    shuffles = shuffles.reshape(lane_count, owners * SUB_ROWS)
    lookup = (target * SUB_ROWS + position).reshape(lane_count, owners * SUB_ROWS)
    placed = jnp.take_along_axis(shuffles, lookup, axis=1).reshape(lane_count, owners, SUB_ROWS)
    row_index = jnp.arange(lane_count)[:, None, None]
    values = target // lane_count * CLUSTER + row_index * BLK + target % lane_count * SUB_ROWS + placed
    local_rows = jax.vmap(lambda sub_key: jax.random.permutation(sub_key, SRC_DEV))(jax.random.split(key_list[3], lane_count * owners))[:, :SUB_ROWS]
    table = jax.vmap(lambda spots, entries: jnp.full((SRC_DEV,), -1, jnp.int32).at[spots].set(entries.astype(jnp.int32)))(local_rows, values.reshape(lane_count * owners, SUB_ROWS))
    table = table.reshape(lane_count, 2, lane_count, SRC_DEV).transpose(1, 0, 2, 3).reshape(2, lane_count * lane_count * SRC_DEV)
    return table.astype(jnp.int32)


def draw_slot_of_row(key, part):
    return slot_table(key)


def draw_corpus(key, part):
    table = slot_table(key)
    total = 2 * CLUSTER
    key_list = jax.random.split(jax.random.fold_in(key, 23), 9)
    basis = jax.random.normal(key_list[0], (total, D), jnp.float32)
    partner = jnp.concatenate([jax.random.permutation(key_list[1], CLUSTER), CLUSTER + jax.random.permutation(key_list[2], CLUSTER)])
    strong = jax.random.randint(key_list[3], (total,), 0, 4) == 0
    mixing = jnp.where(strong, jax.random.uniform(key_list[4], (total,), jnp.float32, 1.0, 4.0), jax.random.uniform(key_list[5], (total,), jnp.float32, 0.0, 0.3))
    cluster_rows = basis + mixing[:, None] * basis[partner]
    filler = jax.random.normal(key_list[8], (2, GRID_ROWS, D), jnp.float32)
    chosen = cluster_rows[jnp.clip(table, 0, total - 1)]
    result = jnp.where((table >= 0)[..., None], chosen, filler)
    return jnp.clip(result, -64.0, 64.0).astype(jnp.bfloat16)


def setup_inputs(seed: int = 0) -> dict:
    streams_of = jax.random.split(jax.random.key(seed), 3)
    return {
        "corpus": draw_corpus(jax.random.fold_in(streams_of[2], 71), 0),
        "slot_of_row": draw_slot_of_row(jax.random.fold_in(streams_of[2], 71), 0),
    }


epsilon = 1e-06

def reference(corpus, slot_of_row):
    features = corpus.shape[2]
    flat_rows = corpus.reshape(-1, features)
    slots = slot_of_row.reshape(-1).astype(jnp.int32)
    total = GROUPS * CLUSTER
    target = jnp.where(slots >= 0, slots, total).astype(jnp.int32)
    cluster_rows = jnp.zeros((total, features), corpus.dtype).at[target].set(flat_rows, mode='drop')
    widened = cluster_rows.astype(jnp.float32)
    row_squares = lax.optimization_barrier(jnp.sum(widened * widened, axis=1, keepdims=True))
    inverse_norm = lax.rsqrt(row_squares + epsilon)
    unit_rows = (widened * inverse_norm).astype(jnp.bfloat16)
    per_group = CLUSTER // BLK

    def one_block(pair_index):
        group_start = pair_index // per_group * CLUSTER
        local_start = pair_index % per_group * BLK
        queries = lax.dynamic_slice_in_dim(unit_rows, (group_start + local_start).astype(jnp.int32), BLK, 0)
        members = lax.dynamic_slice_in_dim(unit_rows, group_start.astype(jnp.int32), CLUSTER, 0)
        scores = jnp.dot(queries, members.T, preferred_element_type=jnp.float32)
        same = (local_start + jnp.arange(BLK, dtype=jnp.int32))[:, None] == jnp.arange(CLUSTER, dtype=jnp.int32)[None, :]
        scores = jnp.where(same, -2.0, scores)
        return lax.optimization_barrier(jnp.max(scores, axis=1))
    best = lax.map(one_block, jnp.arange(GROUPS * per_group, dtype=jnp.int32))
    return best.reshape(GROUPS, CLUSTER)
```

```python
import functools

import jax
import jax.numpy as jnp
from jax import lax
from jax.experimental import pallas as pl
from jax.experimental.pallas import tpu as pltpu
from jax.sharding import PartitionSpec as P

MESH = pl.DeviceIdType.MESH
NT = (((1,), (1,)), ((), ()))
NN = (((1,), (0,)), ((), ()))
CORES = 2
EPSILON = 1e-06


def dot(a, b, dims):
    return lax.dot_general(a, b, dims, preferred_element_type=jnp.float32)


def kernel(geo, slots_ref, corpus_ref, out_ref, spot, ids_src, send, send_ids, got, got_ids,
           picks, summed, raw, units, best, parts, s_send, s_recv, i_send, i_recv,
           b_send, b_recv, p_send, p_recv):
    ti_count, tj_count, count, features, sub, cap, chunks, parts_f = geo
    width = features // parts_f
    owners = 2 * tj_count
    xs = ti_count // CORES
    zs = tj_count // 2
    blk = sub * tj_count
    cluster = blk * ti_count
    step = sub // chunks
    g, ti, tj = lax.axis_index("grp"), lax.axis_index("ti"), lax.axis_index("tj")
    x, core = ti // CORES, ti % CORES
    zh, zl = tj // zs, tj % zs
    lin = g * tj_count + tj

    def dev(gg, tt, jj):
        return {"grp": gg, "ti": tt, "tj": jj}

    def owner_dev(k):
        d = lax.rem(lin + k, owners)
        return d, dev(d // tj_count, ti, lax.rem(d, tj_count))

    def row_dev(dx, dy):
        return dev(lax.rem(g + dy, 2), lax.rem(x + dx, xs) * CORES + core, tj)

    def col_dev(dc, dz):
        return dev(g, x * CORES + lax.rem(core + dc, CORES), zh * zs + lax.rem(zl + dz, zs))

    def final_dev(dx, dy):
        return dev(zh, lax.rem(x + dx, xs) * CORES + core, lax.rem(g + dy, 2) * zs + zl)

    def feeder_dev(dx, dy):
        return dev(dy, lax.rem(x + dx, xs) * CORES + core, g * zs + zl)

    barrier = pltpu.get_barrier_semaphore()
    greeted = 0
    targets = [owner_dev(k)[1] for k in range(1, owners)]
    targets += [row_dev(dx, dy) for dx in range(1, xs) for dy in range(2)]
    targets += [col_dev(dc, dz) for dc in range(1, CORES) for dz in range(zs)]
    targets += [final_dev(dx, dy) for dx in range(1, xs) for dy in range(2)]
    targets += [feeder_dev(dx, dy) for dx in range(1, xs) for dy in range(2)]
    for target in targets:
        pl.semaphore_signal(barrier, inc=1, device_id=target, device_id_type=MESH)
        greeted += 1

    v = slots_ref[...]
    member = v >= 0
    second = (v >= cluster).astype(jnp.int32)
    inblk = v - second * cluster - ti * blk
    s = jnp.zeros_like(v)
    for k in range(1, tj_count):
        s = s + (inblk >= k * sub).astype(jnp.int32)
    pos = inblk - s * sub
    s_hi = (s >= zs).astype(jnp.int32)
    owner = s_hi * tj_count + second * zs + s - s_hi * zs
    owner = jnp.where(member, owner, owners)
    piece = 256 if count % 256 == 0 else 128
    before = (
        lax.broadcasted_iota(jnp.int32, (piece, piece), 0)
        < lax.broadcasted_iota(jnp.int32, (piece, piece), 1)
    ).astype(jnp.bfloat16)
    carry = jnp.zeros((owners, 1), jnp.float32)
    owner_iota = lax.broadcasted_iota(jnp.int32, (owners, piece), 0)
    for p in range(count // piece):
        part = slice(p * piece, (p + 1) * piece)
        mine = owner_iota == owner[:, part]
        hot = mine.astype(jnp.float32)
        ranks = dot(hot.astype(jnp.bfloat16), before, NN) + carry
        carry = carry + jnp.sum(hot, axis=1, keepdims=True)
        rank = jnp.sum(jnp.where(mine, ranks, 0.0), axis=0, keepdims=True).astype(jnp.int32)
        spot[:, part] = jnp.where(member[:, part], owner[:, part] * cap + rank, owners * cap)
    line = lax.broadcasted_iota(jnp.int32, (16, count), 0)
    ids_src[...] = jnp.where(
        line == 0, pos >> 5, jnp.where(line == 1, pos & 31, (line == 2).astype(jnp.int32))
    ).astype(jnp.float32).astype(jnp.bfloat16)

    row_peers = [(dx, dy) for dx in range(xs) for dy in range(2)]
    col_peers = [(dc, dz) for dc in range(CORES) for dz in range(zs)]
    own = len(row_peers) - 1
    row_at = {peer: i - 1 if i else own for i, peer in enumerate(row_peers)}
    col_at = {peer: own + i for i, peer in enumerate(col_peers)}
    lanes = [pl.ds(f * width, width) for f in range(parts_f)]
    half = sub // 2

    def pick_of(k):
        d = lax.rem(lin + k, owners)
        return (
            spot[...] == d * cap + lax.broadcasted_iota(jnp.int32, (cap, count), 0)
        ).astype(jnp.float32).astype(jnp.bfloat16)

    def row_copy(k, f):
        return pltpu.make_async_remote_copy(
            send.at[k, :, lanes[f]], got.at[k, :, lanes[f]], s_send.at[k, f], s_recv.at[k, f],
            device_id=owner_dev(k)[1], device_id_type=MESH)

    def id_copy(k):
        return pltpu.make_async_remote_copy(
            send_ids.at[k], got_ids.at[k], i_send.at[k], i_recv.at[k],
            device_id=owner_dev(k)[1], device_id_type=MESH)

    def start_pair(k, f):
        if f == 0:
            id_copy(k).start()
        row_copy(k, f).start()

    def pack(f):
        def one(k, _):
            pick = pick_of(k)
            send[k, :, lanes[f]] = dot(pick, corpus_ref[0, :, lanes[f]], NN).astype(jnp.bfloat16)
            if f == 0:
                send_ids[k, :, :cap] = dot(ids_src[...], pick, NT).astype(jnp.bfloat16)

            @pl.when(k > 1)
            def _():
                start_pair(k - 1, f)
            return 0

        lax.fori_loop(1, owners, one, 0)
        pick = pick_of(0)
        got[0, :, lanes[f]] = dot(pick, corpus_ref[0, :, lanes[f]], NN).astype(jnp.bfloat16)
        if f == 0:
            got_ids[0, :, :cap] = dot(ids_src[...], pick, NT).astype(jnp.bfloat16)
        start_pair(owners - 1, f)

    def place(f):
        def one(k, first):
            if f == 0:
                line_ids = got_ids[k, :, :cap].astype(jnp.float32)
                where = (line_ids[0:1] * 32.0 + line_ids[1:2]).astype(jnp.int32)
                where = jnp.where(line_ids[2:3] > 0.5, where, sub)
                picks[k] = (
                    where == lax.broadcasted_iota(jnp.int32, (sub, cap), 0)
                ).astype(jnp.float32).astype(jnp.bfloat16)
            term = dot(picks[k], got[k, :, lanes[f]], NN)
            summed[...] = term if first else summed[...] + term

        def arrived(k, _):
            if f == 0:
                id_copy(k).wait_recv()
            row_copy(k, f).wait_recv()
            one(k, False)
            return 0

        one(0, True)
        lax.fori_loop(1, owners, arrived, 0)

    started, waited = [], set()

    def block_copy(source, target, f, h, device):
        area = (pl.ds(h * half, half), lanes[f])
        return pltpu.make_async_remote_copy(
            raw.at[(source,) + area], raw.at[(target,) + area],
            b_send.at[target, f, h], b_recv.at[target, f, h],
            device_id=device, device_id_type=MESH)

    def ship(source, target, f, h, device):
        copy = block_copy(source, target, f, h, device)
        copy.start()
        started.append(copy)

    def need(block, f, h):
        if (block, f, h) not in waited:
            waited.add((block, f, h))
            block_copy(own, block, f, h, row_dev(0, 1)).wait_recv()

    def launch(f):
        for n in range(2):
            for dx, dy in row_peers[1:]:
                if xs == 2 and dx and dy:
                    continue
                ship(own, row_at[(-dx) % xs, (-dy) % 2], f, 1 - n if dy else n, row_dev(dx, dy))
            for dc, dz in col_peers[1:]:
                if zs == 2 and dc and dz:
                    continue
                ship(own, col_at[(-dc) % CORES, (-dz) % zs], f, n, col_dev(dc, dz))

    def relay(f):
        if xs == 2:
            need(row_at[1, 0], f, 0)
            ship(row_at[1, 0], row_at[1, 1], f, 0, row_dev(0, 1))
            need(row_at[0, 1], f, 1)
            ship(row_at[0, 1], row_at[1, 1], f, 1, row_dev(1, 0))
        if zs == 2:
            for h in range(2):
                need(col_at[0, 1], f, h)
                ship(col_at[0, 1], col_at[1, 1], f, h, col_dev(1, 0))

    pl.semaphore_wait(barrier, greeted)
    ahead = 2
    for f in range(min(ahead, parts_f)):
        pack(f)
    for f in range(parts_f):
        place(f)
        raw[own, :, lanes[f]] = summed[...].astype(jnp.bfloat16)
        if f == 0:
            best[...] = jnp.full(best.shape, -2.0, jnp.float32)
        if f:
            relay(f - 1)
        launch(f)
        if f + ahead < parts_f:
            pack(f + ahead)

    def norm(block):
        for f in range(parts_f):
            for h in range(2):
                if block != own:
                    need(block, f, h)

        def one(n, _):
            area = pl.ds(pl.multiple_of(n * 128, 128), 128)
            wide = raw[block, area, :].astype(jnp.float32)
            squares = jnp.sum(wide * wide, axis=1, keepdims=True)
            units[block, area, :] = (wide * lax.rsqrt(squares + EPSILON)).astype(jnp.bfloat16)
            return 0

        lax.fori_loop(0, sub // 128, one, 0)

    def tile(row, i, col, diagonal=False):
        part = pl.ds(pl.multiple_of(i * step, step), step)
        scores = dot(units[own + col], units[row, part, :], NT)
        if diagonal:
            same = (
                lax.broadcasted_iota(jnp.int32, (sub, step), 0)
                == i * step + lax.broadcasted_iota(jnp.int32, (sub, step), 1)
            )
            scores = jnp.where(same, -2.0, scores)
        top = jnp.max(scores.reshape(sub // 8, 8, step), axis=0)
        best[row, i] = jnp.maximum(best[row, i], top)
        return 0

    norm(own)
    lax.fori_loop(0, chunks, lambda i, _: tile(own, i, 0, True), 0)
    relay(parts_f - 1)
    for col in range(1, len(col_peers)):
        norm(own + col)
        lax.fori_loop(0, chunks, lambda i, _, col=col: tile(own, i, col), 0)

    def part_copy(peer):
        return pltpu.make_async_remote_copy(
            best.at[row_at[peer]], parts.at[x * 2 + g],
            p_send.at[row_at[peer]], p_recv.at[x * 2 + g],
            device_id=final_dev(*peer), device_id_type=MESH)

    stays = zh == g

    @pl.when(stays)
    def _():
        parts[x * 2 + g] = best[own]

    @pl.when(jnp.logical_not(stays))
    def _():
        part_copy((0, 0)).start()

    order = [peer for peer in row_peers[1:] if not (peer[0] and peer[1])]
    order += [peer for peer in row_peers[1:] if peer[0] and peer[1]]
    total = chunks * len(col_peers)
    for peer in order:
        row = row_at[peer]
        norm(row)
        lax.fori_loop(
            0, total, lambda n, _, row=row: tile(row, n // len(col_peers), n % len(col_peers)), 0)
        part_copy(peer).start()

    for feeder in range(len(row_peers)):
        arrived = pltpu.make_async_remote_copy(
            best.at[0], parts.at[feeder], p_send.at[0], p_recv.at[feeder],
            device_id=row_dev(0, 1), device_id_type=MESH)
        here = jnp.logical_and(stays, x * 2 + g == feeder)

        @pl.when(jnp.logical_not(here))
        def _(arrived=arrived):
            arrived.wait_recv()
    for i in range(chunks):
        top = jnp.max(parts[:, i], axis=0)
        out_ref[:, i * step : (i + 1) * step] = jnp.max(top, axis=0, keepdims=True)

    @pl.when(jnp.logical_not(stays))
    def _():
        part_copy((0, 0)).wait_send()

    for peer in row_peers[1:]:
        part_copy(peer).wait_send()
    for copy in started:
        copy.wait_send()

    def drain(k, _):
        id_copy(k).wait_send()
        for f in range(parts_f):
            row_copy(k, f).wait_send()
        return 0

    lax.fori_loop(1, owners, drain, 0)


def per_device(corpus, slot_of_row):
    ti_count, tj_count = lax.axis_size("ti"), lax.axis_size("tj")
    _, count, features = corpus.shape
    sub = count // 2
    cap = sub // tj_count
    owners = 2 * tj_count
    chunks, parts_f = 1, 4
    step = sub // chunks
    row_blocks, col_blocks = ti_count // CORES * 2, tj_count // 2 * CORES
    blocks = row_blocks + col_blocks - 1
    wide_cap = -(-cap // 128) * 128
    dma = pltpu.SemaphoreType.DMA
    vmem = pl.BlockSpec(memory_space=pltpu.VMEM)
    return pl.pallas_call(
        functools.partial(kernel, (ti_count, tj_count, count, features, sub, cap, chunks, parts_f)),
        out_shape=jax.ShapeDtypeStruct((1, sub), jnp.float32),
        in_specs=[vmem, vmem],
        out_specs=vmem,
        scratch_shapes=[
            pltpu.VMEM((1, count), jnp.int32),
            pltpu.VMEM((16, count), jnp.bfloat16),
            pltpu.VMEM((owners, cap, features), jnp.bfloat16),
            pltpu.VMEM((owners, 16, wide_cap), jnp.bfloat16),
            pltpu.VMEM((owners, cap, features), jnp.bfloat16),
            pltpu.VMEM((owners, 16, wide_cap), jnp.bfloat16),
            pltpu.VMEM((owners, sub, cap), jnp.bfloat16),
            pltpu.VMEM((sub, features // parts_f), jnp.float32),
            pltpu.VMEM((blocks, sub, features), jnp.bfloat16),
            pltpu.VMEM((blocks, sub, features), jnp.bfloat16),
            pltpu.VMEM((row_blocks, chunks, 8, step), jnp.float32),
            pltpu.VMEM((row_blocks, chunks, 8, step), jnp.float32),
            dma((owners, parts_f)), dma((owners, parts_f)), dma((owners,)), dma((owners,)),
            dma((blocks, parts_f, 2)), dma((blocks, parts_f, 2)),
            dma((row_blocks,)), dma((row_blocks,)),
        ],
        compiler_params=pltpu.CompilerParams(
            collective_id=0, has_side_effects=True, vmem_limit_bytes=60 * 1024 * 1024),
    )(slot_of_row, corpus)


def square_kernel(geo, slots_ref, corpus_ref, out_ref, rows, spot, ids_src, picks, send, send_ids,
                  got, got_ids, wall, raw, acc, xbest, ybest, mine, parts,
                  l_sem, d_send, d_recv, i_send, i_recv, g_send, g_recv, p_send, p_recv):
    ti_count, tj_count, count, features, sub, cap, spans, phases = geo
    groups = 2 * tj_count
    homes = groups // 2
    blk = sub * tj_count
    cluster = blk * ti_count
    g, ti, tj = lax.axis_index("grp"), lax.axis_index("ti"), lax.axis_index("tj")
    x, core = ti // CORES, lax.rem(ti, CORES)
    zh, zl = tj // 2, lax.rem(tj, 2)
    lin = g * tj_count + tj
    inner = zl != zh
    outer = jnp.logical_not(inner)

    def dev(gg, tt, jj):
        return {"grp": gg, "ti": tt, "tj": jj}

    def home(o):
        half = o // 2
        return lax.rem(o, 2), half * 2 + 1 - half

    def at(dx, dc, dg=0):
        xx = 1 - x if dx else x
        cc = 1 - core if dc else core
        return dev(1 - g if dg else g, xx * CORES + cc, tj)

    pair_dev = dev(g, ti, zh * 2 + 1 - zl)
    core_dev, x_dev, y_dev = at(0, 1), at(1, 0), at(0, 0, 1)

    barrier = pltpu.get_barrier_semaphore()
    devices = 2 * ti_count * tj_count
    me = (g * ti_count + ti) * tj_count + tj

    def greet(t, _):
        other = lax.rem(me + t, devices)
        pl.semaphore_signal(
            barrier, inc=1, device_id_type=MESH,
            device_id=dev(other // (ti_count * tj_count),
                          lax.rem(other // tj_count, ti_count), lax.rem(other, tj_count)))
        return 0

    piece = 256 if count % 256 == 0 else 128
    pieces = count // piece

    def load(n):
        area = pl.ds(n * piece, piece)
        return pltpu.make_async_copy(corpus_ref.at[0, area, :], rows.at[area, :], l_sem.at[n])

    for n in range(pieces):
        load(n).start()
    lax.fori_loop(1, devices, greet, 0)

    v = slots_ref[...]
    member = v >= 0
    second = (v >= cluster).astype(jnp.int32)
    inblk = v - second * cluster - ti * blk
    s = jnp.zeros_like(v)
    for k in range(1, tj_count):
        s = s + (inblk >= k * sub).astype(jnp.int32)
    pos = inblk - s * sub
    group = jnp.where(member, second * tj_count + s, groups)
    before = (
        lax.broadcasted_iota(jnp.int32, (piece, piece), 0)
        < lax.broadcasted_iota(jnp.int32, (piece, piece), 1)
    ).astype(jnp.bfloat16)
    carry = jnp.zeros((groups, 1), jnp.float32)
    group_iota = lax.broadcasted_iota(jnp.int32, (groups, piece), 0)
    for n in range(pieces):
        part = slice(n * piece, (n + 1) * piece)
        hits = group_iota == group[:, part]
        hot = hits.astype(jnp.float32)
        ranks = dot(hot.astype(jnp.bfloat16), before, NN) + carry
        carry = carry + jnp.sum(hot, axis=1, keepdims=True)
        rank = jnp.sum(jnp.where(hits, ranks, 0.0), axis=0, keepdims=True).astype(jnp.int32)
        spot[:, part] = jnp.where(member[:, part], group[:, part] * cap + rank, groups * cap)
    line = lax.broadcasted_iota(jnp.int32, (16, count), 0)
    ids_src[...] = jnp.where(
        line == 0, pos >> 5, jnp.where(line == 1, pos & 31, (line == 2).astype(jnp.int32))
    ).astype(jnp.float32).astype(jnp.bfloat16)

    def choose(q, _):
        area = pl.ds(pl.multiple_of(q * cap, cap), cap)
        pick = (
            spot[...] == q * cap + lax.broadcasted_iota(jnp.int32, (cap, count), 0)
        ).astype(jnp.float32).astype(jnp.bfloat16)
        picks[area, :] = pick
        send_ids[q, :, :cap] = dot(ids_src[...], pick, NT).astype(jnp.bfloat16)
        return 0

    lax.fori_loop(0, groups, choose, 0)

    thin = piece // 2
    for n in range(pieces):
        load(n).wait()

        def norm(m, _, n=n):
            area = pl.ds(pl.multiple_of(n * piece + m * thin, thin), thin)
            wide = rows[area, :].astype(jnp.float32)
            squares = jnp.sum(wide * wide, axis=1, keepdims=True)
            rows[area, :] = (wide * lax.rsqrt(squares + EPSILON)).astype(jnp.bfloat16)
            return 0

        lax.fori_loop(0, 2, norm, 0)

    lanes = [pl.ds(a, b - a) for a, b in spans]
    last = len(spans) - 1
    far = (1 - zh) * (homes // 2)

    def row_copy(o, src, f):
        hg, hj = home(o)
        return pltpu.make_async_remote_copy(
            send.at[o, :, :, lanes[f]], got.at[:, pl.ds(pl.multiple_of(src * cap, cap), cap), lanes[f]],
            d_send.at[o, f], d_recv.at[src, f], device_id=dev(hg, ti, hj), device_id_type=MESH)

    def id_copy(o, src):
        hg, hj = home(o)
        return pltpu.make_async_remote_copy(
            send_ids.at[pl.ds(o * 2, 2)], got_ids.at[src],
            i_send.at[o], i_recv.at[src], device_id=dev(hg, ti, hj), device_id_type=MESH)

    def is_me(o):
        hg, hj = home(o)
        return jnp.logical_and(hg == g, hj == tj)

    def dispatch(o, fs):
        @pl.when(is_me(o))
        def _():
            if fs[0] == 0:
                pltpu.make_async_copy(
                    send_ids.at[pl.ds(o * 2, 2)], got_ids.at[lin], i_recv.at[lin]).start()
            for f in fs:
                pltpu.make_async_copy(
                    send.at[o, :, :, lanes[f]],
                    got.at[:, pl.ds(pl.multiple_of(lin * cap, cap), cap), lanes[f]],
                    d_recv.at[lin, f]).start()

        @pl.when(jnp.logical_not(is_me(o)))
        def _():
            if fs[0] == 0:
                id_copy(o, lin).start()
            for f in fs:
                row_copy(o, lin, f).start()

    def pack(fs, j):
        o = lax.rem(far + j, homes)
        low, high = spans[fs[0]][0], spans[fs[-1]][1]
        area = pl.ds(pl.multiple_of(o * 2 * cap, 2 * cap), 2 * cap)
        chosen = dot(picks[area, :], rows[:, low:high], NN).astype(jnp.bfloat16)
        send[o, :, :, low:high] = chosen.reshape(2, cap, high - low)

    def pack_all(fs, first):
        def one(j, _):
            pack(fs, j)

            @pl.when(j > 0)
            def _():
                dispatch(lax.rem(far + j - 1, homes), fs)
            return 0

        if first:
            pack(fs, 0)
            pl.semaphore_wait(barrier, devices - 1)
            lax.fori_loop(1, homes, one, 0)
        else:
            lax.fori_loop(0, homes, one, 0)
        dispatch(lax.rem(far + homes - 1, homes), fs)

    runs, f = [], 0
    while f <= last:
        n = f + 1
        while n <= last and spans[n][1] - spans[f][0] <= 256:
            n += 1
        runs.append(list(range(f, n)))
        f = n
    for i, fs in enumerate(runs):
        pack_all(fs, i == 0)

    xbest[...] = jnp.full(xbest.shape, -2.0, jnp.float32)
    ybest[...] = jnp.full(ybest.shape, -2.0, jnp.float32)

    def read_ids():
        for src in range(groups):
            id_copy(0, src).wait_recv()
            for r in range(2):
                wall[r, :, src * cap : (src + 1) * cap] = got_ids[src, r, :, :cap].astype(jnp.float32)
        for r in range(2):
            where = (wall[r, 0:1] * 32.0 + wall[r, 1:2]).astype(jnp.int32)
            where = jnp.where(wall[r, 2:3] > 0.5, where, sub)

            def one(n, _, r=r, where=where):
                area = pl.ds(pl.multiple_of(r * sub + n * 128, 128), 128)
                picks[area, :] = (
                    where == n * 128 + lax.broadcasted_iota(jnp.int32, (128, count), 0)
                ).astype(jnp.float32).astype(jnp.bfloat16)
                return 0

            lax.fori_loop(0, sub // 128, one, 0)

    own, own_c, near_x, near_x_c, near_y, near_y_c, deep, deep_c = range(8)

    def block_copy(source, target, f, device):
        return pltpu.make_async_remote_copy(
            raw.at[source, :, lanes[f]], raw.at[target, :, lanes[f]],
            g_send.at[target, f], g_recv.at[target, f], device_id=device, device_id_type=MESH)

    def arrive(target, f):
        block_copy(own, target, f, core_dev).wait_recv()

    step = sub // 2 if sub % 256 else 256

    def place(f):
        def arrived(src, _):
            row_copy(0, src, f).wait_recv()
            return 0

        lax.fori_loop(0, groups, arrived, 0)
        for r, target in ((1, deep), (0, own)):
            def one(n, _, r=r, target=target):
                area = pl.ds(pl.multiple_of(n * step, step), step)
                chosen = picks[pl.ds(pl.multiple_of(r * sub + n * step, step), step), :]
                raw[target, area, lanes[f]] = dot(chosen, got[r, :, lanes[f]], NN).astype(jnp.bfloat16)
                return 0

            lax.fori_loop(0, sub // step, one, 0)

    def supply(f):
        @pl.when(inner)
        def _():
            if f == 0:
                read_ids()
            place(f)
            block_copy(deep, own, f, pair_dev).start()

        @pl.when(outer)
        def _():
            arrive(own, f)

        block_copy(own, near_y, f, y_dev).start()
        block_copy(own, near_x, f, x_dev).start()
        block_copy(own, own_c, f, core_dev).start()

        @pl.when(inner)
        def _():
            block_copy(deep, deep_c, f, core_dev).start()

    def forward(f):
        arrive(near_y, f)

        @pl.when(inner)
        def _():
            block_copy(near_y, deep, f, pair_dev).start()

        block_copy(near_y, near_y_c, f, core_dev).start()
        arrive(near_x, f)
        block_copy(near_x, near_x_c, f, core_dev).start()

    def collect_near(f):
        arrive(own_c, f)

        @pl.when(inner)
        def _():
            arrive(deep_c, f)

    def collect_rest(f):
        arrive(near_x_c, f)
        arrive(near_y_c, f)

        @pl.when(outer)
        def _():
            arrive(deep, f)

    inner_jobs = [(own, own_c), (own, deep), (own, deep_c), (own, near_x), (near_x, deep), (near_x, deep_c),
                  (own, near_y), (near_y, deep), (near_y, deep_c), (near_x, near_y)]
    outer_jobs = [(own, own_c), (own, near_x), (own, near_y), (near_x, near_y), (deep, near_x), (deep, near_x_c)]
    inner_early, outer_early = 3, 1

    def shift(a, b):
        if (a, b) == (own, near_x) or (a, b) == (near_x, near_y):
            return x
        return g if (a, b) == (own, near_y) else 0

    def table(jobs, j):
        a, b = 0, 0
        for n, (p, q) in enumerate(jobs):
            a = a + jnp.where(j == n, p, 0)
            b = b + jnp.where(j == n, q + shift(p, q), 0)
        return a, b

    def tile(a, b, slot, n, phase, diagonal=False):
        low, high = phases[phase]
        part = pl.ds(pl.multiple_of(n * step, step), step)
        scores = dot(raw[a, part, low:high], raw[b, :, low:high], NT)
        if phase:
            scores = scores + acc[slot, part, :]
        if phase < len(phases) - 1:
            acc[slot, part, :] = scores
            return
        if diagonal:
            same = (
                n * step + lax.broadcasted_iota(jnp.int32, (step, sub), 0)
                == lax.broadcasted_iota(jnp.int32, (step, sub), 1)
            )
            scores = jnp.where(same, -2.0, scores)
        xbest[b] = jnp.maximum(xbest[b], jnp.max(scores.reshape(step // 8, 8, sub), axis=0))
        if diagonal:
            return
        side = scores[:, :128]
        for k in range(1, sub // 128):
            side = jnp.maximum(side, scores[:, k * 128 : (k + 1) * 128])
        y = jnp.minimum(a // 2, 2)
        ybest[y, part, :] = jnp.maximum(ybest[y, part, :], side)

    per = sub // step

    def diagonal(phase):
        def one(n, _):
            tile(own, own, 0, n, phase, True)
            return 0

        lax.fori_loop(0, per, one, 0)

    def others(phase, start, stop):
        def one(n, _):
            j = n // per
            ia, ib = table(inner_jobs, j)
            oa, ob = table(outer_jobs, j)
            tile(jnp.where(inner, ia, oa), jnp.where(inner, ib, ob), j + 1, lax.rem(n, per), phase)
            return 0

        lax.fori_loop(start * per, stop * per, one, 0)

    skip = (lax.rem(x + g, 2) != core).astype(jnp.int32)
    early = jnp.where(inner, inner_early, outer_early)
    total = jnp.where(inner, len(inner_jobs), len(outer_jobs))

    edges = [max(f for f in range(last + 1) if spans[f][1] <= high) for _, high in phases]
    for f in range(last + 1):
        supply(f)
        if f:
            forward(f - 1)
        for phase, edge in enumerate(edges[:-1]):
            if edge == f - 1:
                for e in range(edges[phase - 1] + 1 if phase else 0, edge + 1):
                    collect_near(e)
                    collect_rest(e)
                diagonal(phase)
                others(phase, skip, total)
    final = len(phases) - 1
    left = range(edges[final - 1] + 1 if final else 0, last + 1)
    diagonal(final)
    for e in left:
        collect_near(e)
    others(final, skip, early)
    forward(last)
    for e in left:
        collect_rest(e)
    others(final, early, total)

    sides = [ybest[0], ybest[1], ybest[2]]
    tops = [jnp.max(jnp.transpose(side).reshape(16, 8, sub), axis=0) for side in sides]
    y_of = {own: 0, near_x: 1}
    for b in range(8):
        top = xbest[b]
        if b in y_of:
            top = jnp.maximum(top, tops[y_of[b]])
        if b == near_y:
            top = jnp.maximum(top, jnp.where(inner, tops[2], -2.0))
        if b == deep:
            top = jnp.maximum(top, jnp.where(inner, -2.0, tops[2]))
        mine[b] = jnp.max(top, axis=0, keepdims=True)

    role = outer.astype(jnp.int32)

    def final_dev(b):
        dx, dc, dg = b in (near_x, near_x_c), b in (own_c, near_x_c, near_y_c, deep_c), b in (near_y, near_y_c)
        gg = 1 - g if dg else g
        rr = role
        if b == deep:
            gg = jnp.where(inner, g, 1 - g)
        if b in (deep, deep_c):
            rr = 1 - role
        xx = 1 - x if dx else x
        cc = 1 - core if dc else core
        return zh, xx * CORES + cc, gg * 2 + rr

    def part_copy(b):
        gg, tt, jj = final_dev(b)
        return pltpu.make_async_remote_copy(
            mine.at[b], parts.at[b], p_send.at[b], p_recv.at[b],
            device_id=dev(gg, tt, jj), device_id_type=MESH)

    def stays(b):
        gg, tt, jj = final_dev(b)
        return jnp.logical_and(gg == g, jnp.logical_and(tt == ti, jj == tj))

    def holds(b):
        return inner if b == deep_c else True

    for b in range(8):
        @pl.when(jnp.logical_and(holds(b), stays(b)))
        def _(b=b):
            parts[b] = mine[b]

        @pl.when(jnp.logical_and(holds(b), jnp.logical_not(stays(b))))
        def _(b=b):
            part_copy(b).start()

    half, rr = tj // 2, lax.rem(tj, 2)

    @pl.when(rr == 0)
    def _():
        parts[deep_c] = jnp.full((1, sub), -2.0, jnp.float32)

    def giver(b):
        dx, dc, dg = b in (near_x, near_x_c), b in (own_c, near_x_c, near_y_c, deep_c), b in (near_y, near_y_c)
        gg = 1 - half if dg else half
        plane = rr
        if b == deep:
            gg = jnp.where(rr == 0, 1 - half, half)
        if b in (deep, deep_c):
            plane = 1 - rr
        xx = 1 - x if dx else x
        cc = 1 - core if dc else core
        zz = jnp.where(plane == 0, 1 - g, g)
        return gg, xx * CORES + cc, g * 2 + zz

    for b in range(8):
        gg, tt, jj = giver(b)
        here = jnp.logical_and(gg == g, jnp.logical_and(tt == ti, jj == tj))
        comes = jnp.logical_not(here)
        if b == deep_c:
            comes = jnp.logical_and(comes, rr == 1)

        @pl.when(comes)
        def _(b=b):
            part_copy(b).wait_recv()

    out_ref[...] = jnp.max(parts[...], axis=0)

    for b in range(8):
        @pl.when(jnp.logical_and(holds(b), jnp.logical_not(stays(b))))
        def _(b=b):
            part_copy(b).wait_send()

    def drain(o, _):
        @pl.when(jnp.logical_not(is_me(o)))
        def _():
            id_copy(o, lin).wait_send()
            for f in range(last + 1):
                row_copy(o, lin, f).wait_send()
        return 0

    lax.fori_loop(0, homes, drain, 0)
    for f in range(last + 1):
        for target in (near_y, near_x, own_c, near_y_c, near_x_c):
            block_copy(own, target, f, core_dev).wait_send()

        @pl.when(inner)
        def _(f=f):
            for target in (own, deep_c, deep):
                block_copy(own, target, f, core_dev).wait_send()


def square(corpus, slot_of_row):
    ti_count, tj_count = lax.axis_size("ti"), lax.axis_size("tj")
    _, count, features = corpus.shape
    sub = count // 2
    cap = sub // tj_count
    groups, homes = 2 * tj_count, tj_count
    unit = features // 8
    spans = [(0, 2 * unit), (2 * unit, 4 * unit), (4 * unit, 6 * unit), (6 * unit, 7 * unit), (7 * unit, features)]
    phases = [(0, 4 * unit), (4 * unit, features)]
    wide_cap = -(-cap // 128) * 128
    jobs = 11
    piece = 256 if count % 256 == 0 else 128
    n = len(spans)
    dma = pltpu.SemaphoreType.DMA
    vmem = pl.BlockSpec(memory_space=pltpu.VMEM)
    bf16, f32 = jnp.bfloat16, jnp.float32
    return pl.pallas_call(
        functools.partial(
            square_kernel, (ti_count, tj_count, count, features, sub, cap, spans, phases)),
        out_shape=jax.ShapeDtypeStruct((1, sub), f32),
        in_specs=[vmem, pl.BlockSpec(memory_space=pl.ANY)],
        out_specs=vmem,
        scratch_shapes=[
            pltpu.VMEM((count, features), bf16),
            pltpu.VMEM((1, count), jnp.int32),
            pltpu.VMEM((16, count), bf16),
            pltpu.VMEM((count, count), bf16),
            pltpu.VMEM((homes, 2, cap, features), bf16),
            pltpu.VMEM((groups, 16, wide_cap), bf16),
            pltpu.VMEM((2, groups * cap, features), bf16),
            pltpu.VMEM((groups, 2, 16, wide_cap), bf16),
            pltpu.VMEM((2, 16, count), f32),
            pltpu.VMEM((8, sub, features), bf16),
            pltpu.VMEM((jobs, sub, sub), f32),
            pltpu.VMEM((8, 8, sub), f32),
            pltpu.VMEM((3, sub, 128), f32),
            pltpu.VMEM((8, 1, sub), f32),
            pltpu.VMEM((8, 1, sub), f32),
            dma((count // piece,)),
            dma((homes, n)), dma((groups, n)), dma((homes,)), dma((groups,)),
            dma((8, n)), dma((8, n)), dma((8,)), dma((8,)),
        ],
        compiler_params=pltpu.CompilerParams(
            collective_id=1, has_side_effects=True, vmem_limit_bytes=62 * 1024 * 1024),
    )(slot_of_row, corpus)


def solution(mesh):
    in_specs = (P("grp", ("ti", "tj"), None), P("grp", ("ti", "tj")))
    out_specs = P("grp", ("ti", "tj"))
    is_square = mesh.shape["ti"] == 2 * CORES and mesh.shape["tj"] == 4
    return jax.shard_map(
        square if is_square else per_device, mesh=mesh, in_specs=in_specs, out_specs=out_specs, check_vma=False
    )
```

```python
import functools

import jax
import jax.numpy as jnp
from jax import lax
from jax.experimental import pallas as pl
from jax.experimental.pallas import tpu as pltpu
from jax.sharding import PartitionSpec as P

MESH = pl.DeviceIdType.MESH
NT = (((1,), (1,)), ((), ()))
NN = (((1,), (0,)), ((), ()))
CORES = 2
EPSILON = 1e-06


def dot(a, b, dims):
    return lax.dot_general(a, b, dims, preferred_element_type=jnp.float32)


def kernel(geo, slots_ref, corpus_ref, out_ref, spot, ids_src, send, send_ids, got, got_ids,
           picks, summed, raw, units, best, parts, s_send, s_recv, i_send, i_recv,
           b_send, b_recv, p_send, p_recv):
    ti_count, tj_count, count, features, sub, cap, chunks, parts_f = geo
    width = features // parts_f
    owners = 2 * tj_count
    xs = ti_count // CORES
    zs = tj_count // 2
    blk = sub * tj_count
    cluster = blk * ti_count
    step = sub // chunks
    g, ti, tj = lax.axis_index("grp"), lax.axis_index("ti"), lax.axis_index("tj")
    x, core = ti // CORES, ti % CORES
    zh, zl = tj // zs, tj % zs
    lin = g * tj_count + tj

    def dev(gg, tt, jj):
        return {"grp": gg, "ti": tt, "tj": jj}

    def owner_dev(k):
        d = lax.rem(lin + k, owners)
        return d, dev(d // tj_count, ti, lax.rem(d, tj_count))

    def row_dev(dx, dy):
        return dev(lax.rem(g + dy, 2), lax.rem(x + dx, xs) * CORES + core, tj)

    def col_dev(dc, dz):
        return dev(g, x * CORES + lax.rem(core + dc, CORES), zh * zs + lax.rem(zl + dz, zs))

    def final_dev(dx, dy):
        return dev(zh, lax.rem(x + dx, xs) * CORES + core, lax.rem(g + dy, 2) * zs + zl)

    def feeder_dev(dx, dy):
        return dev(dy, lax.rem(x + dx, xs) * CORES + core, g * zs + zl)

    barrier = pltpu.get_barrier_semaphore()
    greeted = 0
    targets = [owner_dev(k)[1] for k in range(1, owners)]
    targets += [row_dev(dx, dy) for dx in range(1, xs) for dy in range(2)]
    targets += [col_dev(dc, dz) for dc in range(1, CORES) for dz in range(zs)]
    targets += [final_dev(dx, dy) for dx in range(1, xs) for dy in range(2)]
    targets += [feeder_dev(dx, dy) for dx in range(1, xs) for dy in range(2)]
    for target in targets:
        pl.semaphore_signal(barrier, inc=1, device_id=target, device_id_type=MESH)
        greeted += 1

    v = slots_ref[...]
    member = v >= 0
    second = (v >= cluster).astype(jnp.int32)
    inblk = v - second * cluster - ti * blk
    s = jnp.zeros_like(v)
    for k in range(1, tj_count):
        s = s + (inblk >= k * sub).astype(jnp.int32)
    pos = inblk - s * sub
    s_hi = (s >= zs).astype(jnp.int32)
    owner = s_hi * tj_count + second * zs + s - s_hi * zs
    owner = jnp.where(member, owner, owners)
    piece = 256 if count % 256 == 0 else 128
    before = (
        lax.broadcasted_iota(jnp.int32, (piece, piece), 0)
        < lax.broadcasted_iota(jnp.int32, (piece, piece), 1)
    ).astype(jnp.bfloat16)
    carry = jnp.zeros((owners, 1), jnp.float32)
    owner_iota = lax.broadcasted_iota(jnp.int32, (owners, piece), 0)
    for p in range(count // piece):
        part = slice(p * piece, (p + 1) * piece)
        mine = owner_iota == owner[:, part]
        hot = mine.astype(jnp.float32)
        ranks = dot(hot.astype(jnp.bfloat16), before, NN) + carry
        carry = carry + jnp.sum(hot, axis=1, keepdims=True)
        rank = jnp.sum(jnp.where(mine, ranks, 0.0), axis=0, keepdims=True).astype(jnp.int32)
        spot[:, part] = jnp.where(member[:, part], owner[:, part] * cap + rank, owners * cap)
    line = lax.broadcasted_iota(jnp.int32, (16, count), 0)
    ids_src[...] = jnp.where(
        line == 0, pos >> 5, jnp.where(line == 1, pos & 31, (line == 2).astype(jnp.int32))
    ).astype(jnp.float32).astype(jnp.bfloat16)

    row_peers = [(dx, dy) for dx in range(xs) for dy in range(2)]
    col_peers = [(dc, dz) for dc in range(CORES) for dz in range(zs)]
    own = len(row_peers) - 1
    row_at = {peer: i - 1 if i else own for i, peer in enumerate(row_peers)}
    col_at = {peer: own + i for i, peer in enumerate(col_peers)}
    lanes = [pl.ds(f * width, width) for f in range(parts_f)]
    half = sub // 2

    def pick_of(k):
        d = lax.rem(lin + k, owners)
        return (
            spot[...] == d * cap + lax.broadcasted_iota(jnp.int32, (cap, count), 0)
        ).astype(jnp.float32).astype(jnp.bfloat16)

    def row_copy(k, f):
        return pltpu.make_async_remote_copy(
            send.at[k, :, lanes[f]], got.at[k, :, lanes[f]], s_send.at[k, f], s_recv.at[k, f],
            device_id=owner_dev(k)[1], device_id_type=MESH)

    def id_copy(k):
        return pltpu.make_async_remote_copy(
            send_ids.at[k], got_ids.at[k], i_send.at[k], i_recv.at[k],
            device_id=owner_dev(k)[1], device_id_type=MESH)

    def start_pair(k, f):
        if f == 0:
            id_copy(k).start()
        row_copy(k, f).start()

    def pack(f):
        def one(k, _):
            pick = pick_of(k)
            send[k, :, lanes[f]] = dot(pick, corpus_ref[0, :, lanes[f]], NN).astype(jnp.bfloat16)
            if f == 0:
                send_ids[k, :, :cap] = dot(ids_src[...], pick, NT).astype(jnp.bfloat16)

            @pl.when(k > 1)
            def _():
                start_pair(k - 1, f)
            return 0

        lax.fori_loop(1, owners, one, 0)
        pick = pick_of(0)
        got[0, :, lanes[f]] = dot(pick, corpus_ref[0, :, lanes[f]], NN).astype(jnp.bfloat16)
        if f == 0:
            got_ids[0, :, :cap] = dot(ids_src[...], pick, NT).astype(jnp.bfloat16)
        start_pair(owners - 1, f)

    def place(f):
        def one(k, first):
            if f == 0:
                line_ids = got_ids[k, :, :cap].astype(jnp.float32)
                where = (line_ids[0:1] * 32.0 + line_ids[1:2]).astype(jnp.int32)
                where = jnp.where(line_ids[2:3] > 0.5, where, sub)
                picks[k] = (
                    where == lax.broadcasted_iota(jnp.int32, (sub, cap), 0)
                ).astype(jnp.float32).astype(jnp.bfloat16)
            term = dot(picks[k], got[k, :, lanes[f]], NN)
            summed[...] = term if first else summed[...] + term

        def arrived(k, _):
            if f == 0:
                id_copy(k).wait_recv()
            row_copy(k, f).wait_recv()
            one(k, False)
            return 0

        one(0, True)
        lax.fori_loop(1, owners, arrived, 0)

    started, waited = [], set()

    def block_copy(source, target, f, h, device):
        area = (pl.ds(h * half, half), lanes[f])
        return pltpu.make_async_remote_copy(
            raw.at[(source,) + area], raw.at[(target,) + area],
            b_send.at[target, f, h], b_recv.at[target, f, h],
            device_id=device, device_id_type=MESH)

    def ship(source, target, f, h, device):
        copy = block_copy(source, target, f, h, device)
        copy.start()
        started.append(copy)

    def need(block, f, h):
        if (block, f, h) not in waited:
            waited.add((block, f, h))
            block_copy(own, block, f, h, row_dev(0, 1)).wait_recv()

    def launch(f):
        for n in range(2):
            for dx, dy in row_peers[1:]:
                if xs == 2 and dx and dy:
                    continue
                ship(own, row_at[(-dx) % xs, (-dy) % 2], f, 1 - n if dy else n, row_dev(dx, dy))
            for dc, dz in col_peers[1:]:
                if zs == 2 and dc and dz:
                    continue
                ship(own, col_at[(-dc) % CORES, (-dz) % zs], f, n, col_dev(dc, dz))

    def relay(f):
        if xs == 2:
            need(row_at[1, 0], f, 0)
            ship(row_at[1, 0], row_at[1, 1], f, 0, row_dev(0, 1))
            need(row_at[0, 1], f, 1)
            ship(row_at[0, 1], row_at[1, 1], f, 1, row_dev(1, 0))
        if zs == 2:
            for h in range(2):
                need(col_at[0, 1], f, h)
                ship(col_at[0, 1], col_at[1, 1], f, h, col_dev(1, 0))

    pl.semaphore_wait(barrier, greeted)
    ahead = 2
    for f in range(min(ahead, parts_f)):
        pack(f)
    for f in range(parts_f):
        place(f)
        raw[own, :, lanes[f]] = summed[...].astype(jnp.bfloat16)
        if f == 0:
            best[...] = jnp.full(best.shape, -2.0, jnp.float32)
        if f:
            relay(f - 1)
        launch(f)
        if f + ahead < parts_f:
            pack(f + ahead)

    def norm(block):
        for f in range(parts_f):
            for h in range(2):
                if block != own:
                    need(block, f, h)

        def one(n, _):
            area = pl.ds(pl.multiple_of(n * 128, 128), 128)
            wide = raw[block, area, :].astype(jnp.float32)
            squares = jnp.sum(wide * wide, axis=1, keepdims=True)
            units[block, area, :] = (wide * lax.rsqrt(squares + EPSILON)).astype(jnp.bfloat16)
            return 0

        lax.fori_loop(0, sub // 128, one, 0)

    def tile(row, i, col, diagonal=False):
        part = pl.ds(pl.multiple_of(i * step, step), step)
        scores = dot(units[own + col], units[row, part, :], NT)
        if diagonal:
            same = (
                lax.broadcasted_iota(jnp.int32, (sub, step), 0)
                == i * step + lax.broadcasted_iota(jnp.int32, (sub, step), 1)
            )
            scores = jnp.where(same, -2.0, scores)
        top = jnp.max(scores.reshape(sub // 8, 8, step), axis=0)
        best[row, i] = jnp.maximum(best[row, i], top)
        return 0

    norm(own)
    lax.fori_loop(0, chunks, lambda i, _: tile(own, i, 0, True), 0)
    relay(parts_f - 1)
    for col in range(1, len(col_peers)):
        norm(own + col)
        lax.fori_loop(0, chunks, lambda i, _, col=col: tile(own, i, col), 0)

    def part_copy(peer):
        return pltpu.make_async_remote_copy(
            best.at[row_at[peer]], parts.at[x * 2 + g],
            p_send.at[row_at[peer]], p_recv.at[x * 2 + g],
            device_id=final_dev(*peer), device_id_type=MESH)

    stays = zh == g

    @pl.when(stays)
    def _():
        parts[x * 2 + g] = best[own]

    @pl.when(jnp.logical_not(stays))
    def _():
        part_copy((0, 0)).start()

    order = [peer for peer in row_peers[1:] if not (peer[0] and peer[1])]
    order += [peer for peer in row_peers[1:] if peer[0] and peer[1]]
    total = chunks * len(col_peers)
    for peer in order:
        row = row_at[peer]
        norm(row)
        lax.fori_loop(
            0, total, lambda n, _, row=row: tile(row, n // len(col_peers), n % len(col_peers)), 0)
        part_copy(peer).start()

    for feeder in range(len(row_peers)):
        arrived = pltpu.make_async_remote_copy(
            best.at[0], parts.at[feeder], p_send.at[0], p_recv.at[feeder],
            device_id=row_dev(0, 1), device_id_type=MESH)
        here = jnp.logical_and(stays, x * 2 + g == feeder)

        @pl.when(jnp.logical_not(here))
        def _(arrived=arrived):
            arrived.wait_recv()
    for i in range(chunks):
        top = jnp.max(parts[:, i], axis=0)
        out_ref[:, i * step : (i + 1) * step] = jnp.max(top, axis=0, keepdims=True)

    @pl.when(jnp.logical_not(stays))
    def _():
        part_copy((0, 0)).wait_send()

    for peer in row_peers[1:]:
        part_copy(peer).wait_send()
    for copy in started:
        copy.wait_send()

    def drain(k, _):
        id_copy(k).wait_send()
        for f in range(parts_f):
            row_copy(k, f).wait_send()
        return 0

    lax.fori_loop(1, owners, drain, 0)


def per_device(corpus, slot_of_row):
    ti_count, tj_count = lax.axis_size("ti"), lax.axis_size("tj")
    _, count, features = corpus.shape
    sub = count // 2
    cap = sub // tj_count
    owners = 2 * tj_count
    chunks, parts_f = 1, 4
    step = sub // chunks
    row_blocks, col_blocks = ti_count // CORES * 2, tj_count // 2 * CORES
    blocks = row_blocks + col_blocks - 1
    wide_cap = -(-cap // 128) * 128
    dma = pltpu.SemaphoreType.DMA
    vmem = pl.BlockSpec(memory_space=pltpu.VMEM)
    return pl.pallas_call(
        functools.partial(kernel, (ti_count, tj_count, count, features, sub, cap, chunks, parts_f)),
        out_shape=jax.ShapeDtypeStruct((1, sub), jnp.float32),
        in_specs=[vmem, vmem],
        out_specs=vmem,
        scratch_shapes=[
            pltpu.VMEM((1, count), jnp.int32),
            pltpu.VMEM((16, count), jnp.bfloat16),
            pltpu.VMEM((owners, cap, features), jnp.bfloat16),
            pltpu.VMEM((owners, 16, wide_cap), jnp.bfloat16),
            pltpu.VMEM((owners, cap, features), jnp.bfloat16),
            pltpu.VMEM((owners, 16, wide_cap), jnp.bfloat16),
            pltpu.VMEM((owners, sub, cap), jnp.bfloat16),
            pltpu.VMEM((sub, features // parts_f), jnp.float32),
            pltpu.VMEM((blocks, sub, features), jnp.bfloat16),
            pltpu.VMEM((blocks, sub, features), jnp.bfloat16),
            pltpu.VMEM((row_blocks, chunks, 8, step), jnp.float32),
            pltpu.VMEM((row_blocks, chunks, 8, step), jnp.float32),
            dma((owners, parts_f)), dma((owners, parts_f)), dma((owners,)), dma((owners,)),
            dma((blocks, parts_f, 2)), dma((blocks, parts_f, 2)),
            dma((row_blocks,)), dma((row_blocks,)),
        ],
        compiler_params=pltpu.CompilerParams(
            collective_id=0, has_side_effects=True, vmem_limit_bytes=60 * 1024 * 1024),
    )(slot_of_row, corpus)


def square_kernel(geo, slots_ref, corpus_ref, out_ref, rows, spot, ids_src, picks, send, send_ids, hop,
                  got, got_ids, wall, raw, acc, xbest, ybest, mine, parts,
                  l_sem, d_send, d_recv, h_send, h_recv, i_send, i_recv, g_send, g_recv, p_send, p_recv):
    ti_count, tj_count, count, features, sub, cap, spans, phases = geo
    groups = 2 * tj_count
    homes = groups // 2
    blk = sub * tj_count
    cluster = blk * ti_count
    g, ti, tj = lax.axis_index("grp"), lax.axis_index("ti"), lax.axis_index("tj")
    x, core = ti // CORES, lax.rem(ti, CORES)
    zh, zl = tj // 2, lax.rem(tj, 2)
    lin = g * tj_count + tj
    inner = zl != zh
    outer = jnp.logical_not(inner)

    def dev(gg, tt, jj):
        return {"grp": gg, "ti": tt, "tj": jj}

    def home(o):
        half = o // 2
        return lax.rem(o, 2), half * 2 + 1 - half

    def at(dx, dc, dg=0):
        xx = 1 - x if dx else x
        cc = 1 - core if dc else core
        return dev(1 - g if dg else g, xx * CORES + cc, tj)

    pair_dev = dev(g, ti, zh * 2 + 1 - zl)
    core_dev, x_dev, y_dev = at(0, 1), at(1, 0), at(0, 0, 1)

    barrier = pltpu.get_barrier_semaphore()
    devices = 2 * ti_count * tj_count
    me = (g * ti_count + ti) * tj_count + tj

    def greet(t, _):
        other = lax.rem(me + t, devices)
        pl.semaphore_signal(
            barrier, inc=1, device_id_type=MESH,
            device_id=dev(other // (ti_count * tj_count),
                          lax.rem(other // tj_count, ti_count), lax.rem(other, tj_count)))
        return 0

    piece = 256 if count % 256 == 0 else 128
    pieces = count // piece

    def load(n):
        area = pl.ds(n * piece, piece)
        return pltpu.make_async_copy(corpus_ref.at[0, area, :], rows.at[area, :], l_sem.at[n])

    for n in range(pieces):
        load(n).start()
    lax.fori_loop(1, devices, greet, 0)

    v = slots_ref[...]
    member = v >= 0
    second = (v >= cluster).astype(jnp.int32)
    inblk = v - second * cluster - ti * blk
    s = jnp.zeros_like(v)
    for k in range(1, tj_count):
        s = s + (inblk >= k * sub).astype(jnp.int32)
    pos = inblk - s * sub
    group = jnp.where(member, second * tj_count + s, groups)
    before = (
        lax.broadcasted_iota(jnp.int32, (piece, piece), 0)
        < lax.broadcasted_iota(jnp.int32, (piece, piece), 1)
    ).astype(jnp.bfloat16)
    carry = jnp.zeros((groups, 1), jnp.float32)
    group_iota = lax.broadcasted_iota(jnp.int32, (groups, piece), 0)
    for n in range(pieces):
        part = slice(n * piece, (n + 1) * piece)
        hits = group_iota == group[:, part]
        hot = hits.astype(jnp.float32)
        ranks = dot(hot.astype(jnp.bfloat16), before, NN) + carry
        carry = carry + jnp.sum(hot, axis=1, keepdims=True)
        rank = jnp.sum(jnp.where(hits, ranks, 0.0), axis=0, keepdims=True).astype(jnp.int32)
        spot[:, part] = jnp.where(member[:, part], group[:, part] * cap + rank, groups * cap)
    line = lax.broadcasted_iota(jnp.int32, (16, count), 0)
    ids_src[...] = jnp.where(
        line == 0, pos >> 5, jnp.where(line == 1, pos & 31, (line == 2).astype(jnp.int32))
    ).astype(jnp.float32).astype(jnp.bfloat16)

    def choose(q, _):
        area = pl.ds(pl.multiple_of(q * cap, cap), cap)
        pick = (
            spot[...] == q * cap + lax.broadcasted_iota(jnp.int32, (cap, count), 0)
        ).astype(jnp.float32).astype(jnp.bfloat16)
        picks[area, :] = pick
        return 0

    lax.fori_loop(0, groups, choose, 0)

    thin = piece // 2
    for n in range(pieces):
        load(n).wait()

        def norm(m, _, n=n):
            area = pl.ds(pl.multiple_of(n * piece + m * thin, thin), thin)
            wide = rows[area, :].astype(jnp.float32)
            squares = jnp.sum(wide * wide, axis=1, keepdims=True)
            rows[area, :] = (wide * lax.rsqrt(squares + EPSILON)).astype(jnp.bfloat16)
            return 0

        lax.fori_loop(0, 2, norm, 0)

    lanes = [pl.ds(a, b - a) for a, b in spans]
    last = len(spans) - 1
    lin_y = (1 - g) * tj_count + tj

    def seat(src):
        return pl.ds(pl.multiple_of(src * cap, cap), cap)

    def row_copy(o, src, f):
        hg, hj = home(o)
        return pltpu.make_async_remote_copy(
            send.at[o, :, :, lanes[f]], got.at[:, seat(src), lanes[f]],
            d_send.at[o, f], d_recv.at[src, f], device_id=dev(hg, ti, hj), device_id_type=MESH)

    def hop_copy(o, half, f):
        return pltpu.make_async_remote_copy(
            send.at[o, :, :, lanes[f]], hop.at[half, :, :, lanes[f]],
            d_send.at[o, f], h_recv.at[half, f], device_id=y_dev, device_id_type=MESH)

    def relay_copy(half, f):
        hg, hj = home(half * 2 + g)
        return pltpu.make_async_remote_copy(
            hop.at[half, :, :, lanes[f]], got.at[:, seat(lin_y), lanes[f]],
            h_send.at[half, f], d_recv.at[lin_y, f], device_id=dev(hg, ti, hj), device_id_type=MESH)

    def id_copy(o, src):
        hg, hj = home(o)
        return pltpu.make_async_remote_copy(
            send_ids.at[pl.ds(o * 2, 2)], got_ids.at[src],
            i_send.at[o], i_recv.at[src], device_id=dev(hg, ti, hj), device_id_type=MESH)

    def is_me(o):
        hg, hj = home(o)
        return jnp.logical_and(hg == g, hj == tj)

    def level(half):
        return home(half * 2)[1] == tj

    halves = (1 - zh, zh)

    def send_ids_out():
        def one(o, _):
            for q in (o * 2, o * 2 + 1):
                pick = picks[pl.ds(pl.multiple_of(q * cap, cap), cap), :]
                send_ids[q, :, :cap] = dot(ids_src[...], pick, NT).astype(jnp.bfloat16)

            @pl.when(is_me(o))
            def _():
                pltpu.make_async_copy(
                    send_ids.at[pl.ds(o * 2, 2)], got_ids.at[lin], i_recv.at[lin]).start()

            @pl.when(jnp.logical_not(is_me(o)))
            def _():
                id_copy(o, lin).start()
            return 0

        lax.fori_loop(0, homes, one, 0)

    def send_y(f, only=halves):
        for half in only:
            o = half * 2 + 1 - g

            @pl.when(level(half))
            def _(o=o):
                row_copy(o, lin, f).start()

            @pl.when(jnp.logical_not(level(half)))
            def _(o=o, half=half):
                hop_copy(o, half, f).start()

    def send_z(f, only=halves):
        for half in only:
            o = half * 2 + g

            @pl.when(level(half))
            def _(o=o):
                pltpu.make_async_copy(
                    send.at[o, :, :, lanes[f]], got.at[:, seat(lin), lanes[f]], d_recv.at[lin, f]).start()

            @pl.when(jnp.logical_not(level(half)))
            def _(o=o):
                row_copy(o, lin, f).start()

    def relay(f):
        for half in halves:
            @pl.when(jnp.logical_not(level(half)))
            def _(half=half):
                hop_copy(half * 2, half, f).wait_recv()
                relay_copy(half, f).start()

    def pack(fs, first=0, stop=2):
        low, high = spans[fs[0]][0], spans[fs[-1]][1]

        def one(j, _):
            half = lax.rem(1 - zh + j, 2)
            area = pl.ds(pl.multiple_of(half * sub, sub), sub)
            chosen = dot(picks[area, :], rows[:, low:high], NN).astype(jnp.bfloat16)
            send[pl.ds(half * 2, 2), :, :, low:high] = chosen.reshape(2, 2, cap, high - low)
            return 0

        lax.fori_loop(first, stop, one, 0)

    pack([0], 0, 1)
    pl.semaphore_wait(barrier, devices - 1)
    send_y(0, halves[:1])
    send_z(0, halves[:1])
    pack([0], 1, 2)
    send_y(0, halves[1:])
    send_z(0, halves[1:])
    pack([1])
    send_y(1)
    send_ids_out()
    pack([2])
    relay(0)
    send_z(1)
    send_y(2)
    pack([3, 4])
    relay(1)
    send_z(2)

    xbest[...] = jnp.full(xbest.shape, -2.0, jnp.float32)
    ybest[...] = jnp.full(ybest.shape, -2.0, jnp.float32)

    def read_ids():
        for src in range(groups):
            id_copy(0, src).wait_recv()
            for r in range(2):
                wall[r, :, src * cap : (src + 1) * cap] = got_ids[src, r, :, :cap].astype(jnp.float32)
        for r in range(2):
            where = (wall[r, 0:1] * 32.0 + wall[r, 1:2]).astype(jnp.int32)
            where = jnp.where(wall[r, 2:3] > 0.5, where, sub)

            def one(n, _, r=r, where=where):
                area = pl.ds(pl.multiple_of(r * sub + n * 128, 128), 128)
                picks[area, :] = (
                    where == n * 128 + lax.broadcasted_iota(jnp.int32, (128, count), 0)
                ).astype(jnp.float32).astype(jnp.bfloat16)
                return 0

            lax.fori_loop(0, sub // 128, one, 0)

    own, own_c, near_x, near_x_c, near_y, near_y_c, deep, deep_c, skew = range(9)
    left, right = core == 0, core == 1

    def block_copy(source, target, f, device):
        return pltpu.make_async_remote_copy(
            raw.at[source, :, lanes[f]], raw.at[target, :, lanes[f]],
            g_send.at[target, f], g_recv.at[target, f], device_id=device, device_id_type=MESH)

    def arrive(target, f):
        block_copy(own, target, f, core_dev).wait_recv()

    def place(f):
        def arrived(src, _):
            row_copy(0, src, f).wait_recv()
            return 0

        lax.fori_loop(0, groups, arrived, 0)
        for r, target in ((1, deep), (0, own)):
            chosen = picks[r * sub : (r + 1) * sub, :]
            raw[target, :, lanes[f]] = dot(chosen, got[r, :, lanes[f]], NN).astype(jnp.bfloat16)

    def supply(f):
        @pl.when(inner)
        def _():
            if f == 0:
                read_ids()
            place(f)
            block_copy(deep, own, f, pair_dev).start()

        @pl.when(outer)
        def _():
            arrive(own, f)

        block_copy(own, near_y, f, y_dev).start()
        block_copy(own, near_x, f, x_dev).start()
        block_copy(own, own_c, f, core_dev).start()

        @pl.when(inner)
        def _():
            block_copy(deep, deep_c, f, core_dev).start()

    def forward(f):
        arrive(near_y, f)

        @pl.when(jnp.logical_and(inner, left))
        def _():
            block_copy(near_y, deep, f, pair_dev).start()

        @pl.when(jnp.logical_and(inner, right))
        def _():
            block_copy(near_y, skew, f, x_dev).start()

        block_copy(near_y, near_y_c, f, core_dev).start()
        arrive(near_x, f)
        block_copy(near_x, near_x_c, f, core_dev).start()

    def collect_near(f):
        arrive(own_c, f)

        @pl.when(inner)
        def _():
            arrive(deep_c, f)

    def collect_rest(f):
        arrive(near_x_c, f)
        arrive(near_y_c, f)

        @pl.when(jnp.logical_and(outer, left))
        def _():
            arrive(deep, f)

    inner_jobs = [(own, own_c), (own, deep), (own, deep_c), (own, near_x), (near_x, deep), (near_x, deep_c),
                  (own, near_y), (near_y, deep), (near_y, deep_c), (near_x, near_y)]
    outer_jobs = [(own, own_c), (own, near_x), (own, near_y), (near_x, near_y), (deep, near_x), (deep, near_x_c)]
    inner_early, outer_early = 3, 1

    def shift(a, b):
        if (a, b) == (own, near_x) or (a, b) == (near_x, near_y):
            return x
        return g if (a, b) == (own, near_y) else 0

    def table(jobs, j):
        a, b = 0, 0
        for n, (p, q) in enumerate(jobs):
            a = a + jnp.where(j == n, p, 0)
            b = b + jnp.where(j == n, q + shift(p, q), 0)
        return a, b

    def tile(a, b, slot, phase, diagonal=False):
        low, high = phases[phase] if slot is not None else (0, features)
        scores = dot(raw[a, :, low:high], raw[b, :, low:high], NT)
        if phase and slot is not None:
            scores = scores + acc[slot]
        if phase < len(phases) - 1:
            acc[slot] = scores
            return
        if diagonal:
            same = (
                lax.broadcasted_iota(jnp.int32, (sub, sub), 0)
                == lax.broadcasted_iota(jnp.int32, (sub, sub), 1)
            )
            scores = jnp.where(same, -2.0, scores)
        xbest[b] = jnp.maximum(xbest[b], jnp.max(scores.reshape(sub // 8, 8, sub), axis=0))
        if diagonal:
            return
        side = scores[:, :128]
        for k in range(1, sub // 128):
            side = jnp.maximum(side, scores[:, k * 128 : (k + 1) * 128])
        y = 3 if slot is None else jnp.minimum(a // 2, 2)
        ybest[y] = jnp.maximum(ybest[y], side)

    def diagonal(phase):
        tile(own, own, 0, phase, True)

    def others(phase, start, stop):
        def one(j, _):
            ia, ib = table(inner_jobs, j)
            oa, ob = table(outer_jobs, j)
            tile(jnp.where(inner, ia, oa), jnp.where(inner, ib, ob), j + 1, phase)
            return 0

        lax.fori_loop(start, stop, one, 0)

    skip = (lax.rem(x + g, 2) != core).astype(jnp.int32)
    early = jnp.where(inner, inner_early, outer_early)
    total = jnp.where(inner, len(inner_jobs), jnp.where(left, len(outer_jobs), len(outer_jobs) - 2))

    def collect(f):
        collect_near(f)
        collect_rest(f)

    def score(phase):
        diagonal(phase)
        others(phase, skip, total)

    supply(0)
    send_y(3)
    send_y(4)
    relay(2)
    send_z(3)
    send_z(4)
    relay(3)
    relay(4)
    forward(0)
    supply(1)
    forward(1)
    supply(2)
    collect(0)
    collect(1)
    score(0)
    forward(2)
    supply(3)
    forward(3)
    final = len(phases) - 1
    if final == 2:
        collect(2)
        score(1)
    supply(4)
    diagonal(final)
    for f in range(3 if final == 2 else 2, 5):
        collect_near(f)
    others(final, skip, early)
    forward(4)
    for f in range(3 if final == 2 else 2, 5):
        collect_rest(f)
    others(final, early, total)

    def score_skew():
        @pl.when(jnp.logical_and(inner, right))
        def _():
            for f in range(last + 1):
                arrive(skew, f)

            def one(n, _):
                tile(skew, deep + n, None, final)
                return 0

            lax.fori_loop(0, 2, one, 0)

    score_skew()
    sides = [ybest[n] for n in range(4)]
    tops = [jnp.max(jnp.transpose(side).reshape(16, 8, sub), axis=0) for side in sides]
    y_of = {own: 0, near_x: 1, skew: 3}
    for b in range(9):
        top = tops[3] if b == skew else xbest[b]
        if b in y_of and b != skew:
            top = jnp.maximum(top, tops[y_of[b]])
        if b == near_y:
            top = jnp.maximum(top, jnp.where(inner, tops[2], -2.0))
        if b == deep:
            top = jnp.maximum(top, jnp.where(inner, -2.0, tops[2]))
        mine[b] = jnp.max(top, axis=0, keepdims=True)

    role = outer.astype(jnp.int32)

    def final_dev(b):
        dx, dc, dg = b in (near_x, near_x_c, skew), b in (own_c, near_x_c, near_y_c, deep_c), b in (near_y, near_y_c, skew)
        gg = 1 - g if dg else g
        rr = role
        if b == deep:
            gg = jnp.where(inner, g, 1 - g)
        if b in (deep, deep_c):
            rr = 1 - role
        xx = 1 - x if dx else x
        cc = 1 - core if dc else core
        return zh, xx * CORES + cc, gg * 2 + rr

    def part_copy(b):
        gg, tt, jj = final_dev(b)
        return pltpu.make_async_remote_copy(
            mine.at[b], parts.at[deep if b == skew else b], p_send.at[b],
            p_recv.at[deep if b == skew else b],
            device_id=dev(gg, tt, jj), device_id_type=MESH)

    def stays(b):
        gg, tt, jj = final_dev(b)
        return jnp.logical_and(gg == g, jnp.logical_and(tt == ti, jj == tj))

    def holds(b):
        if b == deep_c:
            return inner
        if b == deep:
            return jnp.logical_or(inner, left)
        return jnp.logical_and(inner, right) if b == skew else True

    for b in range(9):
        @pl.when(jnp.logical_and(holds(b), stays(b)))
        def _(b=b):
            parts[deep if b == skew else b] = mine[b]

        @pl.when(jnp.logical_and(holds(b), jnp.logical_not(stays(b))))
        def _(b=b):
            part_copy(b).start()

    half, rr = tj // 2, lax.rem(tj, 2)

    @pl.when(rr == 0)
    def _():
        parts[deep_c] = jnp.full((1, sub), -2.0, jnp.float32)

    def giver(b):
        dx, dc, dg = b in (near_x, near_x_c), b in (own_c, near_x_c, near_y_c, deep_c), b in (near_y, near_y_c)
        gg = 1 - half if dg else half
        plane = rr
        xx = 1 - x if dx else x
        if b == deep:
            gg = jnp.where(rr == 0, 1 - half, half)
            xx = jnp.where(jnp.logical_and(rr == 0, right), 1 - x, x)
            plane = jnp.where(jnp.logical_and(rr == 0, left), 1, 0)
        if b == deep_c:
            plane = 1 - rr
        cc = 1 - core if dc else core
        zz = jnp.where(plane == 0, 1 - g, g)
        return gg, xx * CORES + cc, g * 2 + zz

    for b in range(8):
        gg, tt, jj = giver(b)
        here = jnp.logical_and(gg == g, jnp.logical_and(tt == ti, jj == tj))
        comes = jnp.logical_not(here)
        if b == deep_c:
            comes = jnp.logical_and(comes, rr == 1)

        @pl.when(comes)
        def _(b=b):
            part_copy(b).wait_recv()

    out_ref[...] = jnp.max(parts[...], axis=0)

    for b in range(9):
        @pl.when(jnp.logical_and(holds(b), jnp.logical_not(stays(b))))
        def _(b=b):
            part_copy(b).wait_send()

    def drain(o, _):
        @pl.when(jnp.logical_not(is_me(o)))
        def _():
            id_copy(o, lin).wait_send()
            for f in range(last + 1):
                row_copy(o, lin, f).wait_send()
        return 0

    lax.fori_loop(0, homes, drain, 0)
    for half in halves:
        @pl.when(jnp.logical_not(level(half)))
        def _(half=half):
            for f in range(last + 1):
                relay_copy(half, f).wait_send()
    for f in range(last + 1):
        for target in (near_y, near_x, own_c, near_y_c, near_x_c):
            block_copy(own, target, f, core_dev).wait_send()

        @pl.when(inner)
        def _(f=f):
            for target in (own, deep_c):
                block_copy(own, target, f, core_dev).wait_send()

        @pl.when(jnp.logical_and(inner, left))
        def _(f=f):
            block_copy(own, deep, f, core_dev).wait_send()

        @pl.when(jnp.logical_and(inner, right))
        def _(f=f):
            block_copy(own, skew, f, core_dev).wait_send()


def square(corpus, slot_of_row):
    ti_count, tj_count = lax.axis_size("ti"), lax.axis_size("tj")
    _, count, features = corpus.shape
    sub = count // 2
    cap = sub // tj_count
    groups, homes = 2 * tj_count, tj_count
    unit = features // 8
    spans = [(0, 2 * unit), (2 * unit, 4 * unit), (4 * unit, 6 * unit), (6 * unit, 7 * unit), (7 * unit, features)]
    phases = [(0, 4 * unit), (4 * unit, 6 * unit), (6 * unit, features)]
    wide_cap = -(-cap // 128) * 128
    jobs = 11
    piece = 256 if count % 256 == 0 else 128
    n = len(spans)
    dma = pltpu.SemaphoreType.DMA
    vmem = pl.BlockSpec(memory_space=pltpu.VMEM)
    bf16, f32 = jnp.bfloat16, jnp.float32
    return pl.pallas_call(
        functools.partial(
            square_kernel, (ti_count, tj_count, count, features, sub, cap, spans, phases)),
        out_shape=jax.ShapeDtypeStruct((1, sub), f32),
        in_specs=[vmem, pl.BlockSpec(memory_space=pl.ANY)],
        out_specs=vmem,
        scratch_shapes=[
            pltpu.VMEM((count, features), bf16),
            pltpu.VMEM((1, count), jnp.int32),
            pltpu.VMEM((16, count), bf16),
            pltpu.VMEM((count, count), bf16),
            pltpu.VMEM((homes, 2, cap, features), bf16),
            pltpu.VMEM((groups, 16, wide_cap), bf16),
            pltpu.VMEM((2, 2, cap, features), bf16),
            pltpu.VMEM((2, groups * cap, features), bf16),
            pltpu.VMEM((groups, 2, 16, wide_cap), bf16),
            pltpu.VMEM((2, 16, count), f32),
            pltpu.VMEM((9, sub, features), bf16),
            pltpu.VMEM((jobs, sub, sub), f32),
            pltpu.VMEM((8, 8, sub), f32),
            pltpu.VMEM((4, sub, 128), f32),
            pltpu.VMEM((9, 1, sub), f32),
            pltpu.VMEM((8, 1, sub), f32),
            dma((count // piece,)),
            dma((homes, n)), dma((groups, n)), dma((2, n)), dma((2, n)), dma((homes,)), dma((groups,)),
            dma((9, n)), dma((9, n)), dma((9,)), dma((8,)),
        ],
        compiler_params=pltpu.CompilerParams(
            collective_id=1, has_side_effects=True, vmem_limit_bytes=63 * 1024 * 1024),
    )(slot_of_row, corpus)


def solution(mesh):
    in_specs = (P("grp", ("ti", "tj"), None), P("grp", ("ti", "tj")))
    out_specs = P("grp", ("ti", "tj"))
    is_square = mesh.shape["ti"] == 2 * CORES and mesh.shape["tj"] == 4
    return jax.shard_map(
        square if is_square else per_device, mesh=mesh, in_specs=in_specs, out_specs=out_specs, check_vma=False
    )
```

```python
import functools

import jax
import jax.numpy as jnp
from jax import lax
from jax.experimental import pallas as pl
from jax.experimental.pallas import tpu as pltpu
from jax.sharding import PartitionSpec as P

MESH = pl.DeviceIdType.MESH
NT = (((1,), (1,)), ((), ()))
NN = (((1,), (0,)), ((), ()))
CORES = 2
EPSILON = 1e-06


def dot(a, b, dims):
    return lax.dot_general(a, b, dims, preferred_element_type=jnp.float32)


def kernel(geo, slots_ref, corpus_ref, out_ref, spot, ids_src, send, send_ids, got, got_ids,
           picks, summed, raw, units, best, parts, s_send, s_recv, i_send, i_recv,
           b_send, b_recv, p_send, p_recv):
    ti_count, tj_count, count, features, sub, cap, chunks, parts_f = geo
    width = features // parts_f
    owners = 2 * tj_count
    xs = ti_count // CORES
    zs = tj_count // 2
    blk = sub * tj_count
    cluster = blk * ti_count
    step = sub // chunks
    g, ti, tj = lax.axis_index("grp"), lax.axis_index("ti"), lax.axis_index("tj")
    x, core = ti // CORES, ti % CORES
    zh, zl = tj // zs, tj % zs
    lin = g * tj_count + tj

    def dev(gg, tt, jj):
        return {"grp": gg, "ti": tt, "tj": jj}

    def owner_dev(k):
        d = lax.rem(lin + k, owners)
        return d, dev(d // tj_count, ti, lax.rem(d, tj_count))

    def row_dev(dx, dy):
        return dev(lax.rem(g + dy, 2), lax.rem(x + dx, xs) * CORES + core, tj)

    def col_dev(dc, dz):
        return dev(g, x * CORES + lax.rem(core + dc, CORES), zh * zs + lax.rem(zl + dz, zs))

    def final_dev(dx, dy):
        return dev(zh, lax.rem(x + dx, xs) * CORES + core, lax.rem(g + dy, 2) * zs + zl)

    def feeder_dev(dx, dy):
        return dev(dy, lax.rem(x + dx, xs) * CORES + core, g * zs + zl)

    barrier = pltpu.get_barrier_semaphore()
    greeted = 0
    targets = [owner_dev(k)[1] for k in range(1, owners)]
    targets += [row_dev(dx, dy) for dx in range(1, xs) for dy in range(2)]
    targets += [col_dev(dc, dz) for dc in range(1, CORES) for dz in range(zs)]
    targets += [final_dev(dx, dy) for dx in range(1, xs) for dy in range(2)]
    targets += [feeder_dev(dx, dy) for dx in range(1, xs) for dy in range(2)]
    for target in targets:
        pl.semaphore_signal(barrier, inc=1, device_id=target, device_id_type=MESH)
        greeted += 1

    v = slots_ref[...]
    member = v >= 0
    second = (v >= cluster).astype(jnp.int32)
    inblk = v - second * cluster - ti * blk
    s = jnp.zeros_like(v)
    for k in range(1, tj_count):
        s = s + (inblk >= k * sub).astype(jnp.int32)
    pos = inblk - s * sub
    s_hi = (s >= zs).astype(jnp.int32)
    owner = s_hi * tj_count + second * zs + s - s_hi * zs
    owner = jnp.where(member, owner, owners)
    piece = 256 if count % 256 == 0 else 128
    before = (
        lax.broadcasted_iota(jnp.int32, (piece, piece), 0)
        < lax.broadcasted_iota(jnp.int32, (piece, piece), 1)
    ).astype(jnp.bfloat16)
    carry = jnp.zeros((owners, 1), jnp.float32)
    owner_iota = lax.broadcasted_iota(jnp.int32, (owners, piece), 0)
    for p in range(count // piece):
        part = slice(p * piece, (p + 1) * piece)
        mine = owner_iota == owner[:, part]
        hot = mine.astype(jnp.float32)
        ranks = dot(hot.astype(jnp.bfloat16), before, NN) + carry
        carry = carry + jnp.sum(hot, axis=1, keepdims=True)
        rank = jnp.sum(jnp.where(mine, ranks, 0.0), axis=0, keepdims=True).astype(jnp.int32)
        spot[:, part] = jnp.where(member[:, part], owner[:, part] * cap + rank, owners * cap)
    line = lax.broadcasted_iota(jnp.int32, (16, count), 0)
    ids_src[...] = jnp.where(
        line == 0, pos >> 5, jnp.where(line == 1, pos & 31, (line == 2).astype(jnp.int32))
    ).astype(jnp.float32).astype(jnp.bfloat16)

    row_peers = [(dx, dy) for dx in range(xs) for dy in range(2)]
    col_peers = [(dc, dz) for dc in range(CORES) for dz in range(zs)]
    own = len(row_peers) - 1
    row_at = {peer: i - 1 if i else own for i, peer in enumerate(row_peers)}
    col_at = {peer: own + i for i, peer in enumerate(col_peers)}
    lanes = [pl.ds(f * width, width) for f in range(parts_f)]
    half = sub // 2

    def pick_of(k):
        d = lax.rem(lin + k, owners)
        return (
            spot[...] == d * cap + lax.broadcasted_iota(jnp.int32, (cap, count), 0)
        ).astype(jnp.float32).astype(jnp.bfloat16)

    def row_copy(k, f):
        return pltpu.make_async_remote_copy(
            send.at[k, :, lanes[f]], got.at[k, :, lanes[f]], s_send.at[k, f], s_recv.at[k, f],
            device_id=owner_dev(k)[1], device_id_type=MESH)

    def id_copy(k):
        return pltpu.make_async_remote_copy(
            send_ids.at[k], got_ids.at[k], i_send.at[k], i_recv.at[k],
            device_id=owner_dev(k)[1], device_id_type=MESH)

    def start_pair(k, f):
        if f == 0:
            id_copy(k).start()
        row_copy(k, f).start()

    def pack(f):
        def one(k, _):
            pick = pick_of(k)
            send[k, :, lanes[f]] = dot(pick, corpus_ref[0, :, lanes[f]], NN).astype(jnp.bfloat16)
            if f == 0:
                send_ids[k, :, :cap] = dot(ids_src[...], pick, NT).astype(jnp.bfloat16)

            @pl.when(k > 1)
            def _():
                start_pair(k - 1, f)
            return 0

        lax.fori_loop(1, owners, one, 0)
        pick = pick_of(0)
        got[0, :, lanes[f]] = dot(pick, corpus_ref[0, :, lanes[f]], NN).astype(jnp.bfloat16)
        if f == 0:
            got_ids[0, :, :cap] = dot(ids_src[...], pick, NT).astype(jnp.bfloat16)
        start_pair(owners - 1, f)

    def place(f):
        def one(k, first):
            if f == 0:
                line_ids = got_ids[k, :, :cap].astype(jnp.float32)
                where = (line_ids[0:1] * 32.0 + line_ids[1:2]).astype(jnp.int32)
                where = jnp.where(line_ids[2:3] > 0.5, where, sub)
                picks[k] = (
                    where == lax.broadcasted_iota(jnp.int32, (sub, cap), 0)
                ).astype(jnp.float32).astype(jnp.bfloat16)
            term = dot(picks[k], got[k, :, lanes[f]], NN)
            summed[...] = term if first else summed[...] + term

        def arrived(k, _):
            if f == 0:
                id_copy(k).wait_recv()
            row_copy(k, f).wait_recv()
            one(k, False)
            return 0

        one(0, True)
        lax.fori_loop(1, owners, arrived, 0)

    started, waited = [], set()

    def block_copy(source, target, f, h, device):
        area = (pl.ds(h * half, half), lanes[f])
        return pltpu.make_async_remote_copy(
            raw.at[(source,) + area], raw.at[(target,) + area],
            b_send.at[target, f, h], b_recv.at[target, f, h],
            device_id=device, device_id_type=MESH)

    def ship(source, target, f, h, device):
        copy = block_copy(source, target, f, h, device)
        copy.start()
        started.append(copy)

    def need(block, f, h):
        if (block, f, h) not in waited:
            waited.add((block, f, h))
            block_copy(own, block, f, h, row_dev(0, 1)).wait_recv()

    def launch(f):
        for n in range(2):
            for dx, dy in row_peers[1:]:
                if xs == 2 and dx and dy:
                    continue
                ship(own, row_at[(-dx) % xs, (-dy) % 2], f, 1 - n if dy else n, row_dev(dx, dy))
            for dc, dz in col_peers[1:]:
                if zs == 2 and dc and dz:
                    continue
                ship(own, col_at[(-dc) % CORES, (-dz) % zs], f, n, col_dev(dc, dz))

    def relay(f):
        if xs == 2:
            need(row_at[1, 0], f, 0)
            ship(row_at[1, 0], row_at[1, 1], f, 0, row_dev(0, 1))
            need(row_at[0, 1], f, 1)
            ship(row_at[0, 1], row_at[1, 1], f, 1, row_dev(1, 0))
        if zs == 2:
            for h in range(2):
                need(col_at[0, 1], f, h)
                ship(col_at[0, 1], col_at[1, 1], f, h, col_dev(1, 0))

    pl.semaphore_wait(barrier, greeted)
    ahead = 2
    for f in range(min(ahead, parts_f)):
        pack(f)
    for f in range(parts_f):
        place(f)
        raw[own, :, lanes[f]] = summed[...].astype(jnp.bfloat16)
        if f == 0:
            best[...] = jnp.full(best.shape, -2.0, jnp.float32)
        if f:
            relay(f - 1)
        launch(f)
        if f + ahead < parts_f:
            pack(f + ahead)

    def norm(block):
        for f in range(parts_f):
            for h in range(2):
                if block != own:
                    need(block, f, h)

        def one(n, _):
            area = pl.ds(pl.multiple_of(n * 128, 128), 128)
            wide = raw[block, area, :].astype(jnp.float32)
            squares = jnp.sum(wide * wide, axis=1, keepdims=True)
            units[block, area, :] = (wide * lax.rsqrt(squares + EPSILON)).astype(jnp.bfloat16)
            return 0

        lax.fori_loop(0, sub // 128, one, 0)

    def tile(row, i, col, diagonal=False):
        part = pl.ds(pl.multiple_of(i * step, step), step)
        scores = dot(units[own + col], units[row, part, :], NT)
        if diagonal:
            same = (
                lax.broadcasted_iota(jnp.int32, (sub, step), 0)
                == i * step + lax.broadcasted_iota(jnp.int32, (sub, step), 1)
            )
            scores = jnp.where(same, -2.0, scores)
        top = jnp.max(scores.reshape(sub // 8, 8, step), axis=0)
        best[row, i] = jnp.maximum(best[row, i], top)
        return 0

    norm(own)
    lax.fori_loop(0, chunks, lambda i, _: tile(own, i, 0, True), 0)
    relay(parts_f - 1)
    for col in range(1, len(col_peers)):
        norm(own + col)
        lax.fori_loop(0, chunks, lambda i, _, col=col: tile(own, i, col), 0)

    def part_copy(peer):
        return pltpu.make_async_remote_copy(
            best.at[row_at[peer]], parts.at[x * 2 + g],
            p_send.at[row_at[peer]], p_recv.at[x * 2 + g],
            device_id=final_dev(*peer), device_id_type=MESH)

    stays = zh == g

    @pl.when(stays)
    def _():
        parts[x * 2 + g] = best[own]

    @pl.when(jnp.logical_not(stays))
    def _():
        part_copy((0, 0)).start()

    order = [peer for peer in row_peers[1:] if not (peer[0] and peer[1])]
    order += [peer for peer in row_peers[1:] if peer[0] and peer[1]]
    total = chunks * len(col_peers)
    for peer in order:
        row = row_at[peer]
        norm(row)
        lax.fori_loop(
            0, total, lambda n, _, row=row: tile(row, n // len(col_peers), n % len(col_peers)), 0)
        part_copy(peer).start()

    for feeder in range(len(row_peers)):
        arrived = pltpu.make_async_remote_copy(
            best.at[0], parts.at[feeder], p_send.at[0], p_recv.at[feeder],
            device_id=row_dev(0, 1), device_id_type=MESH)
        here = jnp.logical_and(stays, x * 2 + g == feeder)

        @pl.when(jnp.logical_not(here))
        def _(arrived=arrived):
            arrived.wait_recv()
    for i in range(chunks):
        top = jnp.max(parts[:, i], axis=0)
        out_ref[:, i * step : (i + 1) * step] = jnp.max(top, axis=0, keepdims=True)

    @pl.when(jnp.logical_not(stays))
    def _():
        part_copy((0, 0)).wait_send()

    for peer in row_peers[1:]:
        part_copy(peer).wait_send()
    for copy in started:
        copy.wait_send()

    def drain(k, _):
        id_copy(k).wait_send()
        for f in range(parts_f):
            row_copy(k, f).wait_send()
        return 0

    lax.fori_loop(1, owners, drain, 0)


def per_device(corpus, slot_of_row):
    ti_count, tj_count = lax.axis_size("ti"), lax.axis_size("tj")
    _, count, features = corpus.shape
    sub = count // 2
    cap = sub // tj_count
    owners = 2 * tj_count
    chunks, parts_f = 1, 4
    step = sub // chunks
    row_blocks, col_blocks = ti_count // CORES * 2, tj_count // 2 * CORES
    blocks = row_blocks + col_blocks - 1
    wide_cap = -(-cap // 128) * 128
    dma = pltpu.SemaphoreType.DMA
    vmem = pl.BlockSpec(memory_space=pltpu.VMEM)
    return pl.pallas_call(
        functools.partial(kernel, (ti_count, tj_count, count, features, sub, cap, chunks, parts_f)),
        out_shape=jax.ShapeDtypeStruct((1, sub), jnp.float32),
        in_specs=[vmem, vmem],
        out_specs=vmem,
        scratch_shapes=[
            pltpu.VMEM((1, count), jnp.int32),
            pltpu.VMEM((16, count), jnp.bfloat16),
            pltpu.VMEM((owners, cap, features), jnp.bfloat16),
            pltpu.VMEM((owners, 16, wide_cap), jnp.bfloat16),
            pltpu.VMEM((owners, cap, features), jnp.bfloat16),
            pltpu.VMEM((owners, 16, wide_cap), jnp.bfloat16),
            pltpu.VMEM((owners, sub, cap), jnp.bfloat16),
            pltpu.VMEM((sub, features // parts_f), jnp.float32),
            pltpu.VMEM((blocks, sub, features), jnp.bfloat16),
            pltpu.VMEM((blocks, sub, features), jnp.bfloat16),
            pltpu.VMEM((row_blocks, chunks, 8, step), jnp.float32),
            pltpu.VMEM((row_blocks, chunks, 8, step), jnp.float32),
            dma((owners, parts_f)), dma((owners, parts_f)), dma((owners,)), dma((owners,)),
            dma((blocks, parts_f, 2)), dma((blocks, parts_f, 2)),
            dma((row_blocks,)), dma((row_blocks,)),
        ],
        compiler_params=pltpu.CompilerParams(
            collective_id=0, has_side_effects=True, vmem_limit_bytes=60 * 1024 * 1024),
    )(slot_of_row, corpus)


def square_kernel(geo, slots_ref, corpus_ref, out_ref, rows, spot, ids_src, picks, send, send_ids, hop,
                  got, got_ids, wall, raw, acc, xbest, ybest, mine, parts,
                  l_sem, d_send, d_recv, h_send, h_recv, i_send, i_recv, g_send, g_recv, p_send, p_recv):
    ti_count, tj_count, count, features, sub, cap, spans, cuts, phases = geo
    groups = 2 * tj_count
    homes = groups // 2
    blk = sub * tj_count
    cluster = blk * ti_count
    g, ti, tj = lax.axis_index("grp"), lax.axis_index("ti"), lax.axis_index("tj")
    x, core = ti // CORES, lax.rem(ti, CORES)
    zh, zl = tj // 2, lax.rem(tj, 2)
    lin = g * tj_count + tj
    inner = zl != zh
    outer = jnp.logical_not(inner)

    def dev(gg, tt, jj):
        return {"grp": gg, "ti": tt, "tj": jj}

    def home(o):
        half = o // 2
        return lax.rem(o, 2), half * 2 + 1 - half

    def at(dx, dc, dg=0):
        xx = 1 - x if dx else x
        cc = 1 - core if dc else core
        return dev(1 - g if dg else g, xx * CORES + cc, tj)

    pair_dev = dev(g, ti, zh * 2 + 1 - zl)
    core_dev, x_dev, y_dev = at(0, 1), at(1, 0), at(0, 0, 1)

    barrier = pltpu.get_barrier_semaphore()
    devices = 2 * ti_count * tj_count

    piece = 256 if count % 256 == 0 else 128
    pieces = count // piece

    def load(n):
        area = pl.ds(n * piece, piece)
        return pltpu.make_async_copy(corpus_ref.at[0, area, :], rows.at[area, :], l_sem.at[n])

    for n in range(pieces):
        load(n).start()
    for dg in range(2):
        for dt in range(ti_count):
            for dj in range(tj_count):
                if dg or dt or dj:
                    pl.semaphore_signal(
                        barrier, inc=1, device_id_type=MESH,
                        device_id=dev(1 - g if dg else g, lax.rem(ti + dt, ti_count),
                                      lax.rem(tj + dj, tj_count)))

    v = slots_ref[...]
    member = v >= 0
    second = (v >= cluster).astype(jnp.int32)
    inblk = v - second * cluster - ti * blk
    s = jnp.zeros_like(v)
    for k in range(1, tj_count):
        s = s + (inblk >= k * sub).astype(jnp.int32)
    pos = inblk - s * sub
    group = jnp.where(member, second * tj_count + s, groups)
    before = (
        lax.broadcasted_iota(jnp.int32, (piece, piece), 0)
        < lax.broadcasted_iota(jnp.int32, (piece, piece), 1)
    ).astype(jnp.bfloat16)
    carry = jnp.zeros((groups, 1), jnp.float32)
    group_iota = lax.broadcasted_iota(jnp.int32, (groups, piece), 0)
    for n in range(pieces):
        part = slice(n * piece, (n + 1) * piece)
        hits = group_iota == group[:, part]
        hot = hits.astype(jnp.float32)
        ranks = dot(hot.astype(jnp.bfloat16), before, NN) + carry
        carry = carry + jnp.sum(hot, axis=1, keepdims=True)
        rank = jnp.sum(jnp.where(hits, ranks, 0.0), axis=0, keepdims=True).astype(jnp.int32)
        spot[:, part] = jnp.where(member[:, part], group[:, part] * cap + rank, groups * cap)
    line = lax.broadcasted_iota(jnp.int32, (16, count), 0)
    ids_src[...] = jnp.where(
        line == 0, pos >> 5, jnp.where(line == 1, pos & 31, (line == 2).astype(jnp.int32))
    ).astype(jnp.float32).astype(jnp.bfloat16)

    def choose(q, _):
        area = pl.ds(pl.multiple_of(q * cap, cap), cap)
        pick = (
            spot[...] == q * cap + lax.broadcasted_iota(jnp.int32, (cap, count), 0)
        ).astype(jnp.float32).astype(jnp.bfloat16)
        picks[area, :] = pick
        return 0

    lax.fori_loop(0, groups, choose, 0)

    thin = piece // 2
    for n in range(pieces):
        load(n).wait()

        def norm(m, _, n=n):
            area = pl.ds(pl.multiple_of(n * piece + m * thin, thin), thin)
            wide = rows[area, :].astype(jnp.float32)
            squares = jnp.sum(wide * wide, axis=1, keepdims=True)
            rows[area, :] = (wide * lax.rsqrt(squares + EPSILON)).astype(jnp.bfloat16)
            return 0

        lax.fori_loop(0, 2, norm, 0)

    lanes = [pl.ds(a, b - a) for a, b in spans]
    last = len(spans) - 1
    lin_y = (1 - g) * tj_count + tj

    def seat(src):
        return pl.ds(pl.multiple_of(src * cap, cap), cap)

    def row_copy(o, src, f):
        hg, hj = home(o)
        return pltpu.make_async_remote_copy(
            send.at[o, :, :, lanes[f]], got.at[:, seat(src), lanes[f]],
            d_send.at[o, f], d_recv.at[src, f], device_id=dev(hg, ti, hj), device_id_type=MESH)

    def hop_copy(o, half, f):
        return pltpu.make_async_remote_copy(
            send.at[o, :, :, lanes[f]], hop.at[half, :, :, lanes[f]],
            d_send.at[o, f], h_recv.at[half, f], device_id=y_dev, device_id_type=MESH)

    def relay_copy(half, f):
        hg, hj = home(half * 2 + g)
        return pltpu.make_async_remote_copy(
            hop.at[half, :, :, lanes[f]], got.at[:, seat(lin_y), lanes[f]],
            h_send.at[half, f], d_recv.at[lin_y, f], device_id=dev(hg, ti, hj), device_id_type=MESH)

    def id_copy(o, src):
        hg, hj = home(o)
        return pltpu.make_async_remote_copy(
            send_ids.at[pl.ds(o * 2, 2)], got_ids.at[src],
            i_send.at[o], i_recv.at[src], device_id=dev(hg, ti, hj), device_id_type=MESH)

    def is_me(o):
        hg, hj = home(o)
        return jnp.logical_and(hg == g, hj == tj)

    def level(half):
        return home(half * 2)[1] == tj

    halves = (1 - zh, zh)

    def send_ids_out():
        def one(o, _):
            for q in (o * 2, o * 2 + 1):
                pick = picks[pl.ds(pl.multiple_of(q * cap, cap), cap), :]
                send_ids[q, :, :cap] = dot(ids_src[...], pick, NT).astype(jnp.bfloat16)

            @pl.when(is_me(o))
            def _():
                pltpu.make_async_copy(
                    send_ids.at[pl.ds(o * 2, 2)], got_ids.at[lin], i_recv.at[lin]).start()

            @pl.when(jnp.logical_not(is_me(o)))
            def _():
                id_copy(o, lin).start()
            return 0

        lax.fori_loop(0, homes, one, 0)

    def send_y(f, only=halves):
        for half in only:
            o = half * 2 + 1 - g

            @pl.when(level(half))
            def _(o=o):
                row_copy(o, lin, f).start()

            @pl.when(jnp.logical_not(level(half)))
            def _(o=o, half=half):
                hop_copy(o, half, f).start()

    def send_z(f, only=halves):
        for half in only:
            o = half * 2 + g

            @pl.when(level(half))
            def _(o=o):
                pltpu.make_async_copy(
                    send.at[o, :, :, lanes[f]], got.at[:, seat(lin), lanes[f]], d_recv.at[lin, f]).start()

            @pl.when(jnp.logical_not(level(half)))
            def _(o=o):
                row_copy(o, lin, f).start()

    def relay(f):
        for half in halves:
            @pl.when(jnp.logical_not(level(half)))
            def _(half=half):
                hop_copy(half * 2, half, f).wait_recv()
                relay_copy(half, f).start()

    def pack(fs, first=0, stop=2):
        low, high = spans[fs[0]][0], spans[fs[-1]][1]

        def one(j, _):
            half = lax.rem(1 - zh + j, 2)
            area = pl.ds(pl.multiple_of(half * sub, sub), sub)
            chosen = dot(picks[area, :], rows[:, low:high], NN).astype(jnp.bfloat16)
            send[pl.ds(half * 2, 2), :, :, low:high] = chosen.reshape(2, 2, cap, high - low)
            return 0

        lax.fori_loop(first, stop, one, 0)

    pack([0, 1], 0, 1)
    pl.semaphore_wait(barrier, devices - 1)
    send_y(0, halves[:1])
    send_z(0, halves[:1])
    send_ids_out()
    pack([0, 1], 1, 2)
    send_y(0, halves[1:])
    send_z(0, halves[1:])
    send_y(1)
    pack([2])
    relay(0)
    send_z(1)
    send_y(2)
    pack([3])
    relay(1)
    send_z(2)
    pack([4, 5])

    xbest[...] = jnp.full(xbest.shape, -2.0, jnp.float32)
    ybest[...] = jnp.full(ybest.shape, -2.0, jnp.float32)

    def read_ids():
        for src in range(groups):
            id_copy(0, src).wait_recv()
            for r in range(2):
                wall[r, :, src * cap : (src + 1) * cap] = got_ids[src, r, :, :cap].astype(jnp.float32)
        for r in range(2):
            where = (wall[r, 0:1] * 32.0 + wall[r, 1:2]).astype(jnp.int32)
            where = jnp.where(wall[r, 2:3] > 0.5, where, sub)

            def one(n, _, r=r, where=where):
                area = pl.ds(pl.multiple_of(r * sub + n * 128, 128), 128)
                picks[area, :] = (
                    where == n * 128 + lax.broadcasted_iota(jnp.int32, (128, count), 0)
                ).astype(jnp.float32).astype(jnp.bfloat16)
                return 0

            lax.fori_loop(0, sub // 128, one, 0)

    own, own_c, near_x, near_x_c, near_y, near_y_c, deep, deep_c, skew = range(9)
    left, right = core == 0, core == 1

    def block_copy(source, target, c, device):
        f, start, size = cuts[c]
        area = pl.ds(start, size)
        return pltpu.make_async_remote_copy(
            raw.at[source, area, lanes[f]], raw.at[target, area, lanes[f]],
            g_send.at[target, c], g_recv.at[target, c], device_id=device, device_id_type=MESH)

    def of(f):
        return [c for c, cut in enumerate(cuts) if cut[0] == f]

    def arrive(target, f):
        for c in of(f):
            block_copy(own, target, c, core_dev).wait_recv()

    def place(r, target, c):
        f, start, size = cuts[c]
        chosen = picks[r * sub + start : r * sub + start + size, :]
        raw[target, start : start + size, lanes[f]] = dot(
            chosen, got[r, :, lanes[f]], NN).astype(jnp.bfloat16)

    def share(c):
        block_copy(own, near_y, c, y_dev).start()
        block_copy(own, near_x, c, x_dev).start()

    def supply_inner(f):
        @pl.when(inner)
        def _():
            if f == 0:
                read_ids()

            def arrived(src, _):
                row_copy(0, src, f).wait_recv()
                return 0

            lax.fori_loop(0, groups, arrived, 0)
            for c in of(f):
                place(1, deep, c)
                place(0, own, c)
                block_copy(deep, own, c, pair_dev).start()
                share(c)
            for c in of(f):
                block_copy(deep, deep_c, c, core_dev).start()
                block_copy(own, own_c, c, core_dev).start()

    def supply_outer(f):
        @pl.when(outer)
        def _():
            for c in of(f):
                block_copy(own, own, c, core_dev).wait_recv()
                share(c)
                block_copy(own, own_c, c, core_dev).start()

    def supply(f):
        supply_inner(f)
        supply_outer(f)

    def forward(f):
        for c in of(f):
            block_copy(own, near_y, c, core_dev).wait_recv()

            @pl.when(jnp.logical_and(inner, right))
            def _(c=c):
                block_copy(near_y, skew, c, x_dev).start()

            if f == last:
                lower(c)
            block_copy(near_y, near_y_c, c, core_dev).start()
            block_copy(own, near_x, c, core_dev).wait_recv()
            block_copy(near_x, near_x_c, c, core_dev).start()

    def lower(*fs):
        @pl.when(jnp.logical_and(inner, left))
        def _():
            for c in fs:
                block_copy(near_y, deep, c, pair_dev).start()

    def collect_near(f):
        arrive(own_c, f)

        @pl.when(inner)
        def _():
            arrive(deep_c, f)

    def collect_rest(f):
        arrive(near_x_c, f)
        arrive(near_y_c, f)

        @pl.when(jnp.logical_and(outer, left))
        def _():
            arrive(deep, f)

    inner_jobs = [(own, own_c), (own, deep), (own, deep_c), (own, near_x), (near_x, deep), (near_x, deep_c),
                  (own, near_y), (near_y, deep), (near_y, deep_c), (near_x, near_y)]
    outer_jobs = [(own, own_c), (own, near_x), (own, near_y), (near_x, near_y), (deep, near_x), (deep, near_x_c)]
    inner_early, outer_early = 3, 1

    def shift(a, b):
        if (a, b) == (own, near_x) or (a, b) == (near_x, near_y):
            return x
        return g if (a, b) == (own, near_y) else 0

    def table(jobs, j):
        a, b = 0, 0
        for n, (p, q) in enumerate(jobs):
            a = a + jnp.where(j == n, p, 0)
            b = b + jnp.where(j == n, q + shift(p, q), 0)
        return a, b

    def tile(a, b, slot, phase, diagonal=False):
        low, high = phases[phase] if slot is not None else (0, features)
        scores = dot(raw[a, :, low:high], raw[b, :, low:high], NT)
        if phase and slot is not None:
            scores = scores + acc[slot]
        if phase < len(phases) - 1:
            acc[slot] = scores
            return
        if diagonal:
            same = (
                lax.broadcasted_iota(jnp.int32, (sub, sub), 0)
                == lax.broadcasted_iota(jnp.int32, (sub, sub), 1)
            )
            scores = jnp.where(same, -2.0, scores)
        xbest[b] = jnp.maximum(xbest[b], jnp.max(scores.reshape(sub // 8, 8, sub), axis=0))
        if diagonal:
            return
        side = scores[:, :128]
        for k in range(1, sub // 128):
            side = jnp.maximum(side, scores[:, k * 128 : (k + 1) * 128])
        y = 3 if slot is None else jnp.minimum(a // 2, 2)
        ybest[y] = jnp.maximum(ybest[y], side)

    def diagonal(phase):
        tile(own, own, 0, phase, True)

    def others(phase, start, stop):
        def one(j, _):
            ia, ib = table(inner_jobs, j)
            oa, ob = table(outer_jobs, j)
            tile(jnp.where(inner, ia, oa), jnp.where(inner, ib, ob), j + 1, phase)
            return 0

        lax.fori_loop(start, stop, one, 0)

    skip = jnp.where(inner, core, 1 - core)
    early = jnp.where(inner, inner_early, outer_early)
    total = jnp.where(inner, len(inner_jobs), jnp.where(left, len(outer_jobs), len(outer_jobs) - 2))

    def score_early(phase, *fs):
        for f in fs:
            collect_near(f)
        diagonal(phase)
        others(phase, skip, early)

    def score_late(phase, *fs):
        for f in fs:
            collect_rest(f)
        others(phase, early, total)

    final = len(phases) - 1
    supply(0)
    send_y(3)
    relay(2)
    send_z(3)
    supply(1)
    forward(0)
    lower(0)
    send_y(4)
    relay(3)
    send_z(4)

    @pl.when(outer)
    def _():
        send_y(5)

    forward(1)
    supply(2)

    @pl.when(inner)
    def _():
        send_y(5)

    lower(1)
    score_early(0, 0, 1, 2)
    relay(4)
    send_z(5)

    @pl.when(outer)
    def _():
        relay(5)

    forward(2)
    lower(2)

    @pl.when(inner)
    def _():
        relay(5)

    supply(3)
    supply_outer(4)
    score_late(0, 0, 1, 2)
    supply_inner(4)
    score_early(1, 3)
    supply_outer(5)
    forward(3)
    lower(3)
    score_late(1, 3)
    supply_inner(5)
    forward(4)
    lower(4)
    score_early(2, 4, 5)
    forward(5)
    score_late(2, 4, 5)

    def score_skew():
        @pl.when(jnp.logical_and(inner, right))
        def _():
            for f in range(last + 1):
                arrive(skew, f)

            def one(n, _):
                tile(skew, deep + n, None, final)
                return 0

            lax.fori_loop(0, 2, one, 0)

    score_skew()
    tops = []
    for n in range(4):
        with_side = jnp.transpose(ybest[n])
        tops.append(jnp.max(with_side.reshape(16, 8, sub), axis=0))
    y_of = {own: 0, near_x: 1, skew: 3}
    for b in range(9):
        top = tops[3] if b == skew else xbest[b]
        if b in y_of and b != skew:
            top = jnp.maximum(top, tops[y_of[b]])
        if b == near_y:
            top = jnp.maximum(top, jnp.where(inner, tops[2], -2.0))
        if b == deep:
            top = jnp.maximum(top, jnp.where(inner, -2.0, tops[2]))
        mine[b] = jnp.max(top, axis=0, keepdims=True)

    role = outer.astype(jnp.int32)

    def final_dev(b):
        dx, dc, dg = b in (near_x, near_x_c, skew), b in (own_c, near_x_c, near_y_c, deep_c), b in (near_y, near_y_c, skew)
        gg = 1 - g if dg else g
        rr = role
        if b == deep:
            gg = jnp.where(inner, g, 1 - g)
        if b in (deep, deep_c):
            rr = 1 - role
        xx = 1 - x if dx else x
        cc = 1 - core if dc else core
        return zh, xx * CORES + cc, gg * 2 + rr

    def part_copy(b):
        gg, tt, jj = final_dev(b)
        return pltpu.make_async_remote_copy(
            mine.at[b], parts.at[deep if b == skew else b], p_send.at[b],
            p_recv.at[deep if b == skew else b],
            device_id=dev(gg, tt, jj), device_id_type=MESH)

    def stays(b):
        gg, tt, jj = final_dev(b)
        return jnp.logical_and(gg == g, jnp.logical_and(tt == ti, jj == tj))

    def holds(b):
        if b == deep_c:
            return inner
        if b == deep:
            return jnp.logical_or(inner, left)
        return jnp.logical_and(inner, right) if b == skew else True

    for b in range(9):
        @pl.when(jnp.logical_and(holds(b), stays(b)))
        def _(b=b):
            parts[deep if b == skew else b] = mine[b]

        @pl.when(jnp.logical_and(holds(b), jnp.logical_not(stays(b))))
        def _(b=b):
            part_copy(b).start()

    half, rr = tj // 2, lax.rem(tj, 2)

    @pl.when(rr == 0)
    def _():
        parts[deep_c] = jnp.full((1, sub), -2.0, jnp.float32)

    def giver(b):
        dx, dc, dg = b in (near_x, near_x_c), b in (own_c, near_x_c, near_y_c, deep_c), b in (near_y, near_y_c)
        gg = 1 - half if dg else half
        plane = rr
        xx = 1 - x if dx else x
        if b == deep:
            gg = jnp.where(rr == 0, 1 - half, half)
            xx = jnp.where(jnp.logical_and(rr == 0, right), 1 - x, x)
            plane = jnp.where(jnp.logical_and(rr == 0, left), 1, 0)
        if b == deep_c:
            plane = 1 - rr
        cc = 1 - core if dc else core
        zz = jnp.where(plane == 0, 1 - g, g)
        return gg, xx * CORES + cc, g * 2 + zz

    for b in range(8):
        gg, tt, jj = giver(b)
        here = jnp.logical_and(gg == g, jnp.logical_and(tt == ti, jj == tj))
        comes = jnp.logical_not(here)
        if b == deep_c:
            comes = jnp.logical_and(comes, rr == 1)

        @pl.when(comes)
        def _(b=b):
            part_copy(b).wait_recv()

    out_ref[...] = jnp.max(parts[...], axis=0)

    for b in range(9):
        @pl.when(jnp.logical_and(holds(b), jnp.logical_not(stays(b))))
        def _(b=b):
            part_copy(b).wait_send()

    def drain(o, _):
        @pl.when(jnp.logical_not(is_me(o)))
        def _():
            id_copy(o, lin).wait_send()
            for f in range(last + 1):
                row_copy(o, lin, f).wait_send()
        return 0

    lax.fori_loop(0, homes, drain, 0)
    for half in halves:
        @pl.when(jnp.logical_not(level(half)))
        def _(half=half):
            for f in range(last + 1):
                relay_copy(half, f).wait_send()
    for c in range(len(cuts)):
        for target in (near_y, near_x, own_c, near_y_c, near_x_c):
            block_copy(own, target, c, core_dev).wait_send()

        @pl.when(inner)
        def _(c=c):
            for target in (own, deep_c):
                block_copy(own, target, c, core_dev).wait_send()

        @pl.when(jnp.logical_and(inner, left))
        def _(c=c):
            block_copy(own, deep, c, core_dev).wait_send()

        @pl.when(jnp.logical_and(inner, right))
        def _(c=c):
            block_copy(own, skew, c, core_dev).wait_send()


def square(corpus, slot_of_row):
    ti_count, tj_count = lax.axis_size("ti"), lax.axis_size("tj")
    _, count, features = corpus.shape
    sub = count // 2
    cap = sub // tj_count
    groups, homes = 2 * tj_count, tj_count
    unit = features // 8
    edges = (0, 1, 2, 4, 6, 7, 8)
    spans = [(a * unit, b * unit) for a, b in zip(edges, edges[1:])]
    phases = [(0, 4 * unit), (4 * unit, 6 * unit), (6 * unit, features)]
    n = len(spans)
    cuts = [(f, 0, sub) for f in range(n - 1)] + [(n - 1, 0, sub // 2), (n - 1, sub // 2, sub // 2)]
    wide_cap = -(-cap // 128) * 128
    jobs = 11
    piece = 256 if count % 256 == 0 else 128
    dma = pltpu.SemaphoreType.DMA
    vmem = pl.BlockSpec(memory_space=pltpu.VMEM)
    bf16, f32 = jnp.bfloat16, jnp.float32
    return pl.pallas_call(
        functools.partial(
            square_kernel, (ti_count, tj_count, count, features, sub, cap, spans, cuts, phases)),
        out_shape=jax.ShapeDtypeStruct((1, sub), f32),
        in_specs=[vmem, pl.BlockSpec(memory_space=pl.ANY)],
        out_specs=vmem,
        scratch_shapes=[
            pltpu.VMEM((count, features), bf16),
            pltpu.VMEM((1, count), jnp.int32),
            pltpu.VMEM((16, count), bf16),
            pltpu.VMEM((count, count), bf16),
            pltpu.VMEM((homes, 2, cap, features), bf16),
            pltpu.VMEM((groups, 16, wide_cap), bf16),
            pltpu.VMEM((2, 2, cap, features), bf16),
            pltpu.VMEM((2, groups * cap, features), bf16),
            pltpu.VMEM((groups, 2, 16, wide_cap), bf16),
            pltpu.VMEM((2, 16, count), f32),
            pltpu.VMEM((9, sub, features), bf16),
            pltpu.VMEM((jobs, sub, sub), f32),
            pltpu.VMEM((8, 8, sub), f32),
            pltpu.VMEM((4, sub, 128), f32),
            pltpu.VMEM((9, 1, sub), f32),
            pltpu.VMEM((8, 1, sub), f32),
            dma((count // piece,)),
            dma((homes, n)), dma((groups, n)), dma((2, n)), dma((2, n)), dma((homes,)), dma((groups,)),
            dma((9, len(cuts))), dma((9, len(cuts))), dma((9,)), dma((8,)),
        ],
        compiler_params=pltpu.CompilerParams(
            collective_id=1, has_side_effects=True, vmem_limit_bytes=63 * 1024 * 1024),
    )(slot_of_row, corpus)


def solution(mesh):
    in_specs = (P("grp", ("ti", "tj"), None), P("grp", ("ti", "tj")))
    out_specs = P("grp", ("ti", "tj"))
    is_square = mesh.shape["ti"] == 2 * CORES and mesh.shape["tj"] == 4
    return jax.shard_map(
        square if is_square else per_device, mesh=mesh, in_specs=in_specs, out_specs=out_specs, check_vma=False
    )
```

```python
import functools

import jax
import jax.numpy as jnp
from jax import lax
from jax.experimental import pallas as pl
from jax.experimental.pallas import tpu as pltpu
from jax.sharding import PartitionSpec as P

MESH = pl.DeviceIdType.MESH
NT = (((1,), (1,)), ((), ()))
NN = (((1,), (0,)), ((), ()))
CORES = 2
EPSILON = 1e-06


def dot(a, b, dims):
    return lax.dot_general(a, b, dims, preferred_element_type=jnp.float32)


def kernel(geo, slots_ref, corpus_ref, out_ref, spot, ids_src, send, send_ids, got, got_ids,
           picks, summed, raw, units, best, parts, s_send, s_recv, i_send, i_recv,
           b_send, b_recv, p_send, p_recv):
    ti_count, tj_count, count, features, sub, cap, chunks, parts_f = geo
    width = features // parts_f
    owners = 2 * tj_count
    xs = ti_count // CORES
    zs = tj_count // 2
    blk = sub * tj_count
    cluster = blk * ti_count
    step = sub // chunks
    g, ti, tj = lax.axis_index("grp"), lax.axis_index("ti"), lax.axis_index("tj")
    x, core = ti // CORES, ti % CORES
    zh, zl = tj // zs, tj % zs
    lin = g * tj_count + tj

    def dev(gg, tt, jj):
        return {"grp": gg, "ti": tt, "tj": jj}

    def owner_dev(k):
        d = lax.rem(lin + k, owners)
        return d, dev(d // tj_count, ti, lax.rem(d, tj_count))

    def row_dev(dx, dy):
        return dev(lax.rem(g + dy, 2), lax.rem(x + dx, xs) * CORES + core, tj)

    def col_dev(dc, dz):
        return dev(g, x * CORES + lax.rem(core + dc, CORES), zh * zs + lax.rem(zl + dz, zs))

    def final_dev(dx, dy):
        return dev(zh, lax.rem(x + dx, xs) * CORES + core, lax.rem(g + dy, 2) * zs + zl)

    def feeder_dev(dx, dy):
        return dev(dy, lax.rem(x + dx, xs) * CORES + core, g * zs + zl)

    barrier = pltpu.get_barrier_semaphore()
    greeted = 0
    targets = [owner_dev(k)[1] for k in range(1, owners)]
    targets += [row_dev(dx, dy) for dx in range(1, xs) for dy in range(2)]
    targets += [col_dev(dc, dz) for dc in range(1, CORES) for dz in range(zs)]
    targets += [final_dev(dx, dy) for dx in range(1, xs) for dy in range(2)]
    targets += [feeder_dev(dx, dy) for dx in range(1, xs) for dy in range(2)]
    for target in targets:
        pl.semaphore_signal(barrier, inc=1, device_id=target, device_id_type=MESH)
        greeted += 1

    v = slots_ref[...]
    member = v >= 0
    second = (v >= cluster).astype(jnp.int32)
    inblk = v - second * cluster - ti * blk
    s = jnp.zeros_like(v)
    for k in range(1, tj_count):
        s = s + (inblk >= k * sub).astype(jnp.int32)
    pos = inblk - s * sub
    s_hi = (s >= zs).astype(jnp.int32)
    owner = s_hi * tj_count + second * zs + s - s_hi * zs
    owner = jnp.where(member, owner, owners)
    piece = 256 if count % 256 == 0 else 128
    before = (
        lax.broadcasted_iota(jnp.int32, (piece, piece), 0)
        < lax.broadcasted_iota(jnp.int32, (piece, piece), 1)
    ).astype(jnp.bfloat16)
    carry = jnp.zeros((owners, 1), jnp.float32)
    owner_iota = lax.broadcasted_iota(jnp.int32, (owners, piece), 0)
    for p in range(count // piece):
        part = slice(p * piece, (p + 1) * piece)
        mine = owner_iota == owner[:, part]
        hot = mine.astype(jnp.float32)
        ranks = dot(hot.astype(jnp.bfloat16), before, NN) + carry
        carry = carry + jnp.sum(hot, axis=1, keepdims=True)
        rank = jnp.sum(jnp.where(mine, ranks, 0.0), axis=0, keepdims=True).astype(jnp.int32)
        spot[:, part] = jnp.where(member[:, part], owner[:, part] * cap + rank, owners * cap)
    line = lax.broadcasted_iota(jnp.int32, (16, count), 0)
    ids_src[...] = jnp.where(
        line == 0, pos >> 5, jnp.where(line == 1, pos & 31, (line == 2).astype(jnp.int32))
    ).astype(jnp.float32).astype(jnp.bfloat16)

    row_peers = [(dx, dy) for dx in range(xs) for dy in range(2)]
    col_peers = [(dc, dz) for dc in range(CORES) for dz in range(zs)]
    own = len(row_peers) - 1
    row_at = {peer: i - 1 if i else own for i, peer in enumerate(row_peers)}
    col_at = {peer: own + i for i, peer in enumerate(col_peers)}
    lanes = [pl.ds(f * width, width) for f in range(parts_f)]
    half = sub // 2

    def pick_of(k):
        d = lax.rem(lin + k, owners)
        return (
            spot[...] == d * cap + lax.broadcasted_iota(jnp.int32, (cap, count), 0)
        ).astype(jnp.float32).astype(jnp.bfloat16)

    def row_copy(k, f):
        return pltpu.make_async_remote_copy(
            send.at[k, :, lanes[f]], got.at[k, :, lanes[f]], s_send.at[k, f], s_recv.at[k, f],
            device_id=owner_dev(k)[1], device_id_type=MESH)

    def id_copy(k):
        return pltpu.make_async_remote_copy(
            send_ids.at[k], got_ids.at[k], i_send.at[k], i_recv.at[k],
            device_id=owner_dev(k)[1], device_id_type=MESH)

    def start_pair(k, f):
        if f == 0:
            id_copy(k).start()
        row_copy(k, f).start()

    def pack(f):
        def one(k, _):
            pick = pick_of(k)
            send[k, :, lanes[f]] = dot(pick, corpus_ref[0, :, lanes[f]], NN).astype(jnp.bfloat16)
            if f == 0:
                send_ids[k, :, :cap] = dot(ids_src[...], pick, NT).astype(jnp.bfloat16)

            @pl.when(k > 1)
            def _():
                start_pair(k - 1, f)
            return 0

        lax.fori_loop(1, owners, one, 0)
        pick = pick_of(0)
        got[0, :, lanes[f]] = dot(pick, corpus_ref[0, :, lanes[f]], NN).astype(jnp.bfloat16)
        if f == 0:
            got_ids[0, :, :cap] = dot(ids_src[...], pick, NT).astype(jnp.bfloat16)
        start_pair(owners - 1, f)

    def place(f):
        def one(k, first):
            if f == 0:
                line_ids = got_ids[k, :, :cap].astype(jnp.float32)
                where = (line_ids[0:1] * 32.0 + line_ids[1:2]).astype(jnp.int32)
                where = jnp.where(line_ids[2:3] > 0.5, where, sub)
                picks[k] = (
                    where == lax.broadcasted_iota(jnp.int32, (sub, cap), 0)
                ).astype(jnp.float32).astype(jnp.bfloat16)
            term = dot(picks[k], got[k, :, lanes[f]], NN)
            summed[...] = term if first else summed[...] + term

        def arrived(k, _):
            if f == 0:
                id_copy(k).wait_recv()
            row_copy(k, f).wait_recv()
            one(k, False)
            return 0

        one(0, True)
        lax.fori_loop(1, owners, arrived, 0)

    started, waited = [], set()

    def block_copy(source, target, f, h, device):
        area = (pl.ds(h * half, half), lanes[f])
        return pltpu.make_async_remote_copy(
            raw.at[(source,) + area], raw.at[(target,) + area],
            b_send.at[target, f, h], b_recv.at[target, f, h],
            device_id=device, device_id_type=MESH)

    def ship(source, target, f, h, device):
        copy = block_copy(source, target, f, h, device)
        copy.start()
        started.append(copy)

    def need(block, f, h):
        if (block, f, h) not in waited:
            waited.add((block, f, h))
            block_copy(own, block, f, h, row_dev(0, 1)).wait_recv()

    def launch(f):
        for n in range(2):
            for dx, dy in row_peers[1:]:
                if xs == 2 and dx and dy:
                    continue
                ship(own, row_at[(-dx) % xs, (-dy) % 2], f, 1 - n if dy else n, row_dev(dx, dy))
            for dc, dz in col_peers[1:]:
                if zs == 2 and dc and dz:
                    continue
                ship(own, col_at[(-dc) % CORES, (-dz) % zs], f, n, col_dev(dc, dz))

    def relay(f):
        if xs == 2:
            need(row_at[1, 0], f, 0)
            ship(row_at[1, 0], row_at[1, 1], f, 0, row_dev(0, 1))
            need(row_at[0, 1], f, 1)
            ship(row_at[0, 1], row_at[1, 1], f, 1, row_dev(1, 0))
        if zs == 2:
            for h in range(2):
                need(col_at[0, 1], f, h)
                ship(col_at[0, 1], col_at[1, 1], f, h, col_dev(1, 0))

    pl.semaphore_wait(barrier, greeted)
    ahead = 2
    for f in range(min(ahead, parts_f)):
        pack(f)
    for f in range(parts_f):
        place(f)
        raw[own, :, lanes[f]] = summed[...].astype(jnp.bfloat16)
        if f == 0:
            best[...] = jnp.full(best.shape, -2.0, jnp.float32)
        if f:
            relay(f - 1)
        launch(f)
        if f + ahead < parts_f:
            pack(f + ahead)

    def norm(block):
        for f in range(parts_f):
            for h in range(2):
                if block != own:
                    need(block, f, h)

        def one(n, _):
            area = pl.ds(pl.multiple_of(n * 128, 128), 128)
            wide = raw[block, area, :].astype(jnp.float32)
            squares = jnp.sum(wide * wide, axis=1, keepdims=True)
            units[block, area, :] = (wide * lax.rsqrt(squares + EPSILON)).astype(jnp.bfloat16)
            return 0

        lax.fori_loop(0, sub // 128, one, 0)

    def tile(row, i, col, diagonal=False):
        part = pl.ds(pl.multiple_of(i * step, step), step)
        scores = dot(units[own + col], units[row, part, :], NT)
        if diagonal:
            same = (
                lax.broadcasted_iota(jnp.int32, (sub, step), 0)
                == i * step + lax.broadcasted_iota(jnp.int32, (sub, step), 1)
            )
            scores = jnp.where(same, -2.0, scores)
        top = jnp.max(scores.reshape(sub // 8, 8, step), axis=0)
        best[row, i] = jnp.maximum(best[row, i], top)
        return 0

    norm(own)
    lax.fori_loop(0, chunks, lambda i, _: tile(own, i, 0, True), 0)
    relay(parts_f - 1)
    for col in range(1, len(col_peers)):
        norm(own + col)
        lax.fori_loop(0, chunks, lambda i, _, col=col: tile(own, i, col), 0)

    def part_copy(peer):
        return pltpu.make_async_remote_copy(
            best.at[row_at[peer]], parts.at[x * 2 + g],
            p_send.at[row_at[peer]], p_recv.at[x * 2 + g],
            device_id=final_dev(*peer), device_id_type=MESH)

    stays = zh == g

    @pl.when(stays)
    def _():
        parts[x * 2 + g] = best[own]

    @pl.when(jnp.logical_not(stays))
    def _():
        part_copy((0, 0)).start()

    order = [peer for peer in row_peers[1:] if not (peer[0] and peer[1])]
    order += [peer for peer in row_peers[1:] if peer[0] and peer[1]]
    total = chunks * len(col_peers)
    for peer in order:
        row = row_at[peer]
        norm(row)
        lax.fori_loop(
            0, total, lambda n, _, row=row: tile(row, n // len(col_peers), n % len(col_peers)), 0)
        part_copy(peer).start()

    for feeder in range(len(row_peers)):
        arrived = pltpu.make_async_remote_copy(
            best.at[0], parts.at[feeder], p_send.at[0], p_recv.at[feeder],
            device_id=row_dev(0, 1), device_id_type=MESH)
        here = jnp.logical_and(stays, x * 2 + g == feeder)

        @pl.when(jnp.logical_not(here))
        def _(arrived=arrived):
            arrived.wait_recv()
    for i in range(chunks):
        top = jnp.max(parts[:, i], axis=0)
        out_ref[:, i * step : (i + 1) * step] = jnp.max(top, axis=0, keepdims=True)

    @pl.when(jnp.logical_not(stays))
    def _():
        part_copy((0, 0)).wait_send()

    for peer in row_peers[1:]:
        part_copy(peer).wait_send()
    for copy in started:
        copy.wait_send()

    def drain(k, _):
        id_copy(k).wait_send()
        for f in range(parts_f):
            row_copy(k, f).wait_send()
        return 0

    lax.fori_loop(1, owners, drain, 0)


def per_device(corpus, slot_of_row):
    ti_count, tj_count = lax.axis_size("ti"), lax.axis_size("tj")
    _, count, features = corpus.shape
    sub = count // 2
    cap = sub // tj_count
    owners = 2 * tj_count
    chunks, parts_f = 1, 4
    step = sub // chunks
    row_blocks, col_blocks = ti_count // CORES * 2, tj_count // 2 * CORES
    blocks = row_blocks + col_blocks - 1
    wide_cap = -(-cap // 128) * 128
    dma = pltpu.SemaphoreType.DMA
    vmem = pl.BlockSpec(memory_space=pltpu.VMEM)
    return pl.pallas_call(
        functools.partial(kernel, (ti_count, tj_count, count, features, sub, cap, chunks, parts_f)),
        out_shape=jax.ShapeDtypeStruct((1, sub), jnp.float32),
        in_specs=[vmem, vmem],
        out_specs=vmem,
        scratch_shapes=[
            pltpu.VMEM((1, count), jnp.int32),
            pltpu.VMEM((16, count), jnp.bfloat16),
            pltpu.VMEM((owners, cap, features), jnp.bfloat16),
            pltpu.VMEM((owners, 16, wide_cap), jnp.bfloat16),
            pltpu.VMEM((owners, cap, features), jnp.bfloat16),
            pltpu.VMEM((owners, 16, wide_cap), jnp.bfloat16),
            pltpu.VMEM((owners, sub, cap), jnp.bfloat16),
            pltpu.VMEM((sub, features // parts_f), jnp.float32),
            pltpu.VMEM((blocks, sub, features), jnp.bfloat16),
            pltpu.VMEM((blocks, sub, features), jnp.bfloat16),
            pltpu.VMEM((row_blocks, chunks, 8, step), jnp.float32),
            pltpu.VMEM((row_blocks, chunks, 8, step), jnp.float32),
            dma((owners, parts_f)), dma((owners, parts_f)), dma((owners,)), dma((owners,)),
            dma((blocks, parts_f, 2)), dma((blocks, parts_f, 2)),
            dma((row_blocks,)), dma((row_blocks,)),
        ],
        compiler_params=pltpu.CompilerParams(
            collective_id=0, has_side_effects=True, vmem_limit_bytes=60 * 1024 * 1024),
    )(slot_of_row, corpus)


def square_kernel(geo, slots_ref, corpus_ref, out_ref, rows, spot, ids_src, picks, send, send_ids, hop,
                  got, got_ids, wall, raw, acc, xbest, ybest, mine, parts,
                  l_sem, d_send, d_recv, h_send, h_recv, i_send, i_recv, g_send, g_recv, f_recv,
                  p_send, p_recv):
    ti_count, tj_count, count, features, sub, cap, spans, units, cuts, phases = geo
    groups = 2 * tj_count
    homes = groups // 2
    blk = sub * tj_count
    cluster = blk * ti_count
    g, ti, tj = lax.axis_index("grp"), lax.axis_index("ti"), lax.axis_index("tj")
    x, core = ti // CORES, lax.rem(ti, CORES)
    zh, zl = tj // 2, lax.rem(tj, 2)
    lin = g * tj_count + tj
    inner = zl != zh
    outer = jnp.logical_not(inner)

    def dev(gg, tt, jj):
        return {"grp": gg, "ti": tt, "tj": jj}

    def home(o):
        half = o // 2
        return lax.rem(o, 2), half * 2 + 1 - half

    def at(dx, dc, dg=0):
        xx = 1 - x if dx else x
        cc = 1 - core if dc else core
        return dev(1 - g if dg else g, xx * CORES + cc, tj)

    pair_dev = dev(g, ti, zh * 2 + 1 - zl)
    core_dev, x_dev, y_dev = at(0, 1), at(1, 0), at(0, 0, 1)

    barrier = pltpu.get_barrier_semaphore()
    devices = 2 * ti_count * tj_count

    piece = 256 if count % 256 == 0 else 128
    pieces = count // piece

    load = pltpu.make_async_copy(corpus_ref.at[0], rows, l_sem.at[0])
    load.start()
    for dg in range(2):
        for dt in range(ti_count):
            for dj in range(tj_count):
                if dg or dt or dj:
                    pl.semaphore_signal(
                        barrier, inc=1, device_id_type=MESH,
                        device_id=dev(1 - g if dg else g, lax.rem(ti + dt, ti_count),
                                      lax.rem(tj + dj, tj_count)))

    v = slots_ref[...]
    member = v >= 0
    second = (v >= cluster).astype(jnp.int32)
    inblk = v - second * cluster - ti * blk
    s = jnp.zeros_like(v)
    for k in range(1, tj_count):
        s = s + (inblk >= k * sub).astype(jnp.int32)
    pos = inblk - s * sub
    group = jnp.where(member, second * tj_count + s, groups)
    before = (
        lax.broadcasted_iota(jnp.int32, (piece, piece), 0)
        < lax.broadcasted_iota(jnp.int32, (piece, piece), 1)
    ).astype(jnp.bfloat16)
    carry = jnp.zeros((groups, 1), jnp.float32)
    group_iota = lax.broadcasted_iota(jnp.int32, (groups, piece), 0)
    for n in range(pieces):
        part = slice(n * piece, (n + 1) * piece)
        hits = group_iota == group[:, part]
        hot = hits.astype(jnp.float32)
        ranks = dot(hot.astype(jnp.bfloat16), before, NN) + carry
        carry = carry + jnp.sum(hot, axis=1, keepdims=True)
        rank = jnp.sum(jnp.where(hits, ranks, 0.0), axis=0, keepdims=True).astype(jnp.int32)
        spot[:, part] = jnp.where(member[:, part], group[:, part] * cap + rank, groups * cap)
    line = lax.broadcasted_iota(jnp.int32, (16, count), 0)
    ids_src[...] = jnp.where(
        line == 0, pos >> 5, jnp.where(line == 1, pos & 31, (line == 2).astype(jnp.int32))
    ).astype(jnp.float32).astype(jnp.bfloat16)

    def choose(q, _):
        area = pl.ds(pl.multiple_of(q * cap, cap), cap)
        pick = (
            spot[...] == q * cap + lax.broadcasted_iota(jnp.int32, (cap, count), 0)
        ).astype(jnp.float32).astype(jnp.bfloat16)
        picks[area, :] = pick
        return 0

    lax.fori_loop(0, groups, choose, 0)

    thin = piece // 2
    load.wait()

    def norm(m, _):
        area = pl.ds(pl.multiple_of(m * thin, thin), thin)
        wide = rows[area, :].astype(jnp.float32)
        squares = jnp.sum(wide * wide, axis=1, keepdims=True)
        rows[area, :] = (wide * lax.rsqrt(squares + EPSILON)).astype(jnp.bfloat16)
        return 0

    lax.fori_loop(0, count // thin, norm, 0)

    lanes = [pl.ds(a, b - a) for a, b in spans]
    last = len(spans) - 1
    lin_y = (1 - g) * tj_count + tj

    def seat(src):
        return pl.ds(pl.multiple_of(src * cap, cap), cap)

    def landed(ref, sem):
        pltpu.make_async_remote_copy(
            ref, ref, sem, sem, device_id=core_dev, device_id_type=MESH).wait_recv()

    def departed(ref, sem):
        pltpu.make_async_remote_copy(
            ref, ref, sem, sem, device_id=core_dev, device_id_type=MESH).wait_send()

    def row_copy(o, src, u):
        f, half_block, size = units[u]
        hg, hj = home(o)
        both = pl.ds(half_block, size)
        return pltpu.make_async_remote_copy(
            send.at[o, both, :, lanes[f]], got.at[both, seat(src), lanes[f]],
            d_send.at[o], d_recv.at[u], device_id=dev(hg, ti, hj), device_id_type=MESH)

    def hop_copy(o, half, u):
        f, half_block, size = units[u]
        both = pl.ds(half_block, size)
        return pltpu.make_async_remote_copy(
            send.at[o, both, :, lanes[f]], hop.at[half, both, :, lanes[f]],
            d_send.at[o], h_recv.at[half, u], device_id=y_dev, device_id_type=MESH)

    def relay_copy(half, u):
        f, half_block, size = units[u]
        hg, hj = home(half * 2 + g)
        both = pl.ds(half_block, size)
        return pltpu.make_async_remote_copy(
            hop.at[half, both, :, lanes[f]], got.at[both, seat(lin_y), lanes[f]],
            h_send.at[half], d_recv.at[u], device_id=dev(hg, ti, hj), device_id_type=MESH)

    def stay_copy(o, u):
        f, half_block, size = units[u]
        both = pl.ds(half_block, size)
        return pltpu.make_async_copy(
            send.at[o, both, :, lanes[f]], got.at[both, seat(lin), lanes[f]], d_recv.at[u])

    def id_copy(o, src):
        hg, hj = home(o)
        return pltpu.make_async_remote_copy(
            send_ids.at[pl.ds(o * 2, 2)], got_ids.at[src],
            i_send.at[o], i_recv.at[0], device_id=dev(hg, ti, hj), device_id_type=MESH)

    def is_me(o):
        hg, hj = home(o)
        return jnp.logical_and(hg == g, hj == tj)

    def level(half):
        return home(half * 2)[1] == tj

    halves = (1 - zh, zh)

    def send_ids_out():
        def one(o, _):
            for q in (o * 2, o * 2 + 1):
                pick = picks[pl.ds(pl.multiple_of(q * cap, cap), cap), :]
                send_ids[q, :, :cap] = dot(ids_src[...], pick, NT).astype(jnp.bfloat16)

            @pl.when(is_me(o))
            def _():
                pltpu.make_async_copy(
                    send_ids.at[pl.ds(o * 2, 2)], got_ids.at[lin], i_recv.at[0]).start()

            @pl.when(jnp.logical_not(is_me(o)))
            def _():
                id_copy(o, lin).start()
            return 0

        lax.fori_loop(0, homes, one, 0)

    def send_y(f, only=halves):
        for half in only:
            o = half * 2 + 1 - g

            @pl.when(level(half))
            def _(o=o):
                row_copy(o, lin, f).start()

            @pl.when(jnp.logical_not(level(half)))
            def _(o=o, half=half):
                hop_copy(o, half, f).start()

    def send_z(f, only=halves):
        for half in only:
            o = half * 2 + g

            @pl.when(level(half))
            def _(o=o):
                stay_copy(o, f).start()

            @pl.when(jnp.logical_not(level(half)))
            def _(o=o):
                row_copy(o, lin, f).start()

    def relay(f):
        for half in halves:
            @pl.when(jnp.logical_not(level(half)))
            def _(half=half):
                hop_copy(half * 2, half, f).wait_recv()
                relay_copy(half, f).start()

    def pack(fs, first=0, stop=2):
        low, high = spans[fs[0]][0], spans[fs[-1]][1]

        def one(j, _):
            half = lax.rem(1 - zh + j, 2)
            area = pl.ds(pl.multiple_of(half * sub, sub), sub)
            chosen = dot(picks[area, :], rows[:, low:high], NN).astype(jnp.bfloat16)
            send[pl.ds(half * 2, 2), :, :, low:high] = chosen.reshape(2, 2, cap, high - low)
            return 0

        lax.fori_loop(first, stop, one, 0)

    pack([0, 1], 0, 1)
    pl.semaphore_wait(barrier, devices - 1)
    send_y(0, halves[:1])
    send_z(0, halves[:1])
    send_ids_out()
    pack([0, 1], 1, 2)
    send_y(0, halves[1:])
    send_z(0, halves[1:])
    send_y(1)
    pack([2])
    relay(0)
    send_z(1)
    send_y(2)
    send_y(3)
    pack([3])
    relay(1)
    send_z(2)
    pack([4, 5])

    xbest[...] = jnp.full(xbest.shape, -2.0, jnp.float32)
    ybest[...] = jnp.full(ybest.shape, -2.0, jnp.float32)

    def read_ids():
        landed(got_ids, i_recv.at[0])
        for src in range(groups):
            for r in range(2):
                wall[r, :, src * cap : (src + 1) * cap] = got_ids[src, r, :, :cap].astype(jnp.float32)
        for r in range(2):
            where = (wall[r, 0:1] * 32.0 + wall[r, 1:2]).astype(jnp.int32)
            where = jnp.where(wall[r, 2:3] > 0.5, where, sub)

            def one(n, _, r=r, where=where):
                area = pl.ds(pl.multiple_of(r * sub + n * 128, 128), 128)
                picks[area, :] = (
                    where == n * 128 + lax.broadcasted_iota(jnp.int32, (128, count), 0)
                ).astype(jnp.float32).astype(jnp.bfloat16)
                return 0

            lax.fori_loop(0, sub // 128, one, 0)

    own, own_c, near_x, near_x_c, near_y, near_y_c, deep, deep_c, skew = range(9)
    left, right = core == 0, core == 1

    direct, passed = (own, near_x, near_y), (own_c, near_x_c, near_y_c, deep_c, deep, skew)

    def phase_of(f):
        return [n for n, (_, high) in enumerate(phases) if spans[f][1] <= high][0]

    def block_copy(source, target, c, device):
        f, start, size = cuts[c]
        area = pl.ds(start, size)
        if target in direct:
            sem = g_recv.at[direct.index(target), c]
        else:
            sem = f_recv.at[passed.index(target), phase_of(f)]
        return pltpu.make_async_remote_copy(
            raw.at[source, area, lanes[f]], raw.at[target, area, lanes[f]],
            g_send.at[target], sem, device_id=device, device_id_type=MESH)

    def of(f):
        return [c for c, cut in enumerate(cuts) if cut[0] == f]

    def collect(target, phase):
        low, high = phases[phase]
        landed(raw.at[target, :, low:high], f_recv.at[passed.index(target), phase])

    def place(r, target, c):
        f, start, size = cuts[c]
        chosen = picks[r * sub + start : r * sub + start + size, :]
        raw[target, start : start + size, lanes[f]] = dot(
            chosen, got[r, :, lanes[f]], NN).astype(jnp.bfloat16)

    def share(c):
        block_copy(own, near_y, c, y_dev).start()
        block_copy(own, near_x, c, x_dev).start()

    def arrived(u):
        f, half_block, size = units[u]
        landed(got.at[pl.ds(half_block, size), :, lanes[f]], d_recv.at[u])

    def supply_both(f, u):
        arrived(u)
        for c in of(f):
            place(1, deep, c)
            place(0, own, c)
            block_copy(deep, own, c, pair_dev).start()
            share(c)
            block_copy(deep, deep_c, c, core_dev).start()
            block_copy(own, own_c, c, core_dev).start()

    def supply_deep(f, u):
        arrived(u)
        for c in of(f):
            place(1, deep, c)
            block_copy(deep, own, c, pair_dev).start()
            block_copy(deep, deep_c, c, core_dev).start()

    def supply_own(f, u):
        arrived(u)
        for c in of(f):
            place(0, own, c)
            share(c)
            block_copy(own, own_c, c, core_dev).start()

    def supply_outer(f):
        for c in of(f):
            block_copy(own, own, c, core_dev).wait_recv()
            share(c)
            block_copy(own, own_c, c, core_dev).start()

    def forward(f, within):
        for c in of(f):
            block_copy(own, near_y, c, core_dev).wait_recv()
            if within:
                if f != 3:
                    @pl.when(right)
                    def _(c=c):
                        block_copy(near_y, skew, c, x_dev).start()

                @pl.when(left)
                def _(c=c):
                    block_copy(near_y, deep, c, pair_dev).start()

            block_copy(near_y, near_y_c, c, core_dev).start()
            block_copy(own, near_x, c, core_dev).wait_recv()
            block_copy(near_x, near_x_c, c, core_dev).start()

    inner_jobs = [(own, own_c), (own, deep), (own, deep_c), (own, near_x + x), (near_x, deep), (near_x, deep_c),
                  (own, near_y + g), (near_y, deep), (near_y, deep_c), (near_x, near_y + x)]
    right_jobs = [(own, own_c), (own, near_x + x), (own, near_y + g), (near_x, near_y + x), (near_y_c - x, near_x_c)]
    left_jobs = right_jobs[:3] + [(deep, near_x), (deep, near_x_c)]

    def table(jobs, j):
        a, b = 0, 0
        for n, (p, q) in enumerate(jobs):
            a = a + jnp.where(j == n, p, 0)
            b = b + jnp.where(j == n, q, 0)
        return a, b

    def reduce(scores, a, b, y):
        xbest[b] = jnp.maximum(xbest[b], jnp.max(scores.reshape(sub // 8, 8, sub), axis=0))
        if y is None:
            return
        side = scores[:, :128]
        for k in range(1, sub // 128):
            side = jnp.maximum(side, scores[:, k * 128 : (k + 1) * 128])
        ybest[y] = jnp.maximum(ybest[y], side)

    def tile(a, b, slot, phase, diagonal=False):
        low, high = phases[phase]
        scores = dot(raw[a, :, low:high], raw[b, :, low:high], NT)
        if phase:
            scores = scores + acc[slot]
        if phase < len(phases) - 1:
            acc[slot] = scores
            return
        if diagonal:
            same = (
                lax.broadcasted_iota(jnp.int32, (sub, sub), 0)
                == lax.broadcasted_iota(jnp.int32, (sub, sub), 1)
            )
            scores = jnp.where(same, -2.0, scores)
        reduce(scores, a, b, None if diagonal else jnp.minimum(a // 2, 2))

    def score(phase, within, start, stop):
        def one(j, _):
            if within:
                a, b = table(inner_jobs, j)
            else:
                la, lb = table(left_jobs, j)
                ra, rb = table(right_jobs, j)
                a, b = jnp.where(left, la, ra), jnp.where(left, lb, rb)
            tile(a, b, j + 1, phase)
            return 0

        lax.fori_loop(start, stop, one, 0)

    def score_early(phase, within):
        tile(own, own, 0, phase, True)
        collect(own_c, phase)
        if within:
            collect(deep_c, phase)
            score(phase, True, core, 3)
        else:
            score(phase, False, 1 - core, 1)

    def score_late(phase):
        collect(near_x_c, phase)
        collect(near_y_c, phase)
        score(phase, False, 1, jnp.where(left, 3, 5))

    def score_deep(phase):
        @pl.when(left)
        def _():
            collect(deep, phase)
            score(phase, False, 3, 5)

    split = phases[0][1]

    def begin_skew():
        @pl.when(right)
        def _():
            collect(skew, 0)
            acc[1] = dot(raw[skew, :, :split], raw[deep, :, :split], NT)

    def finish_skew():
        @pl.when(right)
        def _():
            for phase in range(1, len(phases)):
                collect(skew, phase)
            reduce(dot(raw[skew, :, split:], raw[deep, :, split:], NT) + acc[1], skew, deep, 3)
            reduce(dot(raw[skew], raw[deep_c], NT), skew, deep_c, 3)

    @pl.when(inner)
    def _():
        read_ids()
        supply_both(0, 0)
        send_y(4)
        relay(2)
        send_z(3)
        relay(3)
        send_z(4)
        supply_both(1, 1)
        forward(0, True)
        send_y(5)
        send_y(6)
        supply_deep(2, 2)
        relay(4)
        send_z(5)
        forward(1, True)
        relay(5)
        send_z(6)
        supply_own(2, 3)
        relay(6)
        send_z(7)
        send_y(7)
        send_y(8)
        send_y(9)
        score_early(0, True)
        supply_deep(3, 4)
        forward(2, True)
        supply_deep(4, 5)
        relay(7)
        send_z(8)
        relay(8)
        send_z(9)
        collect(near_x_c, 0)
        collect(near_y_c, 0)
        score(0, True, 3, 10)
        supply_own(3, 6)
        relay(9)
        score_early(1, True)
        supply_deep(5, 7)
        begin_skew()
        supply_own(4, 8)
        forward(3, True)
        supply_own(5, 9)

        @pl.when(right)
        def _():
            for c in of(3):
                block_copy(near_x, skew, c, y_dev).start()

        collect(near_x_c, 1)
        collect(near_y_c, 1)
        score(1, True, 3, 6)
        forward(4, True)
        score(1, True, 6, 10)
        score_early(2, True)
        forward(5, True)
        collect(near_x_c, 2)
        collect(near_y_c, 2)
        score(2, True, 3, 10)
        finish_skew()

    @pl.when(outer)
    def _():
        supply_outer(0)
        send_y(4)
        send_y(5)
        send_y(6)
        relay(2)
        send_z(3)
        relay(3)
        send_z(4)
        supply_outer(1)
        send_y(7)
        send_y(8)
        send_y(9)
        relay(4)
        send_z(5)
        relay(5)
        send_z(6)
        relay(6)
        send_z(7)
        forward(0, False)
        forward(1, False)
        relay(7)
        send_z(8)
        relay(8)
        send_z(9)
        relay(9)
        supply_outer(2)
        score_early(0, False)
        forward(2, False)
        supply_outer(3)
        score_late(0)
        supply_outer(4)
        score_early(1, False)
        forward(3, False)
        supply_outer(5)
        score_late(1)
        score_deep(0)
        forward(4, False)
        score_early(2, False)
        forward(5, False)
        score_late(2)
        score_deep(1)
        score_deep(2)

    role = outer.astype(jnp.int32)

    def final_dev(b):
        dx, dc, dg = b in (near_x, near_x_c, skew), b in (own_c, near_x_c, near_y_c, deep_c), b in (near_y, near_y_c, skew)
        gg = 1 - g if dg else g
        rr = role
        if b == deep:
            gg = jnp.where(inner, g, 1 - g)
        if b in (deep, deep_c):
            rr = 1 - role
        xx = 1 - x if dx else x
        cc = 1 - core if dc else core
        return zh, xx * CORES + cc, gg * 2 + rr

    def part_copy(b):
        gg, tt, jj = final_dev(b)
        return pltpu.make_async_remote_copy(
            mine.at[b], parts.at[deep if b == skew else b], p_send.at[b],
            p_recv.at[deep if b == skew else b],
            device_id=dev(gg, tt, jj), device_id_type=MESH)

    def stays(b):
        gg, tt, jj = final_dev(b)
        return jnp.logical_and(gg == g, jnp.logical_and(tt == ti, jj == tj))

    def holds(b):
        if b == deep_c:
            return inner
        if b == deep:
            return jnp.logical_or(inner, left)
        return jnp.logical_and(inner, right) if b == skew else True

    def top_of(n):
        return jnp.max(jnp.transpose(ybest[n]).reshape(16, 8, sub), axis=0)

    def give(b, top):
        mine[b] = jnp.max(top, axis=0, keepdims=True)

        @pl.when(jnp.logical_and(holds(b), stays(b)))
        def _():
            parts[deep if b == skew else b] = mine[b]

        @pl.when(jnp.logical_and(holds(b), jnp.logical_not(stays(b))))
        def _():
            part_copy(b).start()

    for b in (near_x_c, own_c, deep_c):
        give(b, xbest[b])
    give(near_x, jnp.maximum(xbest[near_x], top_of(1)))
    last_top = top_of(2)
    crossed = jnp.logical_and(outer, right)
    for b, mine_too in ((near_y, jnp.logical_or(inner, jnp.logical_and(crossed, x == 1))),
                        (near_y_c, jnp.logical_and(crossed, x == 0)),
                        (deep, jnp.logical_and(outer, left))):
        give(b, jnp.maximum(xbest[b], jnp.where(mine_too, last_top, -2.0)))
    give(own, jnp.maximum(xbest[own], top_of(0)))

    @pl.when(jnp.logical_and(inner, right))
    def _():
        give(skew, top_of(3))

    def drain(o, _):
        @pl.when(jnp.logical_not(is_me(o)))
        def _():
            departed(send_ids.at[pl.ds(o * 2, 2)], i_send.at[o])
            departed(send.at[o], d_send.at[o])
        return 0

    lax.fori_loop(0, homes, drain, 0)
    for half in halves:
        @pl.when(jnp.logical_not(level(half)))
        def _(half=half):
            departed(hop.at[half], h_send.at[half])
    for target in (near_y, near_x, own_c, near_y_c, near_x_c):
        departed(raw.at[own], g_send.at[target])

    @pl.when(inner)
    def _():
        for target in (own, deep_c):
            departed(raw.at[own], g_send.at[target])

    @pl.when(jnp.logical_and(inner, left))
    def _():
        departed(raw.at[own], g_send.at[deep])

    @pl.when(jnp.logical_and(inner, right))
    def _():
        departed(raw.at[own], g_send.at[skew])

    half, rr = tj // 2, lax.rem(tj, 2)

    @pl.when(rr == 0)
    def _():
        parts[deep_c] = jnp.full((1, sub), -2.0, jnp.float32)

    def giver(b):
        dx, dc, dg = b in (near_x, near_x_c), b in (own_c, near_x_c, near_y_c, deep_c), b in (near_y, near_y_c)
        gg = 1 - half if dg else half
        plane = rr
        xx = 1 - x if dx else x
        if b == deep:
            gg = jnp.where(rr == 0, 1 - half, half)
            xx = jnp.where(jnp.logical_and(rr == 0, right), 1 - x, x)
            plane = jnp.where(jnp.logical_and(rr == 0, left), 1, 0)
        if b == deep_c:
            plane = 1 - rr
        cc = 1 - core if dc else core
        zz = jnp.where(plane == 0, 1 - g, g)
        return gg, xx * CORES + cc, g * 2 + zz

    for b in range(8):
        gg, tt, jj = giver(b)
        here = jnp.logical_and(gg == g, jnp.logical_and(tt == ti, jj == tj))
        comes = jnp.logical_not(here)
        if b == deep_c:
            comes = jnp.logical_and(comes, rr == 1)

        @pl.when(comes)
        def _(b=b):
            part_copy(b).wait_recv()

    out_ref[...] = jnp.max(parts[...], axis=0)

    for b in range(9):
        @pl.when(jnp.logical_and(holds(b), jnp.logical_not(stays(b))))
        def _(b=b):
            part_copy(b).wait_send()


def square(corpus, slot_of_row):
    ti_count, tj_count = lax.axis_size("ti"), lax.axis_size("tj")
    _, count, features = corpus.shape
    sub = count // 2
    cap = sub // tj_count
    groups, homes = 2 * tj_count, tj_count
    unit = features // 8
    edges = (0, 1, 2, 4, 6, 7, 8)
    spans = [(a * unit, b * unit) for a, b in zip(edges, edges[1:])]
    phases = [(0, 4 * unit), (4 * unit, 6 * unit), (6 * unit, features)]
    n = len(spans)
    cuts = [(f, 0, sub) for f in range(n - 1)] + [(n - 1, 0, sub // 2), (n - 1, sub // 2, sub // 2)]
    units = [(0, 0, 2), (1, 0, 2), (2, 1, 1), (2, 0, 1), (3, 1, 1), (4, 1, 1), (3, 0, 1), (5, 1, 1), (4, 0, 1), (5, 0, 1)]
    wide_cap = -(-cap // 128) * 128
    jobs = 11
    piece = 256 if count % 256 == 0 else 128
    dma = pltpu.SemaphoreType.DMA
    vmem = pl.BlockSpec(memory_space=pltpu.VMEM)
    bf16, f32 = jnp.bfloat16, jnp.float32
    return pl.pallas_call(
        functools.partial(
            square_kernel, (ti_count, tj_count, count, features, sub, cap, spans, units, cuts, phases)),
        out_shape=jax.ShapeDtypeStruct((1, sub), f32),
        in_specs=[vmem, pl.BlockSpec(memory_space=pl.ANY)],
        out_specs=vmem,
        scratch_shapes=[
            pltpu.VMEM((count, features), bf16),
            pltpu.VMEM((1, count), jnp.int32),
            pltpu.VMEM((16, count), bf16),
            pltpu.VMEM((count, count), bf16),
            pltpu.VMEM((homes, 2, cap, features), bf16),
            pltpu.VMEM((groups, 16, wide_cap), bf16),
            pltpu.VMEM((2, 2, cap, features), bf16),
            pltpu.VMEM((2, groups * cap, features), bf16),
            pltpu.VMEM((groups, 2, 16, wide_cap), bf16),
            pltpu.VMEM((2, 16, count), f32),
            pltpu.VMEM((9, sub, features), bf16),
            pltpu.VMEM((jobs, sub, sub), f32),
            pltpu.VMEM((8, 8, sub), f32),
            pltpu.VMEM((4, sub, 128), f32),
            pltpu.VMEM((9, 1, sub), f32),
            pltpu.VMEM((8, 1, sub), f32),
            dma((1,)),
            dma((homes,)), dma((len(units),)), dma((2,)), dma((2, len(units))), dma((homes,)), dma((1,)),
            dma((9,)), dma((3, len(cuts))), dma((6, len(phases))), dma((9,)), dma((8,)),
        ],
        compiler_params=pltpu.CompilerParams(
            collective_id=1, has_side_effects=True, vmem_limit_bytes=63 * 1024 * 1024),
    )(slot_of_row, corpus)


def solution(mesh):
    in_specs = (P("grp", ("ti", "tj"), None), P("grp", ("ti", "tj")))
    out_specs = P("grp", ("ti", "tj"))
    is_square = mesh.shape["ti"] == 2 * CORES and mesh.shape["tj"] == 4
    return jax.shard_map(
        square if is_square else per_device, mesh=mesh, in_specs=in_specs, out_specs=out_specs, check_vma=False
    )
```

```python
import functools

import jax
import jax.numpy as jnp
from jax import lax
from jax.experimental import pallas as pl
from jax.experimental.pallas import tpu as pltpu
from jax.sharding import PartitionSpec as P

MESH = pl.DeviceIdType.MESH
NT = (((1,), (1,)), ((), ()))
NN = (((1,), (0,)), ((), ()))
CORES = 2
EPSILON = 1e-06


def dot(a, b, dims):
    return lax.dot_general(a, b, dims, preferred_element_type=jnp.float32)


def kernel(geo, slots_ref, corpus_ref, out_ref, spot, ids_src, send, send_ids, got, got_ids,
           picks, summed, raw, units, best, parts, s_send, s_recv, i_send, i_recv,
           b_send, b_recv, p_send, p_recv):
    ti_count, tj_count, count, features, sub, cap, chunks, parts_f = geo
    width = features // parts_f
    owners = 2 * tj_count
    xs = ti_count // CORES
    zs = tj_count // 2
    blk = sub * tj_count
    cluster = blk * ti_count
    step = sub // chunks
    g, ti, tj = lax.axis_index("grp"), lax.axis_index("ti"), lax.axis_index("tj")
    x, core = ti // CORES, ti % CORES
    zh, zl = tj // zs, tj % zs
    lin = g * tj_count + tj

    def dev(gg, tt, jj):
        return {"grp": gg, "ti": tt, "tj": jj}

    def owner_dev(k):
        d = lax.rem(lin + k, owners)
        return d, dev(d // tj_count, ti, lax.rem(d, tj_count))

    def row_dev(dx, dy):
        return dev(lax.rem(g + dy, 2), lax.rem(x + dx, xs) * CORES + core, tj)

    def col_dev(dc, dz):
        return dev(g, x * CORES + lax.rem(core + dc, CORES), zh * zs + lax.rem(zl + dz, zs))

    def final_dev(dx, dy):
        return dev(zh, lax.rem(x + dx, xs) * CORES + core, lax.rem(g + dy, 2) * zs + zl)

    def feeder_dev(dx, dy):
        return dev(dy, lax.rem(x + dx, xs) * CORES + core, g * zs + zl)

    barrier = pltpu.get_barrier_semaphore()
    greeted = 0
    targets = [owner_dev(k)[1] for k in range(1, owners)]
    targets += [row_dev(dx, dy) for dx in range(1, xs) for dy in range(2)]
    targets += [col_dev(dc, dz) for dc in range(1, CORES) for dz in range(zs)]
    targets += [final_dev(dx, dy) for dx in range(1, xs) for dy in range(2)]
    targets += [feeder_dev(dx, dy) for dx in range(1, xs) for dy in range(2)]
    for target in targets:
        pl.semaphore_signal(barrier, inc=1, device_id=target, device_id_type=MESH)
        greeted += 1

    v = slots_ref[...]
    member = v >= 0
    second = (v >= cluster).astype(jnp.int32)
    inblk = v - second * cluster - ti * blk
    s = jnp.zeros_like(v)
    for k in range(1, tj_count):
        s = s + (inblk >= k * sub).astype(jnp.int32)
    pos = inblk - s * sub
    s_hi = (s >= zs).astype(jnp.int32)
    owner = s_hi * tj_count + second * zs + s - s_hi * zs
    owner = jnp.where(member, owner, owners)
    piece = 256 if count % 256 == 0 else 128
    before = (
        lax.broadcasted_iota(jnp.int32, (piece, piece), 0)
        < lax.broadcasted_iota(jnp.int32, (piece, piece), 1)
    ).astype(jnp.bfloat16)
    carry = jnp.zeros((owners, 1), jnp.float32)
    owner_iota = lax.broadcasted_iota(jnp.int32, (owners, piece), 0)
    for p in range(count // piece):
        part = slice(p * piece, (p + 1) * piece)
        mine = owner_iota == owner[:, part]
        hot = mine.astype(jnp.float32)
        ranks = dot(hot.astype(jnp.bfloat16), before, NN) + carry
        carry = carry + jnp.sum(hot, axis=1, keepdims=True)
        rank = jnp.sum(jnp.where(mine, ranks, 0.0), axis=0, keepdims=True).astype(jnp.int32)
        spot[:, part] = jnp.where(member[:, part], owner[:, part] * cap + rank, owners * cap)
    line = lax.broadcasted_iota(jnp.int32, (16, count), 0)
    ids_src[...] = jnp.where(
        line == 0, pos >> 5, jnp.where(line == 1, pos & 31, (line == 2).astype(jnp.int32))
    ).astype(jnp.float32).astype(jnp.bfloat16)

    row_peers = [(dx, dy) for dx in range(xs) for dy in range(2)]
    col_peers = [(dc, dz) for dc in range(CORES) for dz in range(zs)]
    own = len(row_peers) - 1
    row_at = {peer: i - 1 if i else own for i, peer in enumerate(row_peers)}
    col_at = {peer: own + i for i, peer in enumerate(col_peers)}
    lanes = [pl.ds(f * width, width) for f in range(parts_f)]
    half = sub // 2

    def pick_of(k):
        d = lax.rem(lin + k, owners)
        return (
            spot[...] == d * cap + lax.broadcasted_iota(jnp.int32, (cap, count), 0)
        ).astype(jnp.float32).astype(jnp.bfloat16)

    def row_copy(k, f):
        return pltpu.make_async_remote_copy(
            send.at[k, :, lanes[f]], got.at[k, :, lanes[f]], s_send.at[k, f], s_recv.at[k, f],
            device_id=owner_dev(k)[1], device_id_type=MESH)

    def id_copy(k):
        return pltpu.make_async_remote_copy(
            send_ids.at[k], got_ids.at[k], i_send.at[k], i_recv.at[k],
            device_id=owner_dev(k)[1], device_id_type=MESH)

    def start_pair(k, f):
        if f == 0:
            id_copy(k).start()
        row_copy(k, f).start()

    def pack(f):
        def one(k, _):
            pick = pick_of(k)
            send[k, :, lanes[f]] = dot(pick, corpus_ref[0, :, lanes[f]], NN).astype(jnp.bfloat16)
            if f == 0:
                send_ids[k, :, :cap] = dot(ids_src[...], pick, NT).astype(jnp.bfloat16)

            @pl.when(k > 1)
            def _():
                start_pair(k - 1, f)
            return 0

        lax.fori_loop(1, owners, one, 0)
        pick = pick_of(0)
        got[0, :, lanes[f]] = dot(pick, corpus_ref[0, :, lanes[f]], NN).astype(jnp.bfloat16)
        if f == 0:
            got_ids[0, :, :cap] = dot(ids_src[...], pick, NT).astype(jnp.bfloat16)
        start_pair(owners - 1, f)

    def place(f):
        def one(k, first):
            if f == 0:
                line_ids = got_ids[k, :, :cap].astype(jnp.float32)
                where = (line_ids[0:1] * 32.0 + line_ids[1:2]).astype(jnp.int32)
                where = jnp.where(line_ids[2:3] > 0.5, where, sub)
                picks[k] = (
                    where == lax.broadcasted_iota(jnp.int32, (sub, cap), 0)
                ).astype(jnp.float32).astype(jnp.bfloat16)
            term = dot(picks[k], got[k, :, lanes[f]], NN)
            summed[...] = term if first else summed[...] + term

        def arrived(k, _):
            if f == 0:
                id_copy(k).wait_recv()
            row_copy(k, f).wait_recv()
            one(k, False)
            return 0

        one(0, True)
        lax.fori_loop(1, owners, arrived, 0)

    started, waited = [], set()

    def block_copy(source, target, f, h, device):
        area = (pl.ds(h * half, half), lanes[f])
        return pltpu.make_async_remote_copy(
            raw.at[(source,) + area], raw.at[(target,) + area],
            b_send.at[target, f, h], b_recv.at[target, f, h],
            device_id=device, device_id_type=MESH)

    def ship(source, target, f, h, device):
        copy = block_copy(source, target, f, h, device)
        copy.start()
        started.append(copy)

    def need(block, f, h):
        if (block, f, h) not in waited:
            waited.add((block, f, h))
            block_copy(own, block, f, h, row_dev(0, 1)).wait_recv()

    def launch(f):
        for n in range(2):
            for dx, dy in row_peers[1:]:
                if xs == 2 and dx and dy:
                    continue
                ship(own, row_at[(-dx) % xs, (-dy) % 2], f, 1 - n if dy else n, row_dev(dx, dy))
            for dc, dz in col_peers[1:]:
                if zs == 2 and dc and dz:
                    continue
                ship(own, col_at[(-dc) % CORES, (-dz) % zs], f, n, col_dev(dc, dz))

    def relay(f):
        if xs == 2:
            need(row_at[1, 0], f, 0)
            ship(row_at[1, 0], row_at[1, 1], f, 0, row_dev(0, 1))
            need(row_at[0, 1], f, 1)
            ship(row_at[0, 1], row_at[1, 1], f, 1, row_dev(1, 0))
        if zs == 2:
            for h in range(2):
                need(col_at[0, 1], f, h)
                ship(col_at[0, 1], col_at[1, 1], f, h, col_dev(1, 0))

    pl.semaphore_wait(barrier, greeted)
    ahead = 2
    for f in range(min(ahead, parts_f)):
        pack(f)
    for f in range(parts_f):
        place(f)
        raw[own, :, lanes[f]] = summed[...].astype(jnp.bfloat16)
        if f == 0:
            best[...] = jnp.full(best.shape, -2.0, jnp.float32)
        if f:
            relay(f - 1)
        launch(f)
        if f + ahead < parts_f:
            pack(f + ahead)

    def norm(block):
        for f in range(parts_f):
            for h in range(2):
                if block != own:
                    need(block, f, h)

        def one(n, _):
            area = pl.ds(pl.multiple_of(n * 128, 128), 128)
            wide = raw[block, area, :].astype(jnp.float32)
            squares = jnp.sum(wide * wide, axis=1, keepdims=True)
            units[block, area, :] = (wide * lax.rsqrt(squares + EPSILON)).astype(jnp.bfloat16)
            return 0

        lax.fori_loop(0, sub // 128, one, 0)

    def tile(row, i, col, diagonal=False):
        part = pl.ds(pl.multiple_of(i * step, step), step)
        scores = dot(units[own + col], units[row, part, :], NT)
        if diagonal:
            same = (
                lax.broadcasted_iota(jnp.int32, (sub, step), 0)
                == i * step + lax.broadcasted_iota(jnp.int32, (sub, step), 1)
            )
            scores = jnp.where(same, -2.0, scores)
        top = jnp.max(scores.reshape(sub // 8, 8, step), axis=0)
        best[row, i] = jnp.maximum(best[row, i], top)
        return 0

    norm(own)
    lax.fori_loop(0, chunks, lambda i, _: tile(own, i, 0, True), 0)
    relay(parts_f - 1)
    for col in range(1, len(col_peers)):
        norm(own + col)
        lax.fori_loop(0, chunks, lambda i, _, col=col: tile(own, i, col), 0)

    def part_copy(peer):
        return pltpu.make_async_remote_copy(
            best.at[row_at[peer]], parts.at[x * 2 + g],
            p_send.at[row_at[peer]], p_recv.at[x * 2 + g],
            device_id=final_dev(*peer), device_id_type=MESH)

    stays = zh == g

    @pl.when(stays)
    def _():
        parts[x * 2 + g] = best[own]

    @pl.when(jnp.logical_not(stays))
    def _():
        part_copy((0, 0)).start()

    order = [peer for peer in row_peers[1:] if not (peer[0] and peer[1])]
    order += [peer for peer in row_peers[1:] if peer[0] and peer[1]]
    total = chunks * len(col_peers)
    for peer in order:
        row = row_at[peer]
        norm(row)
        lax.fori_loop(
            0, total, lambda n, _, row=row: tile(row, n // len(col_peers), n % len(col_peers)), 0)
        part_copy(peer).start()

    for feeder in range(len(row_peers)):
        arrived = pltpu.make_async_remote_copy(
            best.at[0], parts.at[feeder], p_send.at[0], p_recv.at[feeder],
            device_id=row_dev(0, 1), device_id_type=MESH)
        here = jnp.logical_and(stays, x * 2 + g == feeder)

        @pl.when(jnp.logical_not(here))
        def _(arrived=arrived):
            arrived.wait_recv()
    for i in range(chunks):
        top = jnp.max(parts[:, i], axis=0)
        out_ref[:, i * step : (i + 1) * step] = jnp.max(top, axis=0, keepdims=True)

    @pl.when(jnp.logical_not(stays))
    def _():
        part_copy((0, 0)).wait_send()

    for peer in row_peers[1:]:
        part_copy(peer).wait_send()
    for copy in started:
        copy.wait_send()

    def drain(k, _):
        id_copy(k).wait_send()
        for f in range(parts_f):
            row_copy(k, f).wait_send()
        return 0

    lax.fori_loop(1, owners, drain, 0)


def per_device(corpus, slot_of_row):
    ti_count, tj_count = lax.axis_size("ti"), lax.axis_size("tj")
    _, count, features = corpus.shape
    sub = count // 2
    cap = sub // tj_count
    owners = 2 * tj_count
    chunks, parts_f = 1, 4
    step = sub // chunks
    row_blocks, col_blocks = ti_count // CORES * 2, tj_count // 2 * CORES
    blocks = row_blocks + col_blocks - 1
    wide_cap = -(-cap // 128) * 128
    dma = pltpu.SemaphoreType.DMA
    vmem = pl.BlockSpec(memory_space=pltpu.VMEM)
    return pl.pallas_call(
        functools.partial(kernel, (ti_count, tj_count, count, features, sub, cap, chunks, parts_f)),
        out_shape=jax.ShapeDtypeStruct((1, sub), jnp.float32),
        in_specs=[vmem, vmem],
        out_specs=vmem,
        scratch_shapes=[
            pltpu.VMEM((1, count), jnp.int32),
            pltpu.VMEM((16, count), jnp.bfloat16),
            pltpu.VMEM((owners, cap, features), jnp.bfloat16),
            pltpu.VMEM((owners, 16, wide_cap), jnp.bfloat16),
            pltpu.VMEM((owners, cap, features), jnp.bfloat16),
            pltpu.VMEM((owners, 16, wide_cap), jnp.bfloat16),
            pltpu.VMEM((owners, sub, cap), jnp.bfloat16),
            pltpu.VMEM((sub, features // parts_f), jnp.float32),
            pltpu.VMEM((blocks, sub, features), jnp.bfloat16),
            pltpu.VMEM((blocks, sub, features), jnp.bfloat16),
            pltpu.VMEM((row_blocks, chunks, 8, step), jnp.float32),
            pltpu.VMEM((row_blocks, chunks, 8, step), jnp.float32),
            dma((owners, parts_f)), dma((owners, parts_f)), dma((owners,)), dma((owners,)),
            dma((blocks, parts_f, 2)), dma((blocks, parts_f, 2)),
            dma((row_blocks,)), dma((row_blocks,)),
        ],
        compiler_params=pltpu.CompilerParams(
            collective_id=0, has_side_effects=True, vmem_limit_bytes=60 * 1024 * 1024),
    )(slot_of_row, corpus)


def square_kernel(geo, slots_ref, corpus_ref, out_ref, rows, spot, ids_src, picks, send, send_ids, hop,
                  got, got_ids, wall, raw, acc, xbest, ybest, mine, parts,
                  l_sem, d_send, d_recv, h_send, h_recv, i_send, i_recv, g_send, g_recv, f_recv,
                  p_send, p_recv):
    ti_count, tj_count, count, features, sub, cap, spans, units, cuts, phases = geo
    groups = 2 * tj_count
    homes = groups // 2
    blk = sub * tj_count
    cluster = blk * ti_count
    g, ti, tj = lax.axis_index("grp"), lax.axis_index("ti"), lax.axis_index("tj")
    x, core = ti // CORES, lax.rem(ti, CORES)
    zh, zl = tj // 2, lax.rem(tj, 2)
    lin = g * tj_count + tj
    inner = zl != zh
    outer = jnp.logical_not(inner)

    def dev(gg, tt, jj):
        return {"grp": gg, "ti": tt, "tj": jj}

    def home(o):
        half = o // 2
        return lax.rem(o, 2), half * 2 + 1 - half

    def at(dx, dc, dg=0):
        xx = 1 - x if dx else x
        cc = 1 - core if dc else core
        return dev(1 - g if dg else g, xx * CORES + cc, tj)

    pair_dev = dev(g, ti, zh * 2 + 1 - zl)
    core_dev, x_dev, y_dev = at(0, 1), at(1, 0), at(0, 0, 1)

    barrier = pltpu.get_barrier_semaphore()
    devices = 2 * ti_count * tj_count

    piece = 256 if count % 256 == 0 else 128
    pieces = count // piece

    load = pltpu.make_async_copy(corpus_ref.at[0], rows, l_sem.at[0])
    load.start()
    for dg in range(2):
        for dt in range(ti_count):
            for dj in range(tj_count):
                if dg or dt or dj:
                    pl.semaphore_signal(
                        barrier, inc=1, device_id_type=MESH,
                        device_id=dev(1 - g if dg else g, lax.rem(ti + dt, ti_count),
                                      lax.rem(tj + dj, tj_count)))

    v = slots_ref[...]
    member = v >= 0
    second = (v >= cluster).astype(jnp.int32)
    inblk = v - second * cluster - ti * blk
    s = jnp.zeros_like(v)
    for k in range(1, tj_count):
        s = s + (inblk >= k * sub).astype(jnp.int32)
    pos = inblk - s * sub
    group = jnp.where(member, second * tj_count + s, groups)
    before = (
        lax.broadcasted_iota(jnp.int32, (piece, piece), 0)
        < lax.broadcasted_iota(jnp.int32, (piece, piece), 1)
    ).astype(jnp.bfloat16)
    carry = jnp.zeros((groups, 1), jnp.float32)
    group_iota = lax.broadcasted_iota(jnp.int32, (groups, piece), 0)
    for n in range(pieces):
        part = slice(n * piece, (n + 1) * piece)
        hits = group_iota == group[:, part]
        hot = hits.astype(jnp.float32)
        ranks = dot(hot.astype(jnp.bfloat16), before, NN) + carry
        carry = carry + jnp.sum(hot, axis=1, keepdims=True)
        rank = jnp.sum(jnp.where(hits, ranks, 0.0), axis=0, keepdims=True).astype(jnp.int32)
        spot[:, part] = jnp.where(member[:, part], group[:, part] * cap + rank, groups * cap)
    line = lax.broadcasted_iota(jnp.int32, (16, count), 0)
    ids_src[...] = jnp.where(
        line == 0, pos >> 5, jnp.where(line == 1, pos & 31, (line == 2).astype(jnp.int32))
    ).astype(jnp.float32).astype(jnp.bfloat16)

    def choose(q, _):
        area = pl.ds(pl.multiple_of(q * cap, cap), cap)
        pick = (
            spot[...] == q * cap + lax.broadcasted_iota(jnp.int32, (cap, count), 0)
        ).astype(jnp.float32).astype(jnp.bfloat16)
        picks[area, :] = pick
        return 0

    lax.fori_loop(0, groups, choose, 0)

    thin = piece // 2
    load.wait()

    def norm(m, _):
        area = pl.ds(pl.multiple_of(m * thin, thin), thin)
        wide = rows[area, :].astype(jnp.float32)
        squares = jnp.sum(wide * wide, axis=1, keepdims=True)
        rows[area, :] = (wide * lax.rsqrt(squares + EPSILON)).astype(jnp.bfloat16)
        return 0

    lax.fori_loop(0, count // thin, norm, 0)

    lanes = [pl.ds(a, b - a) for a, b in spans]
    last = len(spans) - 1
    lin_y = (1 - g) * tj_count + tj

    def seat(src):
        return pl.ds(pl.multiple_of(src * cap, cap), cap)

    def landed(ref, sem):
        pltpu.make_async_remote_copy(
            ref, ref, sem, sem, device_id=core_dev, device_id_type=MESH).wait_recv()

    def departed(ref, sem):
        pltpu.make_async_remote_copy(
            ref, ref, sem, sem, device_id=core_dev, device_id_type=MESH).wait_send()

    def row_copy(o, src, u):
        f, half_block, size = units[u]
        hg, hj = home(o)
        both = pl.ds(half_block, size)
        return pltpu.make_async_remote_copy(
            send.at[o, both, :, lanes[f]], got.at[both, seat(src), lanes[f]],
            d_send.at[o], d_recv.at[u], device_id=dev(hg, ti, hj), device_id_type=MESH)

    def hop_copy(o, half, u):
        f, half_block, size = units[u]
        both = pl.ds(half_block, size)
        return pltpu.make_async_remote_copy(
            send.at[o, both, :, lanes[f]], hop.at[half, both, :, lanes[f]],
            d_send.at[o], h_recv.at[half, u], device_id=y_dev, device_id_type=MESH)

    def relay_copy(half, u):
        f, half_block, size = units[u]
        hg, hj = home(half * 2 + g)
        both = pl.ds(half_block, size)
        return pltpu.make_async_remote_copy(
            hop.at[half, both, :, lanes[f]], got.at[both, seat(lin_y), lanes[f]],
            h_send.at[half], d_recv.at[u], device_id=dev(hg, ti, hj), device_id_type=MESH)

    def stay_copy(o, u):
        f, half_block, size = units[u]
        both = pl.ds(half_block, size)
        return pltpu.make_async_copy(
            send.at[o, both, :, lanes[f]], got.at[both, seat(lin), lanes[f]], d_recv.at[u])

    def id_copy(o, src):
        hg, hj = home(o)
        return pltpu.make_async_remote_copy(
            send_ids.at[pl.ds(o * 2, 2)], got_ids.at[src],
            i_send.at[o], i_recv.at[0], device_id=dev(hg, ti, hj), device_id_type=MESH)

    def is_me(o):
        hg, hj = home(o)
        return jnp.logical_and(hg == g, hj == tj)

    def level(half):
        return home(half * 2)[1] == tj

    halves = (1 - zh, zh)

    def send_ids_out():
        def one(o, _):
            for q in (o * 2, o * 2 + 1):
                pick = picks[pl.ds(pl.multiple_of(q * cap, cap), cap), :]
                send_ids[q, :, :cap] = dot(ids_src[...], pick, NT).astype(jnp.bfloat16)

            @pl.when(is_me(o))
            def _():
                pltpu.make_async_copy(
                    send_ids.at[pl.ds(o * 2, 2)], got_ids.at[lin], i_recv.at[0]).start()

            @pl.when(jnp.logical_not(is_me(o)))
            def _():
                id_copy(o, lin).start()
            return 0

        lax.fori_loop(0, homes, one, 0)

    def send_y(f, only=halves):
        for half in only:
            o = half * 2 + 1 - g

            @pl.when(level(half))
            def _(o=o):
                row_copy(o, lin, f).start()

            @pl.when(jnp.logical_not(level(half)))
            def _(o=o, half=half):
                hop_copy(o, half, f).start()

    def send_z(f, only=halves):
        for half in only:
            o = half * 2 + g

            @pl.when(level(half))
            def _(o=o):
                stay_copy(o, f).start()

            @pl.when(jnp.logical_not(level(half)))
            def _(o=o):
                row_copy(o, lin, f).start()

    def relay(f):
        for half in halves:
            @pl.when(jnp.logical_not(level(half)))
            def _(half=half):
                hop_copy(half * 2, half, f).wait_recv()
                relay_copy(half, f).start()

    def pack(fs, first=0, stop=2):
        low, high = spans[fs[0]][0], spans[fs[-1]][1]

        def one(j, _):
            half = lax.rem(1 - zh + j, 2)
            area = pl.ds(pl.multiple_of(half * sub, sub), sub)
            chosen = dot(picks[area, :], rows[:, low:high], NN).astype(jnp.bfloat16)
            send[pl.ds(half * 2, 2), :, :, low:high] = chosen.reshape(2, 2, cap, high - low)
            return 0

        lax.fori_loop(first, stop, one, 0)

    pack([0, 1], 0, 1)
    pl.semaphore_wait(barrier, devices - 1)
    send_y(0, halves[:1])
    send_z(0, halves[:1])
    send_ids_out()
    pack([0, 1], 1, 2)
    send_y(0, halves[1:])
    send_z(0, halves[1:])
    send_y(1)
    pack([2])
    relay(0)
    send_z(1)
    send_y(2)
    send_y(3)
    pack([3])
    relay(1)
    send_z(2)
    pack([4, 5])

    xbest[...] = jnp.full(xbest.shape, -2.0, jnp.float32)
    ybest[...] = jnp.full(ybest.shape, -2.0, jnp.float32)

    def read_ids():
        landed(got_ids, i_recv.at[0])
        for src in range(groups):
            for r in range(2):
                wall[r, :, src * cap : (src + 1) * cap] = got_ids[src, r, :, :cap].astype(jnp.float32)
        for r in range(2):
            where = (wall[r, 0:1] * 32.0 + wall[r, 1:2]).astype(jnp.int32)
            where = jnp.where(wall[r, 2:3] > 0.5, where, sub)

            def one(n, _, r=r, where=where):
                area = pl.ds(pl.multiple_of(r * sub + n * 128, 128), 128)
                picks[area, :] = (
                    where == n * 128 + lax.broadcasted_iota(jnp.int32, (128, count), 0)
                ).astype(jnp.float32).astype(jnp.bfloat16)
                return 0

            lax.fori_loop(0, sub // 128, one, 0)

    own, own_c, near_x, near_x_c, near_y, near_y_c, deep, deep_c, skew = range(9)
    left, right = core == 0, core == 1

    direct, passed = (own, near_x, near_y), (own_c, near_x_c, near_y_c, deep_c, deep, skew)

    def phase_of(f):
        return [n for n, (_, high) in enumerate(phases) if spans[f][1] <= high][0]

    def block_copy(source, target, c, device):
        f, start, size = cuts[c]
        area = pl.ds(start, size)
        if target in direct:
            sem = g_recv.at[direct.index(target), c]
        else:
            sem = f_recv.at[passed.index(target), phase_of(f)]
        return pltpu.make_async_remote_copy(
            raw.at[source, area, lanes[f]], raw.at[target, area, lanes[f]],
            g_send.at[target], sem, device_id=device, device_id_type=MESH)

    def of(f):
        return [c for c, cut in enumerate(cuts) if cut[0] == f]

    def collect(target, phase):
        low, high = phases[phase]
        landed(raw.at[target, :, low:high], f_recv.at[passed.index(target), phase])

    def place(r, target, c):
        f, start, size = cuts[c]
        chosen = picks[r * sub + start : r * sub + start + size, :]
        raw[target, start : start + size, lanes[f]] = dot(
            chosen, got[r, :, lanes[f]], NN).astype(jnp.bfloat16)

    def share(c):
        block_copy(own, near_y, c, y_dev).start()
        block_copy(own, near_x, c, x_dev).start()

    def arrived(u):
        f, half_block, size = units[u]
        landed(got.at[pl.ds(half_block, size), :, lanes[f]], d_recv.at[u])

    def supply_both(f, u):
        arrived(u)
        for c in of(f):
            place(1, deep, c)
            place(0, own, c)
            block_copy(deep, own, c, pair_dev).start()
            share(c)
            block_copy(deep, deep_c, c, core_dev).start()
            block_copy(own, own_c, c, core_dev).start()

    def supply_deep(f, u):
        arrived(u)
        for c in of(f):
            place(1, deep, c)
            block_copy(deep, own, c, pair_dev).start()
            block_copy(deep, deep_c, c, core_dev).start()

    def supply_own(f, u):
        arrived(u)
        for c in of(f):
            place(0, own, c)
            share(c)
            block_copy(own, own_c, c, core_dev).start()

    def supply_outer(f):
        for c in of(f):
            block_copy(own, own, c, core_dev).wait_recv()
            share(c)
            block_copy(own, own_c, c, core_dev).start()

    def forward(f, within):
        for c in of(f):
            block_copy(own, near_y, c, core_dev).wait_recv()
            if within:
                if f != 3:
                    @pl.when(right)
                    def _(c=c):
                        block_copy(near_y, skew, c, x_dev).start()

                if f != last:
                    @pl.when(left)
                    def _(c=c):
                        block_copy(near_y, deep, c, pair_dev).start()

            block_copy(near_y, near_y_c, c, core_dev).start()
            block_copy(own, near_x, c, core_dev).wait_recv()
            block_copy(near_x, near_x_c, c, core_dev).start()

    inner_jobs = [(own, own_c), (own, deep), (own, deep_c), (near_x, deep), (near_x, deep_c), (near_y, deep), (near_y, deep_c),
                  (own, near_x + x), (own, near_y + g), (near_x, near_y + x)]
    right_jobs = [(own, own_c), (own, near_x + x), (own, near_y + g), (near_x, near_y + x), (near_y_c - x, near_x_c)]
    left_jobs = right_jobs[:3] + [(deep, near_x), (deep, near_x_c)]

    def table(jobs, j):
        a, b = 0, 0
        for n, (p, q) in enumerate(jobs):
            a = a + jnp.where(j == n, p, 0)
            b = b + jnp.where(j == n, q, 0)
        return a, b

    def reduce(scores, a, b, y):
        xbest[b] = jnp.maximum(xbest[b], jnp.max(scores.reshape(sub // 8, 8, sub), axis=0))
        if y is None:
            return
        side = scores[:, :128]
        for k in range(1, sub // 128):
            side = jnp.maximum(side, scores[:, k * 128 : (k + 1) * 128])
        ybest[y] = jnp.maximum(ybest[y], side)

    def tile(a, b, slot, phase, diagonal=False):
        low, high = phases[phase]
        scores = dot(raw[a, :, low:high], raw[b, :, low:high], NT)
        if phase:
            scores = scores + acc[slot]
        if phase < len(phases) - 1:
            acc[slot] = scores
            return
        if diagonal:
            same = (
                lax.broadcasted_iota(jnp.int32, (sub, sub), 0)
                == lax.broadcasted_iota(jnp.int32, (sub, sub), 1)
            )
            scores = jnp.where(same, -2.0, scores)
        reduce(scores, a, b, None if diagonal else jnp.minimum(a // 2, 2))

    def score(phase, within, start, stop):
        def one(j, _):
            if within:
                a, b = table(inner_jobs, j)
            else:
                la, lb = table(left_jobs, j)
                ra, rb = table(right_jobs, j)
                a, b = jnp.where(left, la, ra), jnp.where(left, lb, rb)
            tile(a, b, j + 1, phase)
            return 0

        lax.fori_loop(start, stop, one, 0)

    def score_early(phase, within):
        tile(own, own, 0, phase, True)
        collect(own_c, phase)
        if within:
            collect(deep_c, phase)
            score(phase, True, core, 3)
        else:
            score(phase, False, 1 - core, 1)

    def score_late(phase):
        collect(near_x_c, phase)
        collect(near_y_c, phase)
        score(phase, False, 1, jnp.where(left, 3, 5))

    def score_deep(phase):
        @pl.when(left)
        def _():
            collect(deep, phase)
            score(phase, False, 3, 5)

    split = phases[0][1]

    def begin_skew():
        @pl.when(right)
        def _():
            collect(skew, 0)
            acc[1] = dot(raw[skew, :, :split], raw[deep, :, :split], NT)

    def finish_skew():
        @pl.when(right)
        def _():
            for phase in range(1, len(phases)):
                collect(skew, phase)
            reduce(dot(raw[skew, :, split:], raw[deep, :, split:], NT) + acc[1], skew, deep, 3)
            reduce(dot(raw[skew], raw[deep_c], NT), skew, deep_c, 3)

    @pl.when(inner)
    def _():
        read_ids()
        supply_both(0, 0)
        send_y(4)
        relay(2)
        send_z(3)
        relay(3)
        send_z(4)
        supply_both(1, 1)
        forward(0, True)
        send_y(5)
        send_y(6)
        supply_deep(2, 2)
        relay(4)
        send_z(5)
        forward(1, True)
        relay(5)
        send_z(6)
        supply_own(2, 3)
        relay(6)
        send_z(7)
        send_y(7)
        send_y(8)
        send_y(9)
        score_early(0, True)
        supply_deep(3, 4)
        forward(2, True)
        supply_deep(4, 5)
        relay(7)
        send_z(8)
        relay(8)
        send_z(9)
        collect(near_x_c, 0)
        collect(near_y_c, 0)
        score(0, True, 3, 10)
        supply_own(3, 6)
        relay(9)
        score_early(1, True)
        supply_deep(5, 7)
        begin_skew()
        supply_own(4, 8)

        @pl.when(right)
        def _():
            forward(3, True)

        supply_own(5, 9)

        @pl.when(left)
        def _():
            forward(3, True)

        score(1, True, 3, 7)

        @pl.when(right)
        def _():
            for c in of(3):
                block_copy(near_x, skew, c, y_dev).start()

        @pl.when(left)
        def _():
            for c in of(last):
                block_copy(own, deep, c, dev(1 - g, ti, zh * 2 + 1 - zl)).start()

        forward(4, True)
        collect(near_x_c, 1)
        collect(near_y_c, 1)
        score(1, True, 7, 10)
        score_early(2, True)
        forward(5, True)
        score(2, True, 3, 7)
        collect(near_x_c, 2)
        collect(near_y_c, 2)
        score(2, True, 7, 10)
        finish_skew()

    @pl.when(outer)
    def _():
        supply_outer(0)
        send_y(4)
        send_y(5)
        send_y(6)
        relay(2)
        send_z(3)
        relay(3)
        send_z(4)
        supply_outer(1)
        send_y(7)
        send_y(8)
        send_y(9)
        relay(4)
        send_z(5)
        relay(5)
        send_z(6)
        relay(6)
        send_z(7)
        forward(0, False)
        forward(1, False)
        relay(7)
        send_z(8)
        relay(8)
        send_z(9)
        relay(9)
        supply_outer(2)
        score_early(0, False)
        forward(2, False)
        supply_outer(3)
        score_late(0)
        supply_outer(4)
        score_early(1, False)
        forward(3, False)
        supply_outer(5)
        score_late(1)
        score_deep(0)
        forward(4, False)
        score_early(2, False)
        forward(5, False)
        score_late(2)
        score_deep(1)
        score_deep(2)

    role = outer.astype(jnp.int32)

    def final_dev(b):
        dx, dc, dg = b in (near_x, near_x_c, skew), b in (own_c, near_x_c, near_y_c, deep_c), b in (near_y, near_y_c, skew)
        gg = 1 - g if dg else g
        rr = role
        if b == deep:
            gg = jnp.where(inner, g, 1 - g)
        if b in (deep, deep_c):
            rr = 1 - role
        xx = 1 - x if dx else x
        cc = 1 - core if dc else core
        return zh, xx * CORES + cc, gg * 2 + rr

    def part_copy(b):
        gg, tt, jj = final_dev(b)
        return pltpu.make_async_remote_copy(
            mine.at[b], parts.at[deep if b == skew else b], p_send.at[b],
            p_recv.at[deep if b == skew else b],
            device_id=dev(gg, tt, jj), device_id_type=MESH)

    def stays(b):
        gg, tt, jj = final_dev(b)
        return jnp.logical_and(gg == g, jnp.logical_and(tt == ti, jj == tj))

    def holds(b):
        if b == deep_c:
            return inner
        if b == deep:
            return jnp.logical_or(inner, left)
        return jnp.logical_and(inner, right) if b == skew else True

    def top_of(n):
        return jnp.max(jnp.transpose(ybest[n]).reshape(16, 8, sub), axis=0)

    def give(b, top):
        mine[b] = jnp.max(top, axis=0, keepdims=True)

        @pl.when(jnp.logical_and(holds(b), stays(b)))
        def _():
            parts[deep if b == skew else b] = mine[b]

        @pl.when(jnp.logical_and(holds(b), jnp.logical_not(stays(b))))
        def _():
            part_copy(b).start()

    for b in (near_x_c, own_c, deep_c):
        give(b, xbest[b])
    give(near_x, jnp.maximum(xbest[near_x], top_of(1)))
    last_top = top_of(2)
    crossed = jnp.logical_and(outer, right)
    for b, mine_too in ((near_y, jnp.logical_or(inner, jnp.logical_and(crossed, x == 1))),
                        (near_y_c, jnp.logical_and(crossed, x == 0)),
                        (deep, jnp.logical_and(outer, left))):
        give(b, jnp.maximum(xbest[b], jnp.where(mine_too, last_top, -2.0)))
    give(own, jnp.maximum(xbest[own], top_of(0)))

    @pl.when(jnp.logical_and(inner, right))
    def _():
        give(skew, top_of(3))

    def drain(o, _):
        @pl.when(jnp.logical_not(is_me(o)))
        def _():
            departed(send_ids.at[pl.ds(o * 2, 2)], i_send.at[o])
            departed(send.at[o], d_send.at[o])
        return 0

    lax.fori_loop(0, homes, drain, 0)
    for half in halves:
        @pl.when(jnp.logical_not(level(half)))
        def _(half=half):
            departed(hop.at[half], h_send.at[half])
    for target in (near_y, near_x, own_c, near_y_c, near_x_c):
        departed(raw.at[own], g_send.at[target])

    @pl.when(inner)
    def _():
        for target in (own, deep_c):
            departed(raw.at[own], g_send.at[target])

    @pl.when(jnp.logical_and(inner, left))
    def _():
        departed(raw.at[own], g_send.at[deep])

    @pl.when(jnp.logical_and(inner, right))
    def _():
        departed(raw.at[own], g_send.at[skew])

    half, rr = tj // 2, lax.rem(tj, 2)

    @pl.when(rr == 0)
    def _():
        parts[deep_c] = jnp.full((1, sub), -2.0, jnp.float32)

    def giver(b):
        dx, dc, dg = b in (near_x, near_x_c), b in (own_c, near_x_c, near_y_c, deep_c), b in (near_y, near_y_c)
        gg = 1 - half if dg else half
        plane = rr
        xx = 1 - x if dx else x
        if b == deep:
            gg = jnp.where(rr == 0, 1 - half, half)
            xx = jnp.where(jnp.logical_and(rr == 0, right), 1 - x, x)
            plane = jnp.where(jnp.logical_and(rr == 0, left), 1, 0)
        if b == deep_c:
            plane = 1 - rr
        cc = 1 - core if dc else core
        zz = jnp.where(plane == 0, 1 - g, g)
        return gg, xx * CORES + cc, g * 2 + zz

    for b in range(8):
        gg, tt, jj = giver(b)
        here = jnp.logical_and(gg == g, jnp.logical_and(tt == ti, jj == tj))
        comes = jnp.logical_not(here)
        if b == deep_c:
            comes = jnp.logical_and(comes, rr == 1)

        @pl.when(comes)
        def _(b=b):
            part_copy(b).wait_recv()

    out_ref[...] = jnp.max(parts[...], axis=0)

    for b in range(9):
        @pl.when(jnp.logical_and(holds(b), jnp.logical_not(stays(b))))
        def _(b=b):
            part_copy(b).wait_send()


def square(corpus, slot_of_row):
    ti_count, tj_count = lax.axis_size("ti"), lax.axis_size("tj")
    _, count, features = corpus.shape
    sub = count // 2
    cap = sub // tj_count
    groups, homes = 2 * tj_count, tj_count
    unit = features // 8
    edges = (0, 1, 2, 4, 6, 7, 8)
    spans = [(a * unit, b * unit) for a, b in zip(edges, edges[1:])]
    phases = [(0, 4 * unit), (4 * unit, 6 * unit), (6 * unit, features)]
    n = len(spans)
    cuts = [(f, 0, sub) for f in range(n - 1)] + [(n - 1, 0, sub // 2), (n - 1, sub // 2, sub // 2)]
    units = [(0, 0, 2), (1, 0, 2), (2, 1, 1), (2, 0, 1), (3, 1, 1), (4, 1, 1), (3, 0, 1), (5, 1, 1), (4, 0, 1), (5, 0, 1)]
    wide_cap = -(-cap // 128) * 128
    jobs = 11
    piece = 256 if count % 256 == 0 else 128
    dma = pltpu.SemaphoreType.DMA
    vmem = pl.BlockSpec(memory_space=pltpu.VMEM)
    bf16, f32 = jnp.bfloat16, jnp.float32
    return pl.pallas_call(
        functools.partial(
            square_kernel, (ti_count, tj_count, count, features, sub, cap, spans, units, cuts, phases)),
        out_shape=jax.ShapeDtypeStruct((1, sub), f32),
        in_specs=[vmem, pl.BlockSpec(memory_space=pl.ANY)],
        out_specs=vmem,
        scratch_shapes=[
            pltpu.VMEM((count, features), bf16),
            pltpu.VMEM((1, count), jnp.int32),
            pltpu.VMEM((16, count), bf16),
            pltpu.VMEM((count, count), bf16),
            pltpu.VMEM((homes, 2, cap, features), bf16),
            pltpu.VMEM((groups, 16, wide_cap), bf16),
            pltpu.VMEM((2, 2, cap, features), bf16),
            pltpu.VMEM((2, groups * cap, features), bf16),
            pltpu.VMEM((groups, 2, 16, wide_cap), bf16),
            pltpu.VMEM((2, 16, count), f32),
            pltpu.VMEM((9, sub, features), bf16),
            pltpu.VMEM((jobs, sub, sub), f32),
            pltpu.VMEM((8, 8, sub), f32),
            pltpu.VMEM((4, sub, 128), f32),
            pltpu.VMEM((9, 1, sub), f32),
            pltpu.VMEM((8, 1, sub), f32),
            dma((1,)),
            dma((homes,)), dma((len(units),)), dma((2,)), dma((2, len(units))), dma((homes,)), dma((1,)),
            dma((9,)), dma((3, len(cuts))), dma((6, len(phases))), dma((9,)), dma((8,)),
        ],
        compiler_params=pltpu.CompilerParams(
            collective_id=1, has_side_effects=True, vmem_limit_bytes=63 * 1024 * 1024),
    )(slot_of_row, corpus)


def solution(mesh):
    in_specs = (P("grp", ("ti", "tj"), None), P("grp", ("ti", "tj")))
    out_specs = P("grp", ("ti", "tj"))
    is_square = mesh.shape["ti"] == 2 * CORES and mesh.shape["tj"] == 4
    return jax.shard_map(
        square if is_square else per_device, mesh=mesh, in_specs=in_specs, out_specs=out_specs, check_vma=False
    )
```

```python
import functools

import jax
import jax.numpy as jnp
from jax import lax
from jax.experimental import pallas as pl
from jax.experimental.pallas import tpu as pltpu
from jax.sharding import PartitionSpec as P

MESH = pl.DeviceIdType.MESH
NT = (((1,), (1,)), ((), ()))
NN = (((1,), (0,)), ((), ()))
CORES = 2
EPSILON = 1e-06


def dot(a, b, dims):
    return lax.dot_general(a, b, dims, preferred_element_type=jnp.float32)


def kernel(geo, slots_ref, corpus_ref, out_ref, spot, ids_src, send, send_ids, got, got_ids,
           picks, summed, raw, units, best, parts, s_send, s_recv, i_send, i_recv,
           b_send, b_recv, p_send, p_recv):
    ti_count, tj_count, count, features, sub, cap, chunks, parts_f = geo
    width = features // parts_f
    owners = 2 * tj_count
    xs = ti_count // CORES
    zs = tj_count // 2
    blk = sub * tj_count
    cluster = blk * ti_count
    step = sub // chunks
    g, ti, tj = lax.axis_index("grp"), lax.axis_index("ti"), lax.axis_index("tj")
    x, core = ti // CORES, ti % CORES
    zh, zl = tj // zs, tj % zs
    lin = g * tj_count + tj

    def dev(gg, tt, jj):
        return {"grp": gg, "ti": tt, "tj": jj}

    def owner_dev(k):
        d = lax.rem(lin + k, owners)
        return d, dev(d // tj_count, ti, lax.rem(d, tj_count))

    def row_dev(dx, dy):
        return dev(lax.rem(g + dy, 2), lax.rem(x + dx, xs) * CORES + core, tj)

    def col_dev(dc, dz):
        return dev(g, x * CORES + lax.rem(core + dc, CORES), zh * zs + lax.rem(zl + dz, zs))

    def final_dev(dx, dy):
        return dev(zh, lax.rem(x + dx, xs) * CORES + core, lax.rem(g + dy, 2) * zs + zl)

    def feeder_dev(dx, dy):
        return dev(dy, lax.rem(x + dx, xs) * CORES + core, g * zs + zl)

    barrier = pltpu.get_barrier_semaphore()
    greeted = 0
    targets = [owner_dev(k)[1] for k in range(1, owners)]
    targets += [row_dev(dx, dy) for dx in range(1, xs) for dy in range(2)]
    targets += [col_dev(dc, dz) for dc in range(1, CORES) for dz in range(zs)]
    targets += [final_dev(dx, dy) for dx in range(1, xs) for dy in range(2)]
    targets += [feeder_dev(dx, dy) for dx in range(1, xs) for dy in range(2)]
    for target in targets:
        pl.semaphore_signal(barrier, inc=1, device_id=target, device_id_type=MESH)
        greeted += 1

    v = slots_ref[...]
    member = v >= 0
    second = (v >= cluster).astype(jnp.int32)
    inblk = v - second * cluster - ti * blk
    s = jnp.zeros_like(v)
    for k in range(1, tj_count):
        s = s + (inblk >= k * sub).astype(jnp.int32)
    pos = inblk - s * sub
    s_hi = (s >= zs).astype(jnp.int32)
    owner = s_hi * tj_count + second * zs + s - s_hi * zs
    owner = jnp.where(member, owner, owners)
    piece = 256 if count % 256 == 0 else 128
    before = (
        lax.broadcasted_iota(jnp.int32, (piece, piece), 0)
        < lax.broadcasted_iota(jnp.int32, (piece, piece), 1)
    ).astype(jnp.bfloat16)
    carry = jnp.zeros((owners, 1), jnp.float32)
    owner_iota = lax.broadcasted_iota(jnp.int32, (owners, piece), 0)
    for p in range(count // piece):
        part = slice(p * piece, (p + 1) * piece)
        mine = owner_iota == owner[:, part]
        hot = mine.astype(jnp.float32)
        ranks = dot(hot.astype(jnp.bfloat16), before, NN) + carry
        carry = carry + jnp.sum(hot, axis=1, keepdims=True)
        rank = jnp.sum(jnp.where(mine, ranks, 0.0), axis=0, keepdims=True).astype(jnp.int32)
        spot[:, part] = jnp.where(member[:, part], owner[:, part] * cap + rank, owners * cap)
    line = lax.broadcasted_iota(jnp.int32, (16, count), 0)
    ids_src[...] = jnp.where(
        line == 0, pos >> 5, jnp.where(line == 1, pos & 31, (line == 2).astype(jnp.int32))
    ).astype(jnp.float32).astype(jnp.bfloat16)

    row_peers = [(dx, dy) for dx in range(xs) for dy in range(2)]
    col_peers = [(dc, dz) for dc in range(CORES) for dz in range(zs)]
    own = len(row_peers) - 1
    row_at = {peer: i - 1 if i else own for i, peer in enumerate(row_peers)}
    col_at = {peer: own + i for i, peer in enumerate(col_peers)}
    lanes = [pl.ds(f * width, width) for f in range(parts_f)]
    half = sub // 2

    def pick_of(k):
        d = lax.rem(lin + k, owners)
        return (
            spot[...] == d * cap + lax.broadcasted_iota(jnp.int32, (cap, count), 0)
        ).astype(jnp.float32).astype(jnp.bfloat16)

    def row_copy(k, f):
        return pltpu.make_async_remote_copy(
            send.at[k, :, lanes[f]], got.at[k, :, lanes[f]], s_send.at[k, f], s_recv.at[k, f],
            device_id=owner_dev(k)[1], device_id_type=MESH)

    def id_copy(k):
        return pltpu.make_async_remote_copy(
            send_ids.at[k], got_ids.at[k], i_send.at[k], i_recv.at[k],
            device_id=owner_dev(k)[1], device_id_type=MESH)

    def start_pair(k, f):
        if f == 0:
            id_copy(k).start()
        row_copy(k, f).start()

    def pack(f):
        def one(k, _):
            pick = pick_of(k)
            send[k, :, lanes[f]] = dot(pick, corpus_ref[0, :, lanes[f]], NN).astype(jnp.bfloat16)
            if f == 0:
                send_ids[k, :, :cap] = dot(ids_src[...], pick, NT).astype(jnp.bfloat16)

            @pl.when(k > 1)
            def _():
                start_pair(k - 1, f)
            return 0

        lax.fori_loop(1, owners, one, 0)
        pick = pick_of(0)
        got[0, :, lanes[f]] = dot(pick, corpus_ref[0, :, lanes[f]], NN).astype(jnp.bfloat16)
        if f == 0:
            got_ids[0, :, :cap] = dot(ids_src[...], pick, NT).astype(jnp.bfloat16)
        start_pair(owners - 1, f)

    def place(f):
        def one(k, first):
            if f == 0:
                line_ids = got_ids[k, :, :cap].astype(jnp.float32)
                where = (line_ids[0:1] * 32.0 + line_ids[1:2]).astype(jnp.int32)
                where = jnp.where(line_ids[2:3] > 0.5, where, sub)
                picks[k] = (
                    where == lax.broadcasted_iota(jnp.int32, (sub, cap), 0)
                ).astype(jnp.float32).astype(jnp.bfloat16)
            term = dot(picks[k], got[k, :, lanes[f]], NN)
            summed[...] = term if first else summed[...] + term

        def arrived(k, _):
            if f == 0:
                id_copy(k).wait_recv()
            row_copy(k, f).wait_recv()
            one(k, False)
            return 0

        one(0, True)
        lax.fori_loop(1, owners, arrived, 0)

    started, waited = [], set()

    def block_copy(source, target, f, h, device):
        area = (pl.ds(h * half, half), lanes[f])
        return pltpu.make_async_remote_copy(
            raw.at[(source,) + area], raw.at[(target,) + area],
            b_send.at[target, f, h], b_recv.at[target, f, h],
            device_id=device, device_id_type=MESH)

    def ship(source, target, f, h, device):
        copy = block_copy(source, target, f, h, device)
        copy.start()
        started.append(copy)

    def need(block, f, h):
        if (block, f, h) not in waited:
            waited.add((block, f, h))
            block_copy(own, block, f, h, row_dev(0, 1)).wait_recv()

    def launch(f):
        for n in range(2):
            for dx, dy in row_peers[1:]:
                if xs == 2 and dx and dy:
                    continue
                ship(own, row_at[(-dx) % xs, (-dy) % 2], f, 1 - n if dy else n, row_dev(dx, dy))
            for dc, dz in col_peers[1:]:
                if zs == 2 and dc and dz:
                    continue
                ship(own, col_at[(-dc) % CORES, (-dz) % zs], f, n, col_dev(dc, dz))

    def relay(f):
        if xs == 2:
            need(row_at[1, 0], f, 0)
            ship(row_at[1, 0], row_at[1, 1], f, 0, row_dev(0, 1))
            need(row_at[0, 1], f, 1)
            ship(row_at[0, 1], row_at[1, 1], f, 1, row_dev(1, 0))
        if zs == 2:
            for h in range(2):
                need(col_at[0, 1], f, h)
                ship(col_at[0, 1], col_at[1, 1], f, h, col_dev(1, 0))

    pl.semaphore_wait(barrier, greeted)
    ahead = 2
    for f in range(min(ahead, parts_f)):
        pack(f)
    for f in range(parts_f):
        place(f)
        raw[own, :, lanes[f]] = summed[...].astype(jnp.bfloat16)
        if f == 0:
            best[...] = jnp.full(best.shape, -2.0, jnp.float32)
        if f:
            relay(f - 1)
        launch(f)
        if f + ahead < parts_f:
            pack(f + ahead)

    def norm(block):
        for f in range(parts_f):
            for h in range(2):
                if block != own:
                    need(block, f, h)

        def one(n, _):
            area = pl.ds(pl.multiple_of(n * 128, 128), 128)
            wide = raw[block, area, :].astype(jnp.float32)
            squares = jnp.sum(wide * wide, axis=1, keepdims=True)
            units[block, area, :] = (wide * lax.rsqrt(squares + EPSILON)).astype(jnp.bfloat16)
            return 0

        lax.fori_loop(0, sub // 128, one, 0)

    def tile(row, i, col, diagonal=False):
        part = pl.ds(pl.multiple_of(i * step, step), step)
        scores = dot(units[own + col], units[row, part, :], NT)
        if diagonal:
            same = (
                lax.broadcasted_iota(jnp.int32, (sub, step), 0)
                == i * step + lax.broadcasted_iota(jnp.int32, (sub, step), 1)
            )
            scores = jnp.where(same, -2.0, scores)
        top = jnp.max(scores.reshape(sub // 8, 8, step), axis=0)
        best[row, i] = jnp.maximum(best[row, i], top)
        return 0

    norm(own)
    lax.fori_loop(0, chunks, lambda i, _: tile(own, i, 0, True), 0)
    relay(parts_f - 1)
    for col in range(1, len(col_peers)):
        norm(own + col)
        lax.fori_loop(0, chunks, lambda i, _, col=col: tile(own, i, col), 0)

    def part_copy(peer):
        return pltpu.make_async_remote_copy(
            best.at[row_at[peer]], parts.at[x * 2 + g],
            p_send.at[row_at[peer]], p_recv.at[x * 2 + g],
            device_id=final_dev(*peer), device_id_type=MESH)

    stays = zh == g

    @pl.when(stays)
    def _():
        parts[x * 2 + g] = best[own]

    @pl.when(jnp.logical_not(stays))
    def _():
        part_copy((0, 0)).start()

    order = [peer for peer in row_peers[1:] if not (peer[0] and peer[1])]
    order += [peer for peer in row_peers[1:] if peer[0] and peer[1]]
    total = chunks * len(col_peers)
    for peer in order:
        row = row_at[peer]
        norm(row)
        lax.fori_loop(
            0, total, lambda n, _, row=row: tile(row, n // len(col_peers), n % len(col_peers)), 0)
        part_copy(peer).start()

    for feeder in range(len(row_peers)):
        arrived = pltpu.make_async_remote_copy(
            best.at[0], parts.at[feeder], p_send.at[0], p_recv.at[feeder],
            device_id=row_dev(0, 1), device_id_type=MESH)
        here = jnp.logical_and(stays, x * 2 + g == feeder)

        @pl.when(jnp.logical_not(here))
        def _(arrived=arrived):
            arrived.wait_recv()
    for i in range(chunks):
        top = jnp.max(parts[:, i], axis=0)
        out_ref[:, i * step : (i + 1) * step] = jnp.max(top, axis=0, keepdims=True)

    @pl.when(jnp.logical_not(stays))
    def _():
        part_copy((0, 0)).wait_send()

    for peer in row_peers[1:]:
        part_copy(peer).wait_send()
    for copy in started:
        copy.wait_send()

    def drain(k, _):
        id_copy(k).wait_send()
        for f in range(parts_f):
            row_copy(k, f).wait_send()
        return 0

    lax.fori_loop(1, owners, drain, 0)


def per_device(corpus, slot_of_row):
    ti_count, tj_count = lax.axis_size("ti"), lax.axis_size("tj")
    _, count, features = corpus.shape
    sub = count // 2
    cap = sub // tj_count
    owners = 2 * tj_count
    chunks, parts_f = 1, 4
    step = sub // chunks
    row_blocks, col_blocks = ti_count // CORES * 2, tj_count // 2 * CORES
    blocks = row_blocks + col_blocks - 1
    wide_cap = -(-cap // 128) * 128
    dma = pltpu.SemaphoreType.DMA
    vmem = pl.BlockSpec(memory_space=pltpu.VMEM)
    return pl.pallas_call(
        functools.partial(kernel, (ti_count, tj_count, count, features, sub, cap, chunks, parts_f)),
        out_shape=jax.ShapeDtypeStruct((1, sub), jnp.float32),
        in_specs=[vmem, vmem],
        out_specs=vmem,
        scratch_shapes=[
            pltpu.VMEM((1, count), jnp.int32),
            pltpu.VMEM((16, count), jnp.bfloat16),
            pltpu.VMEM((owners, cap, features), jnp.bfloat16),
            pltpu.VMEM((owners, 16, wide_cap), jnp.bfloat16),
            pltpu.VMEM((owners, cap, features), jnp.bfloat16),
            pltpu.VMEM((owners, 16, wide_cap), jnp.bfloat16),
            pltpu.VMEM((owners, sub, cap), jnp.bfloat16),
            pltpu.VMEM((sub, features // parts_f), jnp.float32),
            pltpu.VMEM((blocks, sub, features), jnp.bfloat16),
            pltpu.VMEM((blocks, sub, features), jnp.bfloat16),
            pltpu.VMEM((row_blocks, chunks, 8, step), jnp.float32),
            pltpu.VMEM((row_blocks, chunks, 8, step), jnp.float32),
            dma((owners, parts_f)), dma((owners, parts_f)), dma((owners,)), dma((owners,)),
            dma((blocks, parts_f, 2)), dma((blocks, parts_f, 2)),
            dma((row_blocks,)), dma((row_blocks,)),
        ],
        compiler_params=pltpu.CompilerParams(
            collective_id=0, has_side_effects=True, vmem_limit_bytes=60 * 1024 * 1024),
    )(slot_of_row, corpus)


def square_kernel(geo, slots_ref, corpus_ref, out_ref, rows, spot, ids_src, picks, send, send_ids, hop,
                  got, got_ids, wall, raw, acc, xbest, ybest, mine, parts,
                  l_sem, d_send, d_recv, h_send, h_recv, i_send, i_recv, g_send, g_recv, f_recv,
                  p_send, p_recv):
    ti_count, tj_count, count, features, sub, cap, spans, units, cuts, phases = geo
    groups = 2 * tj_count
    homes = groups // 2
    blk = sub * tj_count
    cluster = blk * ti_count
    g, ti, tj = lax.axis_index("grp"), lax.axis_index("ti"), lax.axis_index("tj")
    x, core = ti // CORES, lax.rem(ti, CORES)
    zh, zl = tj // 2, lax.rem(tj, 2)
    lin = g * tj_count + tj
    inner = zl != zh
    outer = jnp.logical_not(inner)

    def dev(gg, tt, jj):
        return {"grp": gg, "ti": tt, "tj": jj}

    def home(o):
        half = o // 2
        return lax.rem(o, 2), half * 2 + 1 - half

    def at(dx, dc, dg=0):
        xx = 1 - x if dx else x
        cc = 1 - core if dc else core
        return dev(1 - g if dg else g, xx * CORES + cc, tj)

    pair_dev = dev(g, ti, zh * 2 + 1 - zl)
    core_dev, x_dev, y_dev = at(0, 1), at(1, 0), at(0, 0, 1)

    barrier = pltpu.get_barrier_semaphore()
    devices = 2 * ti_count * tj_count

    piece = 256 if count % 256 == 0 else 128
    pieces = count // piece

    load = pltpu.make_async_copy(corpus_ref.at[0], rows, l_sem.at[0])
    load.start()
    for dg in range(2):
        for dt in range(ti_count):
            for dj in range(tj_count):
                if dg or dt or dj:
                    pl.semaphore_signal(
                        barrier, inc=1, device_id_type=MESH,
                        device_id=dev(1 - g if dg else g, lax.rem(ti + dt, ti_count),
                                      lax.rem(tj + dj, tj_count)))

    v = slots_ref[...]
    member = v >= 0
    second = (v >= cluster).astype(jnp.int32)
    inblk = v - second * cluster - ti * blk
    s = jnp.zeros_like(v)
    for k in range(1, tj_count):
        s = s + (inblk >= k * sub).astype(jnp.int32)
    pos = inblk - s * sub
    group = jnp.where(member, second * tj_count + s, groups)
    before = (
        lax.broadcasted_iota(jnp.int32, (piece, piece), 0)
        < lax.broadcasted_iota(jnp.int32, (piece, piece), 1)
    ).astype(jnp.bfloat16)
    carry = jnp.zeros((groups, 1), jnp.float32)
    group_iota = lax.broadcasted_iota(jnp.int32, (groups, piece), 0)
    for n in range(pieces):
        part = slice(n * piece, (n + 1) * piece)
        hits = group_iota == group[:, part]
        hot = hits.astype(jnp.float32)
        ranks = dot(hot.astype(jnp.bfloat16), before, NN) + carry
        carry = carry + jnp.sum(hot, axis=1, keepdims=True)
        rank = jnp.sum(jnp.where(hits, ranks, 0.0), axis=0, keepdims=True).astype(jnp.int32)
        spot[:, part] = jnp.where(member[:, part], group[:, part] * cap + rank, groups * cap)
    line = lax.broadcasted_iota(jnp.int32, (16, count), 0)
    ids_src[...] = jnp.where(
        line == 0, pos >> 5, jnp.where(line == 1, pos & 31, (line == 2).astype(jnp.int32))
    ).astype(jnp.float32).astype(jnp.bfloat16)

    def choose(q, _):
        area = pl.ds(pl.multiple_of(q * cap, cap), cap)
        pick = (
            spot[...] == q * cap + lax.broadcasted_iota(jnp.int32, (cap, count), 0)
        ).astype(jnp.float32).astype(jnp.bfloat16)
        picks[area, :] = pick
        return 0

    lax.fori_loop(0, groups, choose, 0)

    thin = piece // 2
    load.wait()

    def norm(m, _):
        area = pl.ds(pl.multiple_of(m * thin, thin), thin)
        wide = rows[area, :].astype(jnp.float32)
        squares = jnp.sum(wide * wide, axis=1, keepdims=True)
        rows[area, :] = (wide * lax.rsqrt(squares + EPSILON)).astype(jnp.bfloat16)
        return 0

    lax.fori_loop(0, count // thin, norm, 0)

    lanes = [pl.ds(a, b - a) for a, b in spans]
    last = len(spans) - 1
    lin_y = (1 - g) * tj_count + tj

    def seat(src):
        return pl.ds(pl.multiple_of(src * cap, cap), cap)

    def landed(ref, sem):
        pltpu.make_async_remote_copy(
            ref, ref, sem, sem, device_id=core_dev, device_id_type=MESH).wait_recv()

    def departed(ref, sem):
        pltpu.make_async_remote_copy(
            ref, ref, sem, sem, device_id=core_dev, device_id_type=MESH).wait_send()

    def row_copy(o, src, u):
        f, half_block, size = units[u]
        hg, hj = home(o)
        both = pl.ds(half_block, size)
        return pltpu.make_async_remote_copy(
            send.at[o, both, :, lanes[f]], got.at[both, seat(src), lanes[f]],
            d_send.at[o], d_recv.at[u], device_id=dev(hg, ti, hj), device_id_type=MESH)

    def hop_copy(o, half, u):
        f, half_block, size = units[u]
        both = pl.ds(half_block, size)
        return pltpu.make_async_remote_copy(
            send.at[o, both, :, lanes[f]], hop.at[half, both, :, lanes[f]],
            d_send.at[o], h_recv.at[half, u], device_id=y_dev, device_id_type=MESH)

    def relay_copy(half, u):
        f, half_block, size = units[u]
        hg, hj = home(half * 2 + g)
        both = pl.ds(half_block, size)
        return pltpu.make_async_remote_copy(
            hop.at[half, both, :, lanes[f]], got.at[both, seat(lin_y), lanes[f]],
            h_send.at[half], d_recv.at[u], device_id=dev(hg, ti, hj), device_id_type=MESH)

    def stay_copy(o, u):
        f, half_block, size = units[u]
        both = pl.ds(half_block, size)
        return pltpu.make_async_copy(
            send.at[o, both, :, lanes[f]], got.at[both, seat(lin), lanes[f]], d_recv.at[u])

    def id_copy(o, src):
        hg, hj = home(o)
        return pltpu.make_async_remote_copy(
            send_ids.at[pl.ds(o * 2, 2)], got_ids.at[src],
            i_send.at[o], i_recv.at[0], device_id=dev(hg, ti, hj), device_id_type=MESH)

    def is_me(o):
        hg, hj = home(o)
        return jnp.logical_and(hg == g, hj == tj)

    def level(half):
        return home(half * 2)[1] == tj

    halves = (1 - zh, zh)

    def send_ids_out():
        def one(o, _):
            for q in (o * 2, o * 2 + 1):
                pick = picks[pl.ds(pl.multiple_of(q * cap, cap), cap), :]
                send_ids[q, :, :cap] = dot(ids_src[...], pick, NT).astype(jnp.bfloat16)

            @pl.when(is_me(o))
            def _():
                pltpu.make_async_copy(
                    send_ids.at[pl.ds(o * 2, 2)], got_ids.at[lin], i_recv.at[0]).start()

            @pl.when(jnp.logical_not(is_me(o)))
            def _():
                id_copy(o, lin).start()
            return 0

        lax.fori_loop(0, homes, one, 0)

    def send_y(f, only=halves):
        for half in only:
            o = half * 2 + 1 - g

            @pl.when(level(half))
            def _(o=o):
                row_copy(o, lin, f).start()

            @pl.when(jnp.logical_not(level(half)))
            def _(o=o, half=half):
                hop_copy(o, half, f).start()

    def send_z(f, only=halves):
        for half in only:
            o = half * 2 + g

            @pl.when(level(half))
            def _(o=o):
                stay_copy(o, f).start()

            @pl.when(jnp.logical_not(level(half)))
            def _(o=o):
                row_copy(o, lin, f).start()

    def relay(f):
        for half in halves:
            @pl.when(jnp.logical_not(level(half)))
            def _(half=half):
                hop_copy(half * 2, half, f).wait_recv()
                relay_copy(half, f).start()

    def pack(fs, first=0, stop=2):
        low, high = spans[fs[0]][0], spans[fs[-1]][1]

        def one(j, _):
            half = lax.rem(1 - zh + j, 2)
            area = pl.ds(pl.multiple_of(half * sub, sub), sub)
            chosen = dot(picks[area, :], rows[:, low:high], NN).astype(jnp.bfloat16)
            send[pl.ds(half * 2, 2), :, :, low:high] = chosen.reshape(2, 2, cap, high - low)
            return 0

        lax.fori_loop(first, stop, one, 0)

    pack([0, 1], 0, 1)
    pl.semaphore_wait(barrier, devices - 1)
    send_y(0, halves[:1])
    send_z(0, halves[:1])
    send_ids_out()
    pack([0, 1], 1, 2)
    send_y(0, halves[1:])
    send_z(0, halves[1:])
    send_y(1)
    pack([2])
    relay(0)
    send_z(1)
    send_y(2)
    send_y(3)
    pack([3])
    relay(1)
    send_z(2)
    pack([4, 5])

    xbest[...] = jnp.full(xbest.shape, -2.0, jnp.float32)
    ybest[...] = jnp.full(ybest.shape, -2.0, jnp.float32)

    def read_ids():
        landed(got_ids, i_recv.at[0])
        for src in range(groups):
            for r in range(2):
                wall[r, :, src * cap : (src + 1) * cap] = got_ids[src, r, :, :cap].astype(jnp.float32)
        for r in range(2):
            where = (wall[r, 0:1] * 32.0 + wall[r, 1:2]).astype(jnp.int32)
            where = jnp.where(wall[r, 2:3] > 0.5, where, sub)

            def one(n, _, r=r, where=where):
                area = pl.ds(pl.multiple_of(r * sub + n * 128, 128), 128)
                picks[area, :] = (
                    where == n * 128 + lax.broadcasted_iota(jnp.int32, (128, count), 0)
                ).astype(jnp.float32).astype(jnp.bfloat16)
                return 0

            lax.fori_loop(0, sub // 128, one, 0)

    own, own_c, near_x, near_x_c, near_y, near_y_c, deep, deep_c, skew = range(9)
    left, right = core == 0, core == 1

    direct, passed = (own, near_x, near_y), (own_c, near_x_c, near_y_c, deep_c, deep, skew)

    def phase_of(f):
        return [n for n, (_, high) in enumerate(phases) if spans[f][1] <= high][0]

    def block_copy(source, target, c, device):
        f, start, size = cuts[c]
        area = pl.ds(start, size)
        if target in direct:
            sem = g_recv.at[direct.index(target), c]
        else:
            sem = f_recv.at[passed.index(target), phase_of(f)]
        return pltpu.make_async_remote_copy(
            raw.at[source, area, lanes[f]], raw.at[target, area, lanes[f]],
            g_send.at[target], sem, device_id=device, device_id_type=MESH)

    def of(f):
        return [c for c, cut in enumerate(cuts) if cut[0] == f]

    def collect(target, phase):
        low, high = phases[phase]
        landed(raw.at[target, :, low:high], f_recv.at[passed.index(target), phase])

    def place(r, target, c):
        f, start, size = cuts[c]
        chosen = picks[r * sub + start : r * sub + start + size, :]
        raw[target, start : start + size, lanes[f]] = dot(
            chosen, got[r, :, lanes[f]], NN).astype(jnp.bfloat16)

    def share(c):
        block_copy(own, near_y, c, y_dev).start()
        block_copy(own, near_x, c, x_dev).start()

    def arrived(u):
        f, half_block, size = units[u]
        landed(got.at[pl.ds(half_block, size), :, lanes[f]], d_recv.at[u])

    def supply_both(f, u):
        arrived(u)
        for c in of(f):
            place(1, deep, c)
            place(0, own, c)
            block_copy(deep, own, c, pair_dev).start()
            share(c)
            block_copy(deep, deep_c, c, core_dev).start()
            block_copy(own, own_c, c, core_dev).start()

    def supply_deep(f, u):
        arrived(u)
        for c in of(f):
            place(1, deep, c)
            block_copy(deep, own, c, pair_dev).start()
            block_copy(deep, deep_c, c, core_dev).start()

    def supply_own(f, u):
        arrived(u)
        for c in of(f):
            place(0, own, c)
            share(c)
            block_copy(own, own_c, c, core_dev).start()

    def supply_outer(f):
        for c in of(f):
            block_copy(own, own, c, core_dev).wait_recv()
            share(c)
            block_copy(own, own_c, c, core_dev).start()

    def forward(f, within):
        for c in of(f):
            block_copy(own, near_y, c, core_dev).wait_recv()
            if within:
                if f != 3:
                    @pl.when(right)
                    def _(c=c):
                        block_copy(near_y, skew, c, x_dev).start()

                if f != last:
                    @pl.when(left)
                    def _(c=c):
                        block_copy(near_y, deep, c, pair_dev).start()

            block_copy(near_y, near_y_c, c, core_dev).start()
            block_copy(own, near_x, c, core_dev).wait_recv()
            block_copy(near_x, near_x_c, c, core_dev).start()

    inner_jobs = [(own, own_c), (own, deep), (own, deep_c), (near_x, deep), (near_x, deep_c), (near_y, deep), (near_y, deep_c),
                  (own, near_x + x), (own, near_y + g), (near_x, near_y + x)]
    right_jobs = [(own, own_c), (own, near_x + x), (own, near_y + g), (near_x, near_y + x), (near_y_c - x, near_x_c)]
    left_jobs = right_jobs[:3] + [(deep, near_x), (deep, near_x_c)]

    def table(jobs, j):
        a, b = 0, 0
        for n, (p, q) in enumerate(jobs):
            a = a + jnp.where(j == n, p, 0)
            b = b + jnp.where(j == n, q, 0)
        return a, b

    def reduce(scores, a, b, y):
        xbest[b] = jnp.maximum(xbest[b], jnp.max(scores.reshape(sub // 8, 8, sub), axis=0))
        if y is None:
            return
        side = scores[:, :128]
        for k in range(1, sub // 128):
            side = jnp.maximum(side, scores[:, k * 128 : (k + 1) * 128])
        ybest[y] = jnp.maximum(ybest[y], side)

    def tile(a, b, slot, phase, diagonal=False):
        low, high = phases[phase]
        scores = dot(raw[a, :, low:high], raw[b, :, low:high], NT)
        if phase:
            scores = scores + acc[slot]
        if phase < len(phases) - 1:
            acc[slot] = scores
            return
        if diagonal:
            same = (
                lax.broadcasted_iota(jnp.int32, (sub, sub), 0)
                == lax.broadcasted_iota(jnp.int32, (sub, sub), 1)
            )
            scores = jnp.where(same, -2.0, scores)
        reduce(scores, a, b, None if diagonal else jnp.minimum(a // 2, 2))

    def score(phase, within, start, stop):
        def one(j, _):
            if within:
                a, b = table(inner_jobs, j)
            else:
                la, lb = table(left_jobs, j)
                ra, rb = table(right_jobs, j)
                a, b = jnp.where(left, la, ra), jnp.where(left, lb, rb)
            tile(a, b, j + 1, phase)
            return 0

        lax.fori_loop(start, stop, one, 0)

    def score_early(phase, within):
        tile(own, own, 0, phase, True)
        collect(own_c, phase)
        if within:
            collect(deep_c, phase)
            score(phase, True, core, 3)
        else:
            score(phase, False, 1 - core, 1)

    def score_late(phase):
        collect(near_x_c, phase)
        collect(near_y_c, phase)
        score(phase, False, 1, jnp.where(left, 3, 5))

    def score_deep(phase):
        @pl.when(left)
        def _():
            collect(deep, phase)
            score(phase, False, 3, 5)

    split = phases[0][1]

    def begin_skew():
        @pl.when(right)
        def _():
            collect(skew, 0)
            acc[1] = dot(raw[skew, :, :split], raw[deep, :, :split], NT)

    def finish_skew():
        @pl.when(right)
        def _():
            for phase in range(1, len(phases)):
                collect(skew, phase)
            reduce(dot(raw[skew, :, split:], raw[deep, :, split:], NT) + acc[1], skew, deep, 3)
            reduce(dot(raw[skew], raw[deep_c], NT), skew, deep_c, 3)

    role = outer.astype(jnp.int32)

    def final_dev(b):
        dx, dc, dg = b in (near_x, near_x_c, skew), b in (own_c, near_x_c, near_y_c, deep_c), b in (near_y, near_y_c, skew)
        gg = 1 - g if dg else g
        rr = role
        if b == deep:
            gg = jnp.where(inner, g, 1 - g)
        if b in (deep, deep_c):
            rr = 1 - role
        xx = 1 - x if dx else x
        cc = 1 - core if dc else core
        return zh, xx * CORES + cc, gg * 2 + rr

    def part_copy(b):
        gg, tt, jj = final_dev(b)
        return pltpu.make_async_remote_copy(
            mine.at[b], parts.at[deep if b == skew else b], p_send.at[b],
            p_recv.at[deep if b == skew else b],
            device_id=dev(gg, tt, jj), device_id_type=MESH)

    def stays(b):
        gg, tt, jj = final_dev(b)
        return jnp.logical_and(gg == g, jnp.logical_and(tt == ti, jj == tj))

    def holds(b):
        if b == deep_c:
            return inner
        if b == deep:
            return jnp.logical_or(inner, left)
        return jnp.logical_and(inner, right) if b == skew else True

    def top_of(n):
        return jnp.max(jnp.transpose(ybest[n]).reshape(16, 8, sub), axis=0)

    def give(b, top):
        mine[b] = jnp.max(top, axis=0, keepdims=True)

        @pl.when(jnp.logical_and(holds(b), stays(b)))
        def _():
            parts[deep if b == skew else b] = mine[b]

        @pl.when(jnp.logical_and(holds(b), jnp.logical_not(stays(b))))
        def _():
            part_copy(b).start()

    @pl.when(inner)
    def _():
        read_ids()
        supply_both(0, 0)
        send_y(4)
        relay(2)
        send_z(3)
        relay(3)
        send_z(4)
        supply_both(1, 1)
        forward(0, True)
        send_y(5)
        send_y(6)
        supply_deep(2, 2)
        relay(4)
        send_z(5)
        forward(1, True)
        relay(5)
        send_z(6)
        supply_own(2, 3)
        relay(6)
        send_z(7)
        send_y(7)
        send_y(8)
        send_y(9)
        score_early(0, True)
        supply_deep(3, 4)
        forward(2, True)
        supply_deep(4, 5)
        relay(7)
        send_z(8)
        relay(8)
        send_z(9)
        collect(near_x_c, 0)
        collect(near_y_c, 0)
        score(0, True, 3, 10)
        supply_own(3, 6)
        relay(9)
        score_early(1, True)
        supply_deep(5, 7)
        begin_skew()
        supply_own(4, 8)

        @pl.when(right)
        def _():
            forward(3, True)

        supply_own(5, 9)

        @pl.when(left)
        def _():
            forward(3, True)

        score(1, True, 3, 7)

        @pl.when(right)
        def _():
            for c in of(3):
                block_copy(near_x, skew, c, y_dev).start()

        @pl.when(left)
        def _():
            for c in of(last):
                block_copy(own, deep, c, dev(1 - g, ti, zh * 2 + 1 - zl)).start()

        forward(4, True)
        collect(near_x_c, 1)
        collect(near_y_c, 1)
        score(1, True, 7, 10)
        score_early(2, True)
        forward(5, True)
        score(2, True, 3, 7)
        collect(near_x_c, 2)
        collect(near_y_c, 2)
        score(2, True, 7, 10)
        for b in (own_c, near_x_c, near_y_c):
            give(b, xbest[b])
        for b in (own, near_x, near_y):
            give(b, jnp.maximum(xbest[b], top_of(b // 2)))
        finish_skew()
        for b in (deep, deep_c):
            give(b, xbest[b])

        @pl.when(right)
        def _():
            give(skew, top_of(3))

    @pl.when(outer)
    def _():
        supply_outer(0)
        send_y(4)
        send_y(5)
        send_y(6)
        relay(2)
        send_z(3)
        relay(3)
        send_z(4)
        supply_outer(1)
        send_y(7)
        send_y(8)
        send_y(9)
        relay(4)
        send_z(5)
        relay(5)
        send_z(6)
        relay(6)
        send_z(7)
        forward(0, False)
        forward(1, False)
        relay(7)
        send_z(8)
        relay(8)
        send_z(9)
        relay(9)
        supply_outer(2)
        score_early(0, False)
        forward(2, False)
        supply_outer(3)
        score_late(0)
        supply_outer(4)
        score_early(1, False)
        forward(3, False)
        supply_outer(5)
        score_late(1)
        score_deep(0)
        forward(4, False)
        score_early(2, False)
        forward(5, False)
        score_late(2)
        give(own_c, xbest[own_c])
        give(own, jnp.maximum(xbest[own], top_of(0)))
        crossed = top_of(2)
        for b, mine_too in ((near_y, jnp.logical_and(right, x == 1)), (near_y_c, jnp.logical_and(right, x == 0))):
            give(b, jnp.maximum(xbest[b], jnp.where(mine_too, crossed, -2.0)))
        score_deep(1)
        score_deep(2)
        give(near_x_c, xbest[near_x_c])
        give(near_x, jnp.maximum(xbest[near_x], top_of(1)))

        @pl.when(left)
        def _():
            give(deep, jnp.maximum(xbest[deep], top_of(2)))

    def drain(o, _):
        @pl.when(jnp.logical_not(is_me(o)))
        def _():
            departed(send_ids.at[pl.ds(o * 2, 2)], i_send.at[o])
            departed(send.at[o], d_send.at[o])
        return 0

    lax.fori_loop(0, homes, drain, 0)
    for half in halves:
        @pl.when(jnp.logical_not(level(half)))
        def _(half=half):
            departed(hop.at[half], h_send.at[half])
    for target in (near_y, near_x, own_c, near_y_c, near_x_c):
        departed(raw.at[own], g_send.at[target])

    @pl.when(inner)
    def _():
        for target in (own, deep_c):
            departed(raw.at[own], g_send.at[target])

    @pl.when(jnp.logical_and(inner, left))
    def _():
        departed(raw.at[own], g_send.at[deep])

    @pl.when(jnp.logical_and(inner, right))
    def _():
        departed(raw.at[own], g_send.at[skew])

    half, rr = tj // 2, lax.rem(tj, 2)

    @pl.when(rr == 0)
    def _():
        parts[deep_c] = jnp.full((1, sub), -2.0, jnp.float32)

    def giver(b):
        dx, dc, dg = b in (near_x, near_x_c), b in (own_c, near_x_c, near_y_c, deep_c), b in (near_y, near_y_c)
        gg = 1 - half if dg else half
        plane = rr
        xx = 1 - x if dx else x
        if b == deep:
            gg = jnp.where(rr == 0, 1 - half, half)
            xx = jnp.where(jnp.logical_and(rr == 0, right), 1 - x, x)
            plane = jnp.where(jnp.logical_and(rr == 0, left), 1, 0)
        if b == deep_c:
            plane = 1 - rr
        cc = 1 - core if dc else core
        zz = jnp.where(plane == 0, 1 - g, g)
        return gg, xx * CORES + cc, g * 2 + zz

    for b in range(8):
        gg, tt, jj = giver(b)
        here = jnp.logical_and(gg == g, jnp.logical_and(tt == ti, jj == tj))
        comes = jnp.logical_not(here)
        if b == deep_c:
            comes = jnp.logical_and(comes, rr == 1)

        @pl.when(comes)
        def _(b=b):
            part_copy(b).wait_recv()

    out_ref[...] = jnp.max(parts[...], axis=0)

    for b in range(9):
        @pl.when(jnp.logical_and(holds(b), jnp.logical_not(stays(b))))
        def _(b=b):
            part_copy(b).wait_send()


def square(corpus, slot_of_row):
    ti_count, tj_count = lax.axis_size("ti"), lax.axis_size("tj")
    _, count, features = corpus.shape
    sub = count // 2
    cap = sub // tj_count
    groups, homes = 2 * tj_count, tj_count
    unit = features // 8
    edges = (0, 1, 2, 4, 6, 7, 8)
    spans = [(a * unit, b * unit) for a, b in zip(edges, edges[1:])]
    phases = [(0, 4 * unit), (4 * unit, 6 * unit), (6 * unit, features)]
    n = len(spans)
    cuts = [(f, 0, sub) for f in range(n - 1)] + [(n - 1, 0, sub // 2), (n - 1, sub // 2, sub // 2)]
    units = [(0, 0, 2), (1, 0, 2), (2, 1, 1), (2, 0, 1), (3, 1, 1), (4, 1, 1), (3, 0, 1), (5, 1, 1), (4, 0, 1), (5, 0, 1)]
    wide_cap = -(-cap // 128) * 128
    jobs = 11
    piece = 256 if count % 256 == 0 else 128
    dma = pltpu.SemaphoreType.DMA
    vmem = pl.BlockSpec(memory_space=pltpu.VMEM)
    bf16, f32 = jnp.bfloat16, jnp.float32
    return pl.pallas_call(
        functools.partial(
            square_kernel, (ti_count, tj_count, count, features, sub, cap, spans, units, cuts, phases)),
        out_shape=jax.ShapeDtypeStruct((1, sub), f32),
        in_specs=[vmem, pl.BlockSpec(memory_space=pl.ANY)],
        out_specs=vmem,
        scratch_shapes=[
            pltpu.VMEM((count, features), bf16),
            pltpu.VMEM((1, count), jnp.int32),
            pltpu.VMEM((16, count), bf16),
            pltpu.VMEM((count, count), bf16),
            pltpu.VMEM((homes, 2, cap, features), bf16),
            pltpu.VMEM((groups, 16, wide_cap), bf16),
            pltpu.VMEM((2, 2, cap, features), bf16),
            pltpu.VMEM((2, groups * cap, features), bf16),
            pltpu.VMEM((groups, 2, 16, wide_cap), bf16),
            pltpu.VMEM((2, 16, count), f32),
            pltpu.VMEM((9, sub, features), bf16),
            pltpu.VMEM((jobs, sub, sub), f32),
            pltpu.VMEM((8, 8, sub), f32),
            pltpu.VMEM((4, sub, 128), f32),
            pltpu.VMEM((9, 1, sub), f32),
            pltpu.VMEM((8, 1, sub), f32),
            dma((1,)),
            dma((homes,)), dma((len(units),)), dma((2,)), dma((2, len(units))), dma((homes,)), dma((1,)),
            dma((9,)), dma((3, len(cuts))), dma((6, len(phases))), dma((9,)), dma((8,)),
        ],
        compiler_params=pltpu.CompilerParams(
            collective_id=1, has_side_effects=True, vmem_limit_bytes=63 * 1024 * 1024),
    )(slot_of_row, corpus)


def solution(mesh):
    in_specs = (P("grp", ("ti", "tj"), None), P("grp", ("ti", "tj")))
    out_specs = P("grp", ("ti", "tj"))
    is_square = mesh.shape["ti"] == 2 * CORES and mesh.shape["tj"] == 4
    return jax.shard_map(
        square if is_square else per_device, mesh=mesh, in_specs=in_specs, out_specs=out_specs, check_vma=False
    )
```

```python
import functools

import jax
import jax.numpy as jnp
from jax import lax
from jax.experimental import pallas as pl
from jax.experimental.pallas import tpu as pltpu
from jax.sharding import PartitionSpec as P

MESH = pl.DeviceIdType.MESH
NT = (((1,), (1,)), ((), ()))
NN = (((1,), (0,)), ((), ()))
CORES = 2
EPSILON = 1e-06


def dot(a, b, dims):
    return lax.dot_general(a, b, dims, preferred_element_type=jnp.float32)


def kernel(geo, slots_ref, corpus_ref, out_ref, spot, ids_src, send, send_ids, got, got_ids,
           picks, summed, raw, units, best, parts, s_send, s_recv, i_send, i_recv,
           b_send, b_recv, p_send, p_recv):
    ti_count, tj_count, count, features, sub, cap, chunks, parts_f = geo
    width = features // parts_f
    owners = 2 * tj_count
    xs = ti_count // CORES
    zs = tj_count // 2
    blk = sub * tj_count
    cluster = blk * ti_count
    step = sub // chunks
    g, ti, tj = lax.axis_index("grp"), lax.axis_index("ti"), lax.axis_index("tj")
    x, core = ti // CORES, ti % CORES
    zh, zl = tj // zs, tj % zs
    lin = g * tj_count + tj

    def dev(gg, tt, jj):
        return {"grp": gg, "ti": tt, "tj": jj}

    def owner_dev(k):
        d = lax.rem(lin + k, owners)
        return d, dev(d // tj_count, ti, lax.rem(d, tj_count))

    def row_dev(dx, dy):
        return dev(lax.rem(g + dy, 2), lax.rem(x + dx, xs) * CORES + core, tj)

    def col_dev(dc, dz):
        return dev(g, x * CORES + lax.rem(core + dc, CORES), zh * zs + lax.rem(zl + dz, zs))

    def final_dev(dx, dy):
        return dev(zh, lax.rem(x + dx, xs) * CORES + core, lax.rem(g + dy, 2) * zs + zl)

    def feeder_dev(dx, dy):
        return dev(dy, lax.rem(x + dx, xs) * CORES + core, g * zs + zl)

    barrier = pltpu.get_barrier_semaphore()
    greeted = 0
    targets = [owner_dev(k)[1] for k in range(1, owners)]
    targets += [row_dev(dx, dy) for dx in range(1, xs) for dy in range(2)]
    targets += [col_dev(dc, dz) for dc in range(1, CORES) for dz in range(zs)]
    targets += [final_dev(dx, dy) for dx in range(1, xs) for dy in range(2)]
    targets += [feeder_dev(dx, dy) for dx in range(1, xs) for dy in range(2)]
    for target in targets:
        pl.semaphore_signal(barrier, inc=1, device_id=target, device_id_type=MESH)
        greeted += 1

    v = slots_ref[...]
    member = v >= 0
    second = (v >= cluster).astype(jnp.int32)
    inblk = v - second * cluster - ti * blk
    s = jnp.zeros_like(v)
    for k in range(1, tj_count):
        s = s + (inblk >= k * sub).astype(jnp.int32)
    pos = inblk - s * sub
    s_hi = (s >= zs).astype(jnp.int32)
    owner = s_hi * tj_count + second * zs + s - s_hi * zs
    owner = jnp.where(member, owner, owners)
    piece = 256 if count % 256 == 0 else 128
    before = (
        lax.broadcasted_iota(jnp.int32, (piece, piece), 0)
        < lax.broadcasted_iota(jnp.int32, (piece, piece), 1)
    ).astype(jnp.bfloat16)
    carry = jnp.zeros((owners, 1), jnp.float32)
    owner_iota = lax.broadcasted_iota(jnp.int32, (owners, piece), 0)
    for p in range(count // piece):
        part = slice(p * piece, (p + 1) * piece)
        mine = owner_iota == owner[:, part]
        hot = mine.astype(jnp.float32)
        ranks = dot(hot.astype(jnp.bfloat16), before, NN) + carry
        carry = carry + jnp.sum(hot, axis=1, keepdims=True)
        rank = jnp.sum(jnp.where(mine, ranks, 0.0), axis=0, keepdims=True).astype(jnp.int32)
        spot[:, part] = jnp.where(member[:, part], owner[:, part] * cap + rank, owners * cap)
    line = lax.broadcasted_iota(jnp.int32, (16, count), 0)
    ids_src[...] = jnp.where(
        line == 0, pos >> 5, jnp.where(line == 1, pos & 31, (line == 2).astype(jnp.int32))
    ).astype(jnp.float32).astype(jnp.bfloat16)

    row_peers = [(dx, dy) for dx in range(xs) for dy in range(2)]
    col_peers = [(dc, dz) for dc in range(CORES) for dz in range(zs)]
    own = len(row_peers) - 1
    row_at = {peer: i - 1 if i else own for i, peer in enumerate(row_peers)}
    col_at = {peer: own + i for i, peer in enumerate(col_peers)}
    lanes = [pl.ds(f * width, width) for f in range(parts_f)]
    half = sub // 2

    def pick_of(k):
        d = lax.rem(lin + k, owners)
        return (
            spot[...] == d * cap + lax.broadcasted_iota(jnp.int32, (cap, count), 0)
        ).astype(jnp.float32).astype(jnp.bfloat16)

    def row_copy(k, f):
        return pltpu.make_async_remote_copy(
            send.at[k, :, lanes[f]], got.at[k, :, lanes[f]], s_send.at[k, f], s_recv.at[k, f],
            device_id=owner_dev(k)[1], device_id_type=MESH)

    def id_copy(k):
        return pltpu.make_async_remote_copy(
            send_ids.at[k], got_ids.at[k], i_send.at[k], i_recv.at[k],
            device_id=owner_dev(k)[1], device_id_type=MESH)

    def start_pair(k, f):
        if f == 0:
            id_copy(k).start()
        row_copy(k, f).start()

    def pack(f):
        def one(k, _):
            pick = pick_of(k)
            send[k, :, lanes[f]] = dot(pick, corpus_ref[0, :, lanes[f]], NN).astype(jnp.bfloat16)
            if f == 0:
                send_ids[k, :, :cap] = dot(ids_src[...], pick, NT).astype(jnp.bfloat16)

            @pl.when(k > 1)
            def _():
                start_pair(k - 1, f)
            return 0

        lax.fori_loop(1, owners, one, 0)
        pick = pick_of(0)
        got[0, :, lanes[f]] = dot(pick, corpus_ref[0, :, lanes[f]], NN).astype(jnp.bfloat16)
        if f == 0:
            got_ids[0, :, :cap] = dot(ids_src[...], pick, NT).astype(jnp.bfloat16)
        start_pair(owners - 1, f)

    def place(f):
        def one(k, first):
            if f == 0:
                line_ids = got_ids[k, :, :cap].astype(jnp.float32)
                where = (line_ids[0:1] * 32.0 + line_ids[1:2]).astype(jnp.int32)
                where = jnp.where(line_ids[2:3] > 0.5, where, sub)
                picks[k] = (
                    where == lax.broadcasted_iota(jnp.int32, (sub, cap), 0)
                ).astype(jnp.float32).astype(jnp.bfloat16)
            term = dot(picks[k], got[k, :, lanes[f]], NN)
            summed[...] = term if first else summed[...] + term

        def arrived(k, _):
            if f == 0:
                id_copy(k).wait_recv()
            row_copy(k, f).wait_recv()
            one(k, False)
            return 0

        one(0, True)
        lax.fori_loop(1, owners, arrived, 0)

    started, waited = [], set()

    def block_copy(source, target, f, h, device):
        area = (pl.ds(h * half, half), lanes[f])
        return pltpu.make_async_remote_copy(
            raw.at[(source,) + area], raw.at[(target,) + area],
            b_send.at[target, f, h], b_recv.at[target, f, h],
            device_id=device, device_id_type=MESH)

    def ship(source, target, f, h, device):
        copy = block_copy(source, target, f, h, device)
        copy.start()
        started.append(copy)

    def need(block, f, h):
        if (block, f, h) not in waited:
            waited.add((block, f, h))
            block_copy(own, block, f, h, row_dev(0, 1)).wait_recv()

    def launch(f):
        for n in range(2):
            for dx, dy in row_peers[1:]:
                if xs == 2 and dx and dy:
                    continue
                ship(own, row_at[(-dx) % xs, (-dy) % 2], f, 1 - n if dy else n, row_dev(dx, dy))
            for dc, dz in col_peers[1:]:
                if zs == 2 and dc and dz:
                    continue
                ship(own, col_at[(-dc) % CORES, (-dz) % zs], f, n, col_dev(dc, dz))

    def relay(f):
        if xs == 2:
            need(row_at[1, 0], f, 0)
            ship(row_at[1, 0], row_at[1, 1], f, 0, row_dev(0, 1))
            need(row_at[0, 1], f, 1)
            ship(row_at[0, 1], row_at[1, 1], f, 1, row_dev(1, 0))
        if zs == 2:
            for h in range(2):
                need(col_at[0, 1], f, h)
                ship(col_at[0, 1], col_at[1, 1], f, h, col_dev(1, 0))

    pl.semaphore_wait(barrier, greeted)
    ahead = 2
    for f in range(min(ahead, parts_f)):
        pack(f)
    for f in range(parts_f):
        place(f)
        raw[own, :, lanes[f]] = summed[...].astype(jnp.bfloat16)
        if f == 0:
            best[...] = jnp.full(best.shape, -2.0, jnp.float32)
        if f:
            relay(f - 1)
        launch(f)
        if f + ahead < parts_f:
            pack(f + ahead)

    def norm(block):
        for f in range(parts_f):
            for h in range(2):
                if block != own:
                    need(block, f, h)

        def one(n, _):
            area = pl.ds(pl.multiple_of(n * 128, 128), 128)
            wide = raw[block, area, :].astype(jnp.float32)
            squares = jnp.sum(wide * wide, axis=1, keepdims=True)
            units[block, area, :] = (wide * lax.rsqrt(squares + EPSILON)).astype(jnp.bfloat16)
            return 0

        lax.fori_loop(0, sub // 128, one, 0)

    def tile(row, i, col, diagonal=False):
        part = pl.ds(pl.multiple_of(i * step, step), step)
        scores = dot(units[own + col], units[row, part, :], NT)
        if diagonal:
            same = (
                lax.broadcasted_iota(jnp.int32, (sub, step), 0)
                == i * step + lax.broadcasted_iota(jnp.int32, (sub, step), 1)
            )
            scores = jnp.where(same, -2.0, scores)
        top = jnp.max(scores.reshape(sub // 8, 8, step), axis=0)
        best[row, i] = jnp.maximum(best[row, i], top)
        return 0

    norm(own)
    lax.fori_loop(0, chunks, lambda i, _: tile(own, i, 0, True), 0)
    relay(parts_f - 1)
    for col in range(1, len(col_peers)):
        norm(own + col)
        lax.fori_loop(0, chunks, lambda i, _, col=col: tile(own, i, col), 0)

    def part_copy(peer):
        return pltpu.make_async_remote_copy(
            best.at[row_at[peer]], parts.at[x * 2 + g],
            p_send.at[row_at[peer]], p_recv.at[x * 2 + g],
            device_id=final_dev(*peer), device_id_type=MESH)

    stays = zh == g

    @pl.when(stays)
    def _():
        parts[x * 2 + g] = best[own]

    @pl.when(jnp.logical_not(stays))
    def _():
        part_copy((0, 0)).start()

    order = [peer for peer in row_peers[1:] if not (peer[0] and peer[1])]
    order += [peer for peer in row_peers[1:] if peer[0] and peer[1]]
    total = chunks * len(col_peers)
    for peer in order:
        row = row_at[peer]
        norm(row)
        lax.fori_loop(
            0, total, lambda n, _, row=row: tile(row, n // len(col_peers), n % len(col_peers)), 0)
        part_copy(peer).start()

    for feeder in range(len(row_peers)):
        arrived = pltpu.make_async_remote_copy(
            best.at[0], parts.at[feeder], p_send.at[0], p_recv.at[feeder],
            device_id=row_dev(0, 1), device_id_type=MESH)
        here = jnp.logical_and(stays, x * 2 + g == feeder)

        @pl.when(jnp.logical_not(here))
        def _(arrived=arrived):
            arrived.wait_recv()
    for i in range(chunks):
        top = jnp.max(parts[:, i], axis=0)
        out_ref[:, i * step : (i + 1) * step] = jnp.max(top, axis=0, keepdims=True)

    @pl.when(jnp.logical_not(stays))
    def _():
        part_copy((0, 0)).wait_send()

    for peer in row_peers[1:]:
        part_copy(peer).wait_send()
    for copy in started:
        copy.wait_send()

    def drain(k, _):
        id_copy(k).wait_send()
        for f in range(parts_f):
            row_copy(k, f).wait_send()
        return 0

    lax.fori_loop(1, owners, drain, 0)


def per_device(corpus, slot_of_row):
    ti_count, tj_count = lax.axis_size("ti"), lax.axis_size("tj")
    _, count, features = corpus.shape
    sub = count // 2
    cap = sub // tj_count
    owners = 2 * tj_count
    chunks, parts_f = 1, 4
    step = sub // chunks
    row_blocks, col_blocks = ti_count // CORES * 2, tj_count // 2 * CORES
    blocks = row_blocks + col_blocks - 1
    wide_cap = -(-cap // 128) * 128
    dma = pltpu.SemaphoreType.DMA
    vmem = pl.BlockSpec(memory_space=pltpu.VMEM)
    return pl.pallas_call(
        functools.partial(kernel, (ti_count, tj_count, count, features, sub, cap, chunks, parts_f)),
        out_shape=jax.ShapeDtypeStruct((1, sub), jnp.float32),
        in_specs=[vmem, vmem],
        out_specs=vmem,
        scratch_shapes=[
            pltpu.VMEM((1, count), jnp.int32),
            pltpu.VMEM((16, count), jnp.bfloat16),
            pltpu.VMEM((owners, cap, features), jnp.bfloat16),
            pltpu.VMEM((owners, 16, wide_cap), jnp.bfloat16),
            pltpu.VMEM((owners, cap, features), jnp.bfloat16),
            pltpu.VMEM((owners, 16, wide_cap), jnp.bfloat16),
            pltpu.VMEM((owners, sub, cap), jnp.bfloat16),
            pltpu.VMEM((sub, features // parts_f), jnp.float32),
            pltpu.VMEM((blocks, sub, features), jnp.bfloat16),
            pltpu.VMEM((blocks, sub, features), jnp.bfloat16),
            pltpu.VMEM((row_blocks, chunks, 8, step), jnp.float32),
            pltpu.VMEM((row_blocks, chunks, 8, step), jnp.float32),
            dma((owners, parts_f)), dma((owners, parts_f)), dma((owners,)), dma((owners,)),
            dma((blocks, parts_f, 2)), dma((blocks, parts_f, 2)),
            dma((row_blocks,)), dma((row_blocks,)),
        ],
        compiler_params=pltpu.CompilerParams(
            collective_id=0, has_side_effects=True, vmem_limit_bytes=60 * 1024 * 1024),
    )(slot_of_row, corpus)


def square_kernel(geo, slots_ref, corpus_ref, out_ref, rows, spot, ids_src, picks, send, send_ids, hop,
                  got, got_ids, wall, raw, acc, xbest, ybest, mine, parts,
                  l_sem, d_send, d_recv, h_send, h_recv, i_send, i_recv, g_send, g_recv, f_recv,
                  p_send, p_recv):
    ti_count, tj_count, count, features, sub, cap, spans, units, cuts, phases = geo
    groups = 2 * tj_count
    homes = groups // 2
    blk = sub * tj_count
    cluster = blk * ti_count
    g, ti, tj = lax.axis_index("grp"), lax.axis_index("ti"), lax.axis_index("tj")
    x, core = ti // CORES, lax.rem(ti, CORES)
    zh, zl = tj // 2, lax.rem(tj, 2)
    lin = g * tj_count + tj
    inner = zl != zh
    outer = jnp.logical_not(inner)

    def dev(gg, tt, jj):
        return {"grp": gg, "ti": tt, "tj": jj}

    def home(o):
        half = o // 2
        return lax.rem(o, 2), half * 2 + 1 - half

    def at(dx, dc, dg=0):
        xx = 1 - x if dx else x
        cc = 1 - core if dc else core
        return dev(1 - g if dg else g, xx * CORES + cc, tj)

    pair_dev = dev(g, ti, zh * 2 + 1 - zl)
    core_dev, x_dev, y_dev = at(0, 1), at(1, 0), at(0, 0, 1)

    barrier = pltpu.get_barrier_semaphore()
    devices = 2 * ti_count * tj_count

    piece = 256 if count % 256 == 0 else 128
    pieces = count // piece

    load = pltpu.make_async_copy(corpus_ref.at[0], rows, l_sem.at[0])
    load.start()
    for dg in range(2):
        for dt in range(ti_count):
            for dj in range(tj_count):
                if dg or dt or dj:
                    pl.semaphore_signal(
                        barrier, inc=1, device_id_type=MESH,
                        device_id=dev(1 - g if dg else g, lax.rem(ti + dt, ti_count),
                                      lax.rem(tj + dj, tj_count)))

    v = slots_ref[...]
    member = v >= 0
    second = (v >= cluster).astype(jnp.int32)
    inblk = v - second * cluster - ti * blk
    s = jnp.zeros_like(v)
    for k in range(1, tj_count):
        s = s + (inblk >= k * sub).astype(jnp.int32)
    pos = inblk - s * sub
    group = jnp.where(member, second * tj_count + s, groups)
    before = (
        lax.broadcasted_iota(jnp.int32, (piece, piece), 0)
        < lax.broadcasted_iota(jnp.int32, (piece, piece), 1)
    ).astype(jnp.bfloat16)
    carry = jnp.zeros((groups, 1), jnp.float32)
    group_iota = lax.broadcasted_iota(jnp.int32, (groups, piece), 0)
    for n in range(pieces):
        part = slice(n * piece, (n + 1) * piece)
        hits = group_iota == group[:, part]
        hot = hits.astype(jnp.float32)
        ranks = dot(hot.astype(jnp.bfloat16), before, NN) + carry
        carry = carry + jnp.sum(hot, axis=1, keepdims=True)
        rank = jnp.sum(jnp.where(hits, ranks, 0.0), axis=0, keepdims=True).astype(jnp.int32)
        spot[:, part] = jnp.where(member[:, part], group[:, part] * cap + rank, groups * cap)
    line = lax.broadcasted_iota(jnp.int32, (16, count), 0)
    ids_src[...] = jnp.where(
        line == 0, pos >> 5, jnp.where(line == 1, pos & 31, (line == 2).astype(jnp.int32))
    ).astype(jnp.float32).astype(jnp.bfloat16)

    def choose(q, _):
        area = pl.ds(pl.multiple_of(q * cap, cap), cap)
        pick = (
            spot[...] == q * cap + lax.broadcasted_iota(jnp.int32, (cap, count), 0)
        ).astype(jnp.float32).astype(jnp.bfloat16)
        picks[area, :] = pick
        return 0

    lax.fori_loop(0, groups, choose, 0)

    thin = piece // 2
    load.wait()

    def norm(m, _):
        area = pl.ds(pl.multiple_of(m * thin, thin), thin)
        wide = rows[area, :].astype(jnp.float32)
        squares = jnp.sum(wide * wide, axis=1, keepdims=True)
        rows[area, :] = (wide * lax.rsqrt(squares + EPSILON)).astype(jnp.bfloat16)
        return 0

    lax.fori_loop(0, count // thin, norm, 0)

    lanes = [pl.ds(a, b - a) for a, b in spans]
    last = len(spans) - 1
    lin_y = (1 - g) * tj_count + tj

    def seat(src):
        return pl.ds(pl.multiple_of(src * cap, cap), cap)

    def landed(ref, sem):
        pltpu.make_async_remote_copy(
            ref, ref, sem, sem, device_id=core_dev, device_id_type=MESH).wait_recv()

    def departed(ref, sem):
        pltpu.make_async_remote_copy(
            ref, ref, sem, sem, device_id=core_dev, device_id_type=MESH).wait_send()

    def row_copy(o, src, u):
        f, half_block, size = units[u]
        hg, hj = home(o)
        both = pl.ds(half_block, size)
        return pltpu.make_async_remote_copy(
            send.at[o, both, :, lanes[f]], got.at[both, seat(src), lanes[f]],
            d_send.at[o], d_recv.at[u], device_id=dev(hg, ti, hj), device_id_type=MESH)

    def hop_copy(o, half, u):
        f, half_block, size = units[u]
        both = pl.ds(half_block, size)
        return pltpu.make_async_remote_copy(
            send.at[o, both, :, lanes[f]], hop.at[half, both, :, lanes[f]],
            d_send.at[o], h_recv.at[half, u], device_id=y_dev, device_id_type=MESH)

    def relay_copy(half, u):
        f, half_block, size = units[u]
        hg, hj = home(half * 2 + g)
        both = pl.ds(half_block, size)
        return pltpu.make_async_remote_copy(
            hop.at[half, both, :, lanes[f]], got.at[both, seat(lin_y), lanes[f]],
            h_send.at[half], d_recv.at[u], device_id=dev(hg, ti, hj), device_id_type=MESH)

    def stay_copy(o, u):
        f, half_block, size = units[u]
        both = pl.ds(half_block, size)
        return pltpu.make_async_copy(
            send.at[o, both, :, lanes[f]], got.at[both, seat(lin), lanes[f]], d_recv.at[u])

    def id_copy(o, src):
        hg, hj = home(o)
        return pltpu.make_async_remote_copy(
            send_ids.at[pl.ds(o * 2, 2)], got_ids.at[src],
            i_send.at[o], i_recv.at[0], device_id=dev(hg, ti, hj), device_id_type=MESH)

    def is_me(o):
        hg, hj = home(o)
        return jnp.logical_and(hg == g, hj == tj)

    def level(half):
        return home(half * 2)[1] == tj

    halves = (1 - zh, zh)

    def send_ids_out():
        def one(o, _):
            for q in (o * 2, o * 2 + 1):
                pick = picks[pl.ds(pl.multiple_of(q * cap, cap), cap), :]
                send_ids[q, :, :cap] = dot(ids_src[...], pick, NT).astype(jnp.bfloat16)

            @pl.when(is_me(o))
            def _():
                pltpu.make_async_copy(
                    send_ids.at[pl.ds(o * 2, 2)], got_ids.at[lin], i_recv.at[0]).start()

            @pl.when(jnp.logical_not(is_me(o)))
            def _():
                id_copy(o, lin).start()
            return 0

        lax.fori_loop(0, homes, one, 0)

    def send_y(f, only=halves):
        for half in only:
            o = half * 2 + 1 - g

            @pl.when(level(half))
            def _(o=o):
                row_copy(o, lin, f).start()

            @pl.when(jnp.logical_not(level(half)))
            def _(o=o, half=half):
                hop_copy(o, half, f).start()

    def send_z(f, only=halves):
        for half in only:
            o = half * 2 + g

            @pl.when(level(half))
            def _(o=o):
                stay_copy(o, f).start()

            @pl.when(jnp.logical_not(level(half)))
            def _(o=o):
                row_copy(o, lin, f).start()

    def relay(f):
        for half in halves:
            @pl.when(jnp.logical_not(level(half)))
            def _(half=half):
                hop_copy(half * 2, half, f).wait_recv()
                relay_copy(half, f).start()

    def pack(fs, first=0, stop=2):
        low, high = spans[fs[0]][0], spans[fs[-1]][1]

        def one(j, _):
            half = lax.rem(1 - zh + j, 2)
            area = pl.ds(pl.multiple_of(half * sub, sub), sub)
            chosen = dot(picks[area, :], rows[:, low:high], NN).astype(jnp.bfloat16)
            send[pl.ds(half * 2, 2), :, :, low:high] = chosen.reshape(2, 2, cap, high - low)
            return 0

        lax.fori_loop(first, stop, one, 0)

    pack([0, 1], 0, 1)
    pl.semaphore_wait(barrier, devices - 1)
    send_y(0, halves[:1])
    send_z(0, halves[:1])
    send_ids_out()
    pack([0, 1], 1, 2)
    send_y(0, halves[1:])
    send_z(0, halves[1:])
    send_y(1)
    pack([2])
    relay(0)
    send_z(1)
    send_y(2)
    send_y(3)
    pack([3])
    relay(1)
    send_z(2)
    pack([4, 5])

    xbest[...] = jnp.full(xbest.shape, -2.0, jnp.float32)
    ybest[...] = jnp.full(ybest.shape, -2.0, jnp.float32)

    def read_ids():
        landed(got_ids, i_recv.at[0])
        for src in range(groups):
            for r in range(2):
                wall[r, :, src * cap : (src + 1) * cap] = got_ids[src, r, :, :cap].astype(jnp.float32)
        for r in range(2):
            where = (wall[r, 0:1] * 32.0 + wall[r, 1:2]).astype(jnp.int32)
            where = jnp.where(wall[r, 2:3] > 0.5, where, sub)

            def one(n, _, r=r, where=where):
                area = pl.ds(pl.multiple_of(r * sub + n * 128, 128), 128)
                picks[area, :] = (
                    where == n * 128 + lax.broadcasted_iota(jnp.int32, (128, count), 0)
                ).astype(jnp.float32).astype(jnp.bfloat16)
                return 0

            lax.fori_loop(0, sub // 128, one, 0)

    own, own_c, near_x, near_x_c, near_y, near_y_c, deep, deep_c, skew = range(9)
    left, right = core == 0, core == 1

    direct, passed = (own, near_x, near_y), (own_c, near_x_c, near_y_c, deep_c, deep, skew)

    def phase_of(f):
        return [n for n, (_, high) in enumerate(phases) if spans[f][1] <= high][0]

    def block_copy(source, target, c, device):
        f, start, size = cuts[c]
        area = pl.ds(start, size)
        if target in direct:
            sem = g_recv.at[direct.index(target), c]
        else:
            sem = f_recv.at[passed.index(target), phase_of(f)]
        return pltpu.make_async_remote_copy(
            raw.at[source, area, lanes[f]], raw.at[target, area, lanes[f]],
            g_send.at[target], sem, device_id=device, device_id_type=MESH)

    def of(f):
        return [c for c, cut in enumerate(cuts) if cut[0] == f]

    def collect(target, phase):
        low, high = phases[phase]
        landed(raw.at[target, :, low:high], f_recv.at[passed.index(target), phase])

    def place(r, target, c):
        f, start, size = cuts[c]
        chosen = picks[r * sub + start : r * sub + start + size, :]
        raw[target, start : start + size, lanes[f]] = dot(
            chosen, got[r, :, lanes[f]], NN).astype(jnp.bfloat16)

    def share(c):
        block_copy(own, near_y, c, y_dev).start()
        block_copy(own, near_x, c, x_dev).start()

    def arrived(u):
        f, half_block, size = units[u]
        landed(got.at[pl.ds(half_block, size), :, lanes[f]], d_recv.at[u])

    def supply_both(f, u):
        arrived(u)
        for c in of(f):
            place(1, deep, c)
            place(0, own, c)
            block_copy(deep, own, c, pair_dev).start()
            share(c)
            block_copy(deep, deep_c, c, core_dev).start()
            block_copy(own, own_c, c, core_dev).start()

    def supply_deep(f, u):
        arrived(u)
        for c in of(f):
            place(1, deep, c)
            block_copy(deep, own, c, pair_dev).start()
            block_copy(deep, deep_c, c, core_dev).start()

    def supply_own(f, u):
        arrived(u)
        for c in of(f):
            place(0, own, c)
            share(c)
            block_copy(own, own_c, c, core_dev).start()

    def supply_outer(f):
        for c in of(f):
            block_copy(own, own, c, core_dev).wait_recv()
            share(c)
            block_copy(own, own_c, c, core_dev).start()

    def forward(f, within):
        for c in of(f):
            block_copy(own, near_y, c, core_dev).wait_recv()
            if within:
                if f != 3:
                    @pl.when(right)
                    def _(c=c):
                        block_copy(near_y, skew, c, x_dev).start()

                if f != last:
                    @pl.when(left)
                    def _(c=c):
                        block_copy(near_y, deep, c, pair_dev).start()

            block_copy(near_y, near_y_c, c, core_dev).start()
            block_copy(own, near_x, c, core_dev).wait_recv()
            block_copy(near_x, near_x_c, c, core_dev).start()

    inner_jobs = [(own, own_c), (own, deep), (own, deep_c), (near_x, deep), (near_x, deep_c), (near_y, deep), (near_y, deep_c),
                  (own, near_x + x), (own, near_y + g), (near_x, near_y + x)]
    right_jobs = [(own, own_c), (own, near_x + x), (own, near_y + g), (near_x, near_y + x), (near_y_c - x, near_x_c)]
    left_jobs = right_jobs[:3] + [(deep, near_x), (deep, near_x_c)]

    def table(jobs, j):
        a, b = 0, 0
        for n, (p, q) in enumerate(jobs):
            a = a + jnp.where(j == n, p, 0)
            b = b + jnp.where(j == n, q, 0)
        return a, b

    def reduce(scores, a, b, y):
        xbest[b] = jnp.maximum(xbest[b], jnp.max(scores.reshape(sub // 8, 8, sub), axis=0))
        if y is None:
            return
        side = scores[:, :128]
        for k in range(1, sub // 128):
            side = jnp.maximum(side, scores[:, k * 128 : (k + 1) * 128])
        ybest[y] = jnp.maximum(ybest[y], side)

    def tile(a, b, slot, phase, diagonal=False):
        low, high = phases[phase]
        scores = dot(raw[a, :, low:high], raw[b, :, low:high], NT)
        if phase:
            scores = scores + acc[slot]
        if phase < len(phases) - 1:
            acc[slot] = scores
            return
        if diagonal:
            same = (
                lax.broadcasted_iota(jnp.int32, (sub, sub), 0)
                == lax.broadcasted_iota(jnp.int32, (sub, sub), 1)
            )
            scores = jnp.where(same, -2.0, scores)
        reduce(scores, a, b, None if diagonal else jnp.minimum(a // 2, 2))

    def score(phase, within, start, stop):
        def one(j, _):
            if within:
                a, b = table(inner_jobs, j)
            else:
                la, lb = table(left_jobs, j)
                ra, rb = table(right_jobs, j)
                a, b = jnp.where(left, la, ra), jnp.where(left, lb, rb)
            tile(a, b, j + 1, phase)
            return 0

        lax.fori_loop(start, stop, one, 0)

    def score_early(phase, within):
        tile(own, own, 0, phase, True)
        collect(own_c, phase)
        if within:
            collect(deep_c, phase)
            score(phase, True, core, 3)
        else:
            score(phase, False, 1 - core, 1)

    def score_late(phase):
        collect(near_x_c, phase)
        collect(near_y_c, phase)
        score(phase, False, 1, jnp.where(left, 3, 5))

    def score_deep(phase):
        @pl.when(left)
        def _():
            collect(deep, phase)
            score(phase, False, 3, 5)

    split = phases[0][1]

    def begin_skew():
        @pl.when(right)
        def _():
            collect(skew, 0)
            acc[1] = dot(raw[skew, :, :split], raw[deep, :, :split], NT)

    def finish_skew():
        @pl.when(right)
        def _():
            for phase in range(1, len(phases)):
                collect(skew, phase)
            reduce(dot(raw[skew, :, split:], raw[deep, :, split:], NT) + acc[1], skew, deep, 3)
            reduce(dot(raw[skew], raw[deep_c], NT), skew, deep_c, 3)

    role = outer.astype(jnp.int32)

    def final_dev(b):
        dx, dc, dg = b in (near_x, near_x_c, skew), b in (own_c, near_x_c, near_y_c, deep_c), b in (near_y, near_y_c, skew)
        gg = 1 - g if dg else g
        rr = role
        if b == deep:
            gg = jnp.where(inner, g, 1 - g)
        if b in (deep, deep_c):
            rr = 1 - role
        xx = 1 - x if dx else x
        cc = 1 - core if dc else core
        return zh, xx * CORES + cc, gg * 2 + rr

    def part_copy(b):
        gg, tt, jj = final_dev(b)
        return pltpu.make_async_remote_copy(
            mine.at[b], parts.at[deep if b == skew else b], p_send.at[b],
            p_recv.at[deep if b == skew else b],
            device_id=dev(gg, tt, jj), device_id_type=MESH)

    def stays(b):
        gg, tt, jj = final_dev(b)
        return jnp.logical_and(gg == g, jnp.logical_and(tt == ti, jj == tj))

    def holds(b):
        if b == deep_c:
            return inner
        if b == deep:
            return jnp.logical_or(inner, left)
        return jnp.logical_and(inner, right) if b == skew else True

    def top_of(n):
        return jnp.max(jnp.transpose(ybest[n]).reshape(16, 8, sub), axis=0)

    def give(b, top):
        mine[b] = jnp.max(top, axis=0, keepdims=True)

        @pl.when(jnp.logical_and(holds(b), stays(b)))
        def _():
            parts[deep if b == skew else b] = mine[b]

        @pl.when(jnp.logical_and(holds(b), jnp.logical_not(stays(b))))
        def _():
            part_copy(b).start()

    @pl.when(inner)
    def _():
        read_ids()
        supply_both(0, 0)
        send_y(4)
        relay(2)
        send_z(3)
        relay(3)
        send_z(4)
        supply_both(1, 1)
        forward(0, True)
        send_y(5)
        send_y(6)
        supply_deep(2, 2)
        relay(4)
        send_z(5)
        forward(1, True)
        relay(5)
        send_z(6)
        supply_own(2, 3)
        relay(6)
        send_z(7)
        send_y(7)
        send_y(8)
        send_y(9)
        score_early(0, True)
        supply_deep(3, 4)
        forward(2, True)
        supply_deep(4, 5)
        relay(7)
        send_z(8)
        relay(8)
        send_z(9)
        collect(near_x_c, 0)
        collect(near_y_c, 0)
        score(0, True, 3, 10)
        supply_own(3, 6)
        relay(9)
        score_early(1, True)
        supply_deep(5, 7)
        begin_skew()
        supply_own(4, 8)

        @pl.when(right)
        def _():
            forward(3, True)

        @pl.when(left)
        def _():
            for c in of(3):
                block_copy(own, near_y, c, core_dev).wait_recv()
                block_copy(near_y, deep, c, pair_dev).start()
                block_copy(near_y, near_y_c, c, core_dev).start()

        supply_own(5, 9)

        @pl.when(left)
        def _():
            for c in of(3):
                block_copy(own, near_x, c, core_dev).wait_recv()
                block_copy(near_x, near_x_c, c, core_dev).start()

        score(1, True, 3, 7)

        @pl.when(right)
        def _():
            for c in of(3):
                block_copy(near_x, skew, c, y_dev).start()

        @pl.when(left)
        def _():
            for c in of(last):
                block_copy(own, deep, c, dev(1 - g, ti, zh * 2 + 1 - zl)).start()

        forward(4, True)
        collect(near_x_c, 1)
        collect(near_y_c, 1)
        score(1, True, 7, 10)
        score_early(2, True)
        forward(5, True)
        score(2, True, 3, 7)
        collect(near_x_c, 2)
        collect(near_y_c, 2)
        score(2, True, 7, 10)
        for b in (own_c, near_x_c, near_y_c):
            give(b, xbest[b])
        for b in (own, near_x, near_y):
            give(b, jnp.maximum(xbest[b], top_of(b // 2)))
        finish_skew()
        for b in (deep, deep_c):
            give(b, xbest[b])

        @pl.when(right)
        def _():
            give(skew, top_of(3))

    @pl.when(outer)
    def _():
        supply_outer(0)
        send_y(4)
        send_y(5)
        send_y(6)
        relay(2)
        send_z(3)
        relay(3)
        send_z(4)
        supply_outer(1)
        send_y(7)
        send_y(8)
        send_y(9)
        relay(4)
        send_z(5)
        relay(5)
        send_z(6)
        relay(6)
        send_z(7)
        forward(0, False)
        forward(1, False)
        relay(7)
        send_z(8)
        relay(8)
        send_z(9)
        relay(9)
        supply_outer(2)
        score_early(0, False)
        forward(2, False)
        supply_outer(3)
        score_late(0)
        supply_outer(4)
        score_early(1, False)
        forward(3, False)
        supply_outer(5)
        score_late(1)
        score_deep(0)
        forward(4, False)
        score_early(2, False)
        forward(5, False)
        score_late(2)
        give(own_c, xbest[own_c])
        give(own, jnp.maximum(xbest[own], top_of(0)))
        crossed = top_of(2)
        for b, mine_too in ((near_y, jnp.logical_and(right, x == 1)), (near_y_c, jnp.logical_and(right, x == 0))):
            give(b, jnp.maximum(xbest[b], jnp.where(mine_too, crossed, -2.0)))
        score_deep(1)
        score_deep(2)
        give(near_x_c, xbest[near_x_c])
        give(near_x, jnp.maximum(xbest[near_x], top_of(1)))

        @pl.when(left)
        def _():
            give(deep, jnp.maximum(xbest[deep], top_of(2)))

    def drain(o, _):
        @pl.when(jnp.logical_not(is_me(o)))
        def _():
            departed(send_ids.at[pl.ds(o * 2, 2)], i_send.at[o])
            departed(send.at[o], d_send.at[o])
        return 0

    lax.fori_loop(0, homes, drain, 0)
    for half in halves:
        @pl.when(jnp.logical_not(level(half)))
        def _(half=half):
            departed(hop.at[half], h_send.at[half])
    for target in (near_y, near_x, own_c, near_y_c, near_x_c):
        departed(raw.at[own], g_send.at[target])

    @pl.when(inner)
    def _():
        for target in (own, deep_c):
            departed(raw.at[own], g_send.at[target])

    @pl.when(jnp.logical_and(inner, left))
    def _():
        departed(raw.at[own], g_send.at[deep])

    @pl.when(jnp.logical_and(inner, right))
    def _():
        departed(raw.at[own], g_send.at[skew])

    half, rr = tj // 2, lax.rem(tj, 2)

    @pl.when(rr == 0)
    def _():
        parts[deep_c] = jnp.full((1, sub), -2.0, jnp.float32)

    def giver(b):
        dx, dc, dg = b in (near_x, near_x_c), b in (own_c, near_x_c, near_y_c, deep_c), b in (near_y, near_y_c)
        gg = 1 - half if dg else half
        plane = rr
        xx = 1 - x if dx else x
        if b == deep:
            gg = jnp.where(rr == 0, 1 - half, half)
            xx = jnp.where(jnp.logical_and(rr == 0, right), 1 - x, x)
            plane = jnp.where(jnp.logical_and(rr == 0, left), 1, 0)
        if b == deep_c:
            plane = 1 - rr
        cc = 1 - core if dc else core
        zz = jnp.where(plane == 0, 1 - g, g)
        return gg, xx * CORES + cc, g * 2 + zz

    for b in range(8):
        gg, tt, jj = giver(b)
        here = jnp.logical_and(gg == g, jnp.logical_and(tt == ti, jj == tj))
        comes = jnp.logical_not(here)
        if b == deep_c:
            comes = jnp.logical_and(comes, rr == 1)

        @pl.when(comes)
        def _(b=b):
            part_copy(b).wait_recv()

    out_ref[...] = jnp.max(parts[...], axis=0)

    for b in range(9):
        @pl.when(jnp.logical_and(holds(b), jnp.logical_not(stays(b))))
        def _(b=b):
            part_copy(b).wait_send()


def square(corpus, slot_of_row):
    ti_count, tj_count = lax.axis_size("ti"), lax.axis_size("tj")
    _, count, features = corpus.shape
    sub = count // 2
    cap = sub // tj_count
    groups, homes = 2 * tj_count, tj_count
    unit = features // 8
    edges = (0, 1, 2, 4, 6, 7, 8)
    spans = [(a * unit, b * unit) for a, b in zip(edges, edges[1:])]
    phases = [(0, 4 * unit), (4 * unit, 6 * unit), (6 * unit, features)]
    n = len(spans)
    cuts = [(f, 0, sub) for f in range(n - 1)] + [(n - 1, 0, sub // 2), (n - 1, sub // 2, sub // 2)]
    units = [(0, 0, 2), (1, 0, 2), (2, 1, 1), (2, 0, 1), (3, 1, 1), (4, 1, 1), (3, 0, 1), (5, 1, 1), (4, 0, 1), (5, 0, 1)]
    wide_cap = -(-cap // 128) * 128
    jobs = 11
    piece = 256 if count % 256 == 0 else 128
    dma = pltpu.SemaphoreType.DMA
    vmem = pl.BlockSpec(memory_space=pltpu.VMEM)
    bf16, f32 = jnp.bfloat16, jnp.float32
    return pl.pallas_call(
        functools.partial(
            square_kernel, (ti_count, tj_count, count, features, sub, cap, spans, units, cuts, phases)),
        out_shape=jax.ShapeDtypeStruct((1, sub), f32),
        in_specs=[vmem, pl.BlockSpec(memory_space=pl.ANY)],
        out_specs=vmem,
        scratch_shapes=[
            pltpu.VMEM((count, features), bf16),
            pltpu.VMEM((1, count), jnp.int32),
            pltpu.VMEM((16, count), bf16),
            pltpu.VMEM((count, count), bf16),
            pltpu.VMEM((homes, 2, cap, features), bf16),
            pltpu.VMEM((groups, 16, wide_cap), bf16),
            pltpu.VMEM((2, 2, cap, features), bf16),
            pltpu.VMEM((2, groups * cap, features), bf16),
            pltpu.VMEM((groups, 2, 16, wide_cap), bf16),
            pltpu.VMEM((2, 16, count), f32),
            pltpu.VMEM((9, sub, features), bf16),
            pltpu.VMEM((jobs, sub, sub), f32),
            pltpu.VMEM((8, 8, sub), f32),
            pltpu.VMEM((4, sub, 128), f32),
            pltpu.VMEM((9, 1, sub), f32),
            pltpu.VMEM((8, 1, sub), f32),
            dma((1,)),
            dma((homes,)), dma((len(units),)), dma((2,)), dma((2, len(units))), dma((homes,)), dma((1,)),
            dma((9,)), dma((3, len(cuts))), dma((6, len(phases))), dma((9,)), dma((8,)),
        ],
        compiler_params=pltpu.CompilerParams(
            collective_id=1, has_side_effects=True, vmem_limit_bytes=63 * 1024 * 1024),
    )(slot_of_row, corpus)


def solution(mesh):
    in_specs = (P("grp", ("ti", "tj"), None), P("grp", ("ti", "tj")))
    out_specs = P("grp", ("ti", "tj"))
    is_square = mesh.shape["ti"] == 2 * CORES and mesh.shape["tj"] == 4
    return jax.shard_map(
        square if is_square else per_device, mesh=mesh, in_specs=in_specs, out_specs=out_specs, check_vma=False
    )
```
